32 devices in a mesh: dp: 8 (over y, x, core), mp: 4 (over z).
Axes of the slice: x: 2, y: 2, z: 4, core: 2. Of those that a mesh axis runs over, the one named last changes fastest.
Arguments:
- x_short: bfloat16 [72, 128, 768], P('dp'), may hold values from -6 to 6
- x_long: bfloat16 [16, 512, 768], P('dp'), may hold values from -6 to 6
- short_lengths: int32 [72], P('dp'), may hold values from 32 to 128, as said below
- long_lengths: int32 [16], P('dp'), may hold values from 128 to 512, as said below
- slope_index: int32 [12], P('mp'), may hold values from 0 to 23
- w_qkv: bfloat16 [768, 3, 768], P(None, None, 'mp'), may hold values from -0.3125 to 0.3125
- b_qv: float32 [64, 2, 12], P(None, None, 'mp'), may hold values from -3 to 3
- w_out: bfloat16 [768, 768], P(None, 'mp'), may hold values from -0.875 to 0.875
- b_out: float32 [768], replicated, may hold values from -3 to 3
- gain1: float32 [768], replicated, may hold values from 0.5 to 1.5
- bias1: float32 [768], replicated, may hold values from -3 to 3
- w_up: bfloat16 [768, 2, 3072], P(None, None, 'mp'), may hold values from -0.21875 to 0.21875
- w_down: bfloat16 [768, 3072], P(None, 'mp'), may hold values from -0.109375 to 0.109375
- b_down: float32 [768], replicated, may hold values from -3 to 3
- gain2: float32 [768], replicated, may hold values from 0.5 to 1.5
- bias2: float32 [768], replicated, may hold values from -3 to 3
- cot_short: bfloat16 [72, 128, 768], P('dp'), may hold values from -6 to 6
- cot_long: bfloat16 [16, 512, 768], P('dp'), may hold values from -6 to 6
Outputs:
- y_short: bfloat16 [72, 128, 768], P('dp')
- y_long: bfloat16 [16, 512, 768], P('dp')
- dx_short: bfloat16 [72, 128, 768], P('dp')
- dx_long: bfloat16 [16, 512, 768], P('dp')
- grad_w_qkv: float32 [768, 3, 768], P('dp', None, 'mp')
- grad_b_qv: float32 [64, 2, 12], P('dp', None, 'mp')
- grad_w_out: float32 [768, 768], P('dp', 'mp')
- grad_b_out: float32 [768], P('dp')
- grad_gain1: float32 [768], P('dp')
- grad_bias1: float32 [768], P('dp')
- grad_w_up: float32 [768, 2, 3072], P('dp', None, 'mp')
- grad_w_down: float32 [768, 3072], P('dp', 'mp')
- grad_b_down: float32 [768], P('dp')
- grad_gain2: float32 [768], P('dp')
- grad_bias2: float32 [768], P('dp')
The draws below stay inside these ranges and needn't reach their ends.
Inputs may be any that keep to these rules, and one draw needn't show every extreme that they name: `short_lengths`: true length of each short sequence; positions from it on are padding. `long_lengths`: true length of each long sequence; positions from it on are padding. `slope_index`: ALiBi slope index of each head, below 24; heads may share an index.
All inputs are finite; a program needn't handle non-finite values.
Results may differ from the reference program's by a relative error of at most 0.025.
The reference program's roundings to bfloat16 on the way count: a program that leaves them out, or rounds other values in their place, can miss the bound.
Values may be sent and summed in bfloat16 or wider, within the bound.
A program may use at most 128 MiB of HBM per device.

```python
import math
import jax
import jax.numpy as jnp
from jax import lax

D = 768
HEADS = 12
HD = 64
FF = 3072
SHORT_LEN = 128
LONG_LEN = 512
SHORT_DEV = 9
LONG_DEV = 2
SHORT_SEQS = 72
LONG_SEQS = 16
N_MP = 4


def draw_lengths(key, number, most):
    base = jax.random.randint(jax.random.fold_in(key, 11), (number,), most // 4, most + 1)
    first_slot = jax.random.randint(jax.random.fold_in(key, 12), (), 0, number)
    other_slot = (first_slot + 1 + jax.random.randint(jax.random.fold_in(key, 13), (), 0, number - 1)) % number
    places = jnp.arange(number)
    base = jnp.where(places == first_slot, most, base)
    return jnp.where(places == other_slot, most // 4, base).astype(jnp.int32)


def draw_short_lengths(key, part):
    return draw_lengths(key, SHORT_SEQS, SHORT_LEN)


def draw_long_lengths(key, part):
    return draw_lengths(key, LONG_SEQS, LONG_LEN)


def with_ends(array, rng, low, top_value):
    shape = array.shape
    index_at = [jax.random.randint(jax.random.fold_in(rng, axis), (), 0, shape[axis]) for axis in range(len(shape))]
    array = array.at[tuple(index_at)].set(low)
    longest = shape.index(max(shape))
    index_at[longest] = (index_at[longest] + 1) % shape[longest]
    return array.at[tuple(index_at)].set(top_value)


def strengthened(entries, own_key, source, target, parts, factor):
    owner, partner = [(jnp.arange(entries.shape[axis_at]) // (entries.shape[axis_at] // parts)).reshape([-1 if axis == axis_at else 1 for axis in range(entries.ndim)]) for axis_at in (source, target)]
    chosen = jax.random.permutation(own_key, parts)[partner]
    strong = (owner == chosen) | (owner == (partner + parts // 2) % parts)
    return jnp.where(strong, factor * entries, entries)


def level_of(key, shape, pieces, low, high):
    factor_of, own = 1.0, jax.random.fold_in(key, 6)
    for dim, shards_of in pieces:
        draws = jnp.exp(jax.random.uniform(jax.random.fold_in(own, dim), (shards_of,), jnp.float32, low / len(pieces), high / len(pieces)))
        factor_of = factor_of * jnp.repeat(draws, shape[dim] // shards_of).reshape([-1 if axis == dim else 1 for axis in range(len(shape))])
    return factor_of


def gaussian(stream_key, extent, spread, reach, cuts=(), dtype=jnp.bfloat16):
    entries = jax.random.normal(stream_key, extent, jnp.float32) * spread
    if len(cuts) > 0:
        entries = level_of(stream_key, extent, cuts, -0.22, 0.18) * entries
    return jnp.clip(entries, min=-reach, max=reach).astype(dtype)


def gaussian_with(key, dims, deviation, limit, split, heavy, kind=jnp.bfloat16):
    drawn = deviation * jax.random.normal(key, dims, jnp.float32)
    if split:
        drawn = drawn * level_of(key, dims, split, -0.22, 0.18)
    return jnp.clip(strengthened(drawn, jax.random.fold_in(key, 3), *heavy), -limit, limit).astype(kind)


def setup_inputs(seed: int = 0) -> dict:
    key_list = jax.random.split(jax.random.key(seed), 19)
    x_short = gaussian_with(key_list[0], (SHORT_SEQS, SHORT_LEN, D), 1.0, 6.0, ((0, 8),), (0, 2, 8, 2.0))
    x_long = gaussian_with(key_list[1], (LONG_SEQS, LONG_LEN, D), 1.0, 6.0, ((0, 8),), (0, 2, 8, 2.0))
    short_lengths = draw_short_lengths(jax.random.fold_in(key_list[18], 71), 0)
    long_lengths = draw_long_lengths(jax.random.fold_in(key_list[18], 71), 0)
    slope_index = with_ends(jax.random.randint(key_list[4], (HEADS,), 0, 2 * HEADS), jax.random.fold_in(key_list[4], 1), 0, (2 * HEADS) - 1).astype(jnp.int32)
    w_qkv = gaussian(key_list[5], (D, 3, D), (D // 2) ** -0.5, 0.3125, ((2, 4),))
    b_qv = gaussian(key_list[6], (HD, 2, HEADS), 0.5, 3.0, ((2, 4),), jnp.float32)
    w_out = gaussian(key_list[7], (D, D), (D // 16) ** -0.5, 0.875, ((1, 4),))
    b_out = gaussian(key_list[8], (D,), 0.5, 3.0, (), jnp.float32)
    gain1 = jnp.clip(1.0 + 0.1 * jax.random.normal(key_list[9], (D,), jnp.float32), 0.5, 1.5)
    bias1 = gaussian(key_list[10], (D,), 0.5, 3.0, (), jnp.float32)
    w_up = gaussian(key_list[11], (D, 2, FF), D ** -0.5, 0.21875, ((2, 4),))
    w_down = gaussian(key_list[12], (D, FF), FF ** -0.5, 0.109375, ((1, 4),))
    b_down = gaussian(key_list[13], (D,), 0.5, 3.0, (), jnp.float32)
    gain2 = jnp.clip(1.0 + 0.1 * jax.random.normal(key_list[14], (D,), jnp.float32), 0.5, 1.5)
    bias2 = gaussian(key_list[15], (D,), 0.5, 3.0, (), jnp.float32)
    cot_short = gaussian_with(key_list[16], (SHORT_SEQS, SHORT_LEN, D), 1.0, 6.0, ((0, 8),), (0, 2, 8, 2.0))
    cot_long = gaussian_with(key_list[17], (LONG_SEQS, LONG_LEN, D), 1.0, 6.0, ((0, 8),), (0, 2, 8, 2.0))
    return dict(x_short=x_short, x_long=x_long, short_lengths=short_lengths, long_lengths=long_lengths, slope_index=slope_index, w_qkv=w_qkv, b_qv=b_qv, w_out=w_out, b_out=b_out, gain1=gain1, bias1=bias1, w_up=w_up, w_down=w_down, b_down=b_down, gain2=gain2, bias2=bias2, cot_short=cot_short, cot_long=cot_long)


EPSILON = 1e-12
MASKED = -1e+30
HIGHEST = lax.Precision.HIGHEST

@jax.custom_vjp
def low(v):
    return lax.optimization_barrier(v.astype(jnp.bfloat16)).astype(jnp.float32)

@jax.custom_vjp
def low_back(v):
    return v

def low_keep(v):
    return (low(v), None)

def low_pass(kept, grad):
    return (grad,)

def back_keep(v):
    return (v, None)

def back_low(kept, grad):
    return (low(grad),)
low.defvjp(low_keep, low_pass)
low_back.defvjp(back_keep, back_low)

def alibi_slopes(slope_index, head_total):
    power = 1 << head_total.bit_length() - 1
    index_f = slope_index.astype(jnp.float32)
    main_part = jnp.exp2(-8.0 * (index_f + 1.0) / power)
    extra_part = jnp.exp2(-4.0 * (2.0 * (index_f - power) + 1.0) / power)
    return jnp.where(slope_index < power, main_part, extra_part)

def layer_norm(totals, gain_vec, shift_vec):
    mean_vec = lax.optimization_barrier(jnp.mean(totals, axis=-1, keepdims=True))
    centred = totals - mean_vec
    variance = lax.optimization_barrier(jnp.mean(centred * centred, axis=-1, keepdims=True))
    return centred * lax.rsqrt(variance + EPSILON) * gain_vec + shift_vec

def attend_group(queries, key_rows, value_rows, lengths, slopes):
    length = queries.shape[1]
    raw_scores = jnp.einsum('sqhe,skhe->shqk', queries, key_rows, precision=HIGHEST)
    position = jnp.arange(length)
    distance = jnp.abs(position[:, None] - position[None, :]).astype(jnp.float32)
    scores = low_back(raw_scores * (1.0 / math.sqrt(HD)) - slopes[None, :, None, None] * distance[None, None])
    key_valid = position[None, None, None, :] < lengths[:, None, None, None]
    soft_probs = jax.nn.softmax(jnp.where(key_valid, scores, MASKED), axis=-1)
    return jnp.einsum('shqk,skhe->sqhe', low(soft_probs), value_rows, precision=HIGHEST)

def attend_bucket(queries, key_rows, value_rows, lengths, slopes, per_dev, length):

    def shaped(flat_rows):
        return flat_rows.reshape(-1, per_dev, length, HEADS, HD)
    groups = (shaped(queries), shaped(key_rows), shaped(value_rows), lengths.reshape(-1, per_dev))
    step_fn = jax.checkpoint(lambda member: attend_group(member[0], member[1], member[2], member[3], slopes))
    context = lax.map(step_fn, groups)
    return context.reshape(-1, HEADS * HD)

def reference(x_short, x_long, short_lengths, long_lengths, slope_index, w_qkv, b_qv, w_out, b_out, gain1, bias1, w_up, w_down, b_down, gain2, bias2, cot_short, cot_long):
    slopes = alibi_slopes(slope_index, HEADS)
    short_rows = SHORT_SEQS * SHORT_LEN

    def forward(params):
        short_in, long_in, w_proj, b_proj, w_attn, b_attn, gain_one, shift_one, w_gate_up, w_back, b_back, gain_two, shift_two = params
        token_rows = jnp.concatenate([short_in.reshape(-1, D), long_in.reshape(-1, D)], 0)
        projected = jnp.einsum('rd,dce->rce', token_rows, w_proj, precision=HIGHEST)
        bias_query = b_proj[:, 0, :].T.reshape(-1)
        bias_value = b_proj[:, 1, :].T.reshape(-1)
        queries = low_back(low(projected[:, 0] + bias_query))
        key_rows = low_back(low(projected[:, 1]))
        value_rows = low_back(low(projected[:, 2] + bias_value))
        ctx_short = attend_bucket(queries[:short_rows], key_rows[:short_rows], value_rows[:short_rows], short_lengths, slopes, SHORT_DEV, SHORT_LEN)
        ctx_long = attend_bucket(queries[short_rows:], key_rows[short_rows:], value_rows[short_rows:], long_lengths, slopes, LONG_DEV, LONG_LEN)
        context = low_back(low(jnp.concatenate([ctx_short, ctx_long], 0)))
        partials = jnp.einsum('rgk,dgk->grd', context.reshape(-1, N_MP, D // N_MP), w_attn.reshape(D, N_MP, D // N_MP), precision=HIGHEST)
        attention = low_back(lax.optimization_barrier(jnp.sum(low(partials), axis=0)))
        hidden1 = layer_norm(token_rows + attention + b_attn, gain_one, shift_one)
        gate_up = jnp.einsum('rd,dcf->rcf', low(hidden1), w_gate_up, precision=HIGHEST)
        gate_rows = low_back(gate_up[:, 0])
        up_rows = low_back(gate_up[:, 1])
        inner = low(jax.nn.gelu(gate_rows, approximate=False) * up_rows)
        partials_two = jnp.einsum('rgk,dgk->grd', inner.reshape(-1, N_MP, FF // N_MP), w_back.reshape(D, N_MP, FF // N_MP), precision=HIGHEST)
        feed_out = low_back(lax.optimization_barrier(jnp.sum(low(partials_two), axis=0)))
        normed_out = layer_norm(hidden1 + feed_out + b_back, gain_two, shift_two)
        return (normed_out[:short_rows].reshape(short_in.shape), normed_out[short_rows:].reshape(long_in.shape))
    params = tuple((member.astype(jnp.float32) for member in (x_short, x_long, w_qkv, b_qv, w_out, b_out, gain1, bias1, w_up, w_down, b_down, gain2, bias2)))
    outputs, pullback = jax.vjp(forward, params)
    grads = pullback((cot_short.astype(jnp.float32), cot_long.astype(jnp.float32)))[0]
    return (outputs[0].astype(jnp.bfloat16), outputs[1].astype(jnp.bfloat16), grads[0].astype(jnp.bfloat16), grads[1].astype(jnp.bfloat16), grads[2], grads[3], grads[4], grads[5], grads[6], grads[7], grads[8], grads[9], grads[10], grads[11], grads[12])
```

```python
import functools
import math

import jax
import jax.numpy as jnp
from jax import lax
from jax.experimental import pallas as pl
from jax.experimental.pallas import tpu as pltpu
from jax.sharding import PartitionSpec as P

F32, BF16 = jnp.float32, jnp.bfloat16
R, D, E = 640, 768, 192
FAR = 1e30
VM = 60 << 20

def nn(a, b): return lax.dot_general(a, b, (((1,), (0,)), ((), ())), preferred_element_type=F32)
def nt(a, b): return lax.dot_general(a, b, (((1,), (1,)), ((), ())), preferred_element_type=F32)

def load_rows(m, long_ref, short_ref, buf, sem):
    @pl.when(m < 2)
    def _():
        c = pltpu.make_async_copy(long_ref.at[pl.ds(4 * m, 4)], buf.at[pl.ds(0, 4)], sem); c.start(); c.wait()
        buf[4] = jnp.zeros((128, D), BF16)
    @pl.when(m == 2)
    def _():
        c = pltpu.make_async_copy(short_ref.at[pl.ds(0, 5)], buf, sem); c.start(); c.wait()
    @pl.when(m == 3)
    def _():
        c = pltpu.make_async_copy(short_ref.at[pl.ds(5, 4)], buf.at[pl.ds(0, 4)], sem); c.start(); c.wait()
        buf[4] = jnp.zeros((128, D), BF16)

def distances(m, slen, llen, dm):
    @pl.when(m < 2)
    def _():
        n = llen[jnp.minimum(m, 1)]
        key = lax.broadcasted_iota(jnp.int32, (512, 128), 0)
        qry = lax.broadcasted_iota(jnp.int32, (512, 128), 1)
        for i in range(4):
            dist = jnp.abs(key - (qry + 128 * i)).astype(F32)
            dm[i] = jnp.where(key < n, dist, FAR)
    @pl.when(m >= 2)
    def _():
        key = lax.broadcasted_iota(jnp.int32, (128, 128), 0)
        qry = lax.broadcasted_iota(jnp.int32, (128, 128), 1)
        dist = jnp.abs(key - qry).astype(F32)
        for i in range(5):
            n = slen[jnp.minimum(5 * (m - 2) + i, 8)] if i == 4 else slen[jnp.maximum(5 * (m - 2), 0) + i]
            dm[i, 0:128, :] = jnp.where(key < n, dist, FAR)

def head_lanes(j):
    return lax.broadcasted_iota(jnp.int32, (1, E), 1) // 64 == j
def head_rows(j):
    return lax.broadcasted_iota(jnp.int32, (E, 1), 0) // 64 == j

def attend_fwd(m, small, q8, k, vt, dm, ct, lse):
    def block(i, keys, koff):
        cols = pl.ds(pl.multiple_of(i * 128, 128), 128)
        qi = q8[cols, :]
        kk = k[pl.ds(koff, keys), :]
        vv = vt[:, pl.ds(koff, keys)]
        d = dm[i, 0:keys, :]
        out = jnp.zeros((E, 128), F32)
        for j in range(3):
            s = nt(kk, jnp.where(head_lanes(j), qi, jnp.zeros_like(qi))) - small[2:3, j:j + 1] * d
            mx = jnp.max(s, axis=0, keepdims=True)
            ex = jnp.exp(s - mx)
            tot = jnp.sum(ex, axis=0, keepdims=True)
            p = (ex * (1.0 / tot)).astype(BF16)
            out = jnp.where(head_rows(j), nn(vv, p), out)
            lse[j:j + 1, cols] = mx + jnp.log(tot)
        ct[:, cols] = out.astype(BF16)
    @pl.when(m < 2)
    def _():
        lax.fori_loop(0, 4, lambda i, u: (block(i, 512, 0), u)[1], 0)
    @pl.when(m >= 2)
    def _():
        lax.fori_loop(0, 5, lambda i, u: (block(i, 128, pl.multiple_of(i * 128, 128)), u)[1], 0)

def attend_bwd(m, small, q8, k, v, kt, gc, dm, lse, gqt, gk, gv):
    gk[...] = jnp.zeros_like(gk)
    gv[...] = jnp.zeros_like(gv)
    def block(i, keys, koff):
        cols = pl.ds(pl.multiple_of(i * 128, 128), 128)
        rows = pl.ds(koff, keys)
        qi, gi = q8[cols, :], gc[cols, :]
        kk, vv, ktt = k[rows, :], v[rows, :], kt[:, rows]
        d = dm[i, 0:keys, :]
        oq = jnp.zeros((E, 128), F32)
        ok = jnp.zeros((keys, E), F32)
        ov = jnp.zeros((keys, E), F32)
        for j in range(3):
            hl = head_lanes(j)
            qj = jnp.where(hl, qi, jnp.zeros_like(qi))
            gj = jnp.where(hl, gi, jnp.zeros_like(gi))
            s = nt(kk, qj) - small[2:3, j:j + 1] * d
            p = jnp.exp(s - lse[j:j + 1, cols])
            gp = nt(vv, gj)
            ov = ov + nn(p.astype(BF16), gj)
            row = jnp.sum(p * gp, axis=0, keepdims=True)
            ds = (p * (gp - row)).astype(BF16)
            oq = jnp.where(head_rows(j), nn(ktt, ds), oq)
            ok = ok + nn(ds, qj)
        gqt[:, cols] = oq * 0.125
        gk[rows, :] += ok
        gv[rows, :] += ov
    @pl.when(m < 2)
    def _():
        lax.fori_loop(0, 4, lambda i, u: (block(i, 512, 0), u)[1], 0)
        gqt[:, 512:640] = jnp.zeros((E, 128), F32)
    @pl.when(m >= 2)
    def _():
        lax.fori_loop(0, 5, lambda i, u: (block(i, 128, pl.multiple_of(i * 128, 128)), u)[1], 0)

def norm_fwd(s):
    mean = jnp.mean(s, axis=1, keepdims=True)
    c = s - mean
    r = lax.rsqrt(jnp.mean(c * c, axis=1, keepdims=True) + 1e-12)
    return c * r, r

def norm_bwd(gn, normed, r):
    return r * (gn - jnp.mean(gn, axis=1, keepdims=True) - normed * jnp.mean(gn * normed, axis=1, keepdims=True))

def row_tiles(fn, tile=128):
    def body(i, u):
        fn(pl.ds(pl.multiple_of(i * tile, tile), tile)); return u
    lax.fori_loop(0, R // tile, body, 0)

def ka(slen, llen, xl, xs, w, small, vec, q8o, ko, vo, co, lseo, n1o, r1o, hlo, xb, dm, vt, ct, acc, sem):
    z = pl.program_id(0)
    m = lax.axis_index("mp")
    @pl.when(z == 0)
    def _():
        load_rows(m, xl, xs, xb, sem)
        distances(m, slen, llen, dm)
        ct[...] = jnp.zeros_like(ct)
        lseo[...] = jnp.zeros_like(lseo)
        acc[...] = jnp.zeros_like(acc)
    x = xb[...].reshape(R, D)
    wz, sm = w.at[0, 0], small.at[0]
    q8o[0] = ((nt(x, wz[0:192, :]) + sm[0:1, 0:192]).astype(BF16).astype(F32) * 0.125).astype(BF16)
    ko[0] = nt(x, wz[192:384, :]).astype(BF16)
    v = (nt(x, wz[384:576, :]) + sm[1:2, 0:192]).astype(BF16)
    vo[0] = v
    vt[...] = v.T
    attend_fwd(m, sm, q8o.at[0], ko.at[0], vt, dm, ct, lseo.at[0])
    co[0] = ct[...].T
    acc[...] += nn(co[0], wz[576:768, :]).astype(BF16).astype(F32)
    @pl.when(z == 3)
    def _():
        for i in range(5):
            rows = slice(128 * i, 128 * i + 128)
            s = xb[i].astype(F32) + acc[rows, :] + vec[0:1, :]
            n, r = norm_fwd(s)
            n1o[rows, :] = n
            r1o[rows, :] = jnp.broadcast_to(r, (128, 128))
            hlo[rows, :] = (n * vec[1:2, :] + vec[2:3, :]).astype(BF16)

def const(shape): return pl.BlockSpec(shape, lambda z, *_: (0,) * len(shape))
def perz(shape): return pl.BlockSpec((1,) + shape, lambda z, *_: (z,) + (0,) * len(shape))
ANY = pl.BlockSpec(memory_space=pl.ANY)
def sds(shape, dt): return jax.ShapeDtypeStruct(shape, dt)
def part(p): return pl.BlockSpec((1, 1, D, D), lambda z, *_: (z, p, 0, 0))

def call(kernel, in_specs, outs, scratch, name, args, grid=(4,), prefetch=2):
    return pl.pallas_call(
        kernel,
        grid_spec=pltpu.PrefetchScalarGridSpec(num_scalar_prefetch=prefetch, grid=grid, in_specs=in_specs,
            out_specs=[o[0] for o in outs], scratch_shapes=scratch),
        out_shape=[o[1] for o in outs],
        compiler_params=pltpu.CompilerParams(dimension_semantics=("arbitrary",), vmem_limit_bytes=VM),
        name=name)(*args)

def run_ka(slen, llen, xl, xs, W, small, vec):
    rz = lambda: (perz((R, E)), sds((4, R, E), BF16))
    return call(ka, [ANY, ANY, part(0), perz((8, 256)), const((8, D))],
        [rz(), rz(), rz(), rz(), (perz((8, R)), sds((4, 8, R), F32)), (const((R, D)), sds((R, D), F32)), (const((R, 128)), sds((R, 128), F32)), (const((R, D)), sds((R, D), BF16))],
        [pltpu.VMEM((5, 128, D), BF16), pltpu.VMEM((5, 512, 128), F32), pltpu.VMEM((E, R), BF16), pltpu.VMEM((E, R), BF16), pltpu.VMEM((R, D), F32), pltpu.SemaphoreType.DMA],
        "attention_forward", (slen, llen, xl, xs, W, small, vec))

def gelu_parts(g):
    cdf = 0.5 * (1.0 + lax.erf(g * (2.0 ** -0.5)))
    pdf = jnp.exp(-0.5 * g * g) * (1.0 / math.sqrt(2 * math.pi))
    return g * cdf, cdf + g * pdf

def kb(cl, cs, wg, wu, wd, hl, n1, vec, ao, bo, io, yo, gfo, gs2o, vgo, acc, cb, sem):
    z = pl.program_id(0)
    m = lax.axis_index("mp")
    @pl.when(z == 0)
    def _():
        load_rows(m, cl, cs, cb, sem)
        acc[...] = jnp.zeros_like(acc)
    def tile(rows):
        h = hl[rows, :]
        gate = nn(h, wg[0, 0])
        up = nn(h, wu[0, 0])
        a, slope = gelu_parts(gate)
        ao[0, rows, :] = a
        bo[0, rows, :] = up * slope
        inner = (a * up).astype(BF16)
        io[0, rows, :] = inner
        acc[rows, :] += nt(inner, wd[0, 0]).astype(BF16).astype(F32)
    row_tiles(tile)
    @pl.when(z == 3)
    def _():
        tot = [jnp.zeros((1, D), F32)] * 3
        for i in range(5):
            rows = slice(128 * i, 128 * i + 128)
            h1 = n1[rows, :] * vec[1:2, :] + vec[2:3, :]
            n, r = norm_fwd(h1 + acc[rows, :] + vec[3:4, :])
            yo[rows, :] = (n * vec[4:5, :] + vec[5:6, :]).astype(BF16)
            gy = cb[i].astype(F32)
            gs = norm_bwd(gy * vec[4:5, :], n, r)
            gs2o[rows, :] = gs
            gfo[rows, :] = gs.astype(BF16)
            tot = [tot[0] + jnp.sum(gy * n, axis=0, keepdims=True), tot[1] + jnp.sum(gy, axis=0, keepdims=True), tot[2] + jnp.sum(gs, axis=0, keepdims=True)]
        vgo[...] = jnp.concatenate(tot + [jnp.zeros((5, D), F32)], axis=0)

def run_kb(cl, cs, W, hl, n1, vec):
    z32 = lambda: (perz((R, D)), sds((4, R, D), F32))
    return call(kb, [ANY, ANY, part(1), part(2), part(3), const((R, D)), const((R, D)), const((8, D))],
        [z32(), z32(), (perz((R, D)), sds((4, R, D), BF16)), (const((R, D)), sds((R, D), BF16)), (const((R, D)), sds((R, D), BF16)), (const((R, D)), sds((R, D), F32)), (const((8, D)), sds((8, D), F32))],
        [pltpu.VMEM((R, D), F32), pltpu.VMEM((5, 128, D), BF16), pltpu.SemaphoreType.DMA],
        "feed_forward", (cl, cs, W, W, W, hl, n1, vec), prefetch=0)

def kc(wg, wu, wd, a, b, inner, gf, hl, gs2, n1, r1, vec, go, gao, gs1o, vgo, acc, gft, hlt, gg):
    z = pl.program_id(0)
    @pl.when(z == 0)
    def _():
        acc[...] = gs2[...]
        gft[...] = gf[...].T
        hlt[...] = hl[...].T
    def tile(rows):
        gi = nn(gf[rows, :], wd[0, 0])
        g1 = (gi * b[0, rows, :]).astype(BF16)
        g2 = (gi * a[0, rows, :]).astype(BF16)
        gg[0, rows, :] = g1
        gg[1, rows, :] = g2
        acc[rows, :] += nt(g1, wg[0, 0]) + nt(g2, wu[0, 0])
    row_tiles(tile)
    def wtile(rows):
        go[0, 2, rows, :] = nn(gft[rows, :], inner[0]).astype(BF16)
        go[0, 0, rows, :] = nn(hlt[rows, :], gg[0]).astype(BF16)
        go[0, 1, rows, :] = nn(hlt[rows, :], gg[1]).astype(BF16)
    lax.fori_loop(0, 6, lambda i, u: (wtile(pl.ds(pl.multiple_of(i * 128, 128), 128)), u)[1], 0)
    @pl.when(z == 3)
    def _():
        tot = [jnp.zeros((1, D), F32)] * 3
        for i in range(5):
            rows = slice(128 * i, 128 * i + 128)
            gh, n = acc[rows, :], n1[rows, :]
            gs = norm_bwd(gh * vec[1:2, :], n, r1[rows, 0:1])
            gs1o[rows, :] = gs
            gao[rows, :] = gs.astype(BF16)
            tot = [tot[0] + jnp.sum(gh * n, axis=0, keepdims=True), tot[1] + jnp.sum(gh, axis=0, keepdims=True), tot[2] + jnp.sum(gs, axis=0, keepdims=True)]
        vgo[...] = jnp.concatenate(tot + [jnp.zeros((5, D), F32)], axis=0)

def run_kc(W, a, b, inner, gf, hl, gs2, n1, r1, vec):
    c = lambda dt: const((R, D))
    return call(kc, [part(1), part(2), part(3), perz((R, D)), perz((R, D)), perz((R, D)), c(0), c(0), c(0), c(0), const((R, 128)), const((8, D))],
        [(pl.BlockSpec((1, 3, D, D), lambda z: (z, 0, 0, 0)), sds((4, 3, D, D), BF16)), (const((R, D)), sds((R, D), BF16)), (const((R, D)), sds((R, D), F32)), (const((8, D)), sds((8, D), F32))],
        [pltpu.VMEM((R, D), F32), pltpu.VMEM((D, R), BF16), pltpu.VMEM((D, R), BF16), pltpu.VMEM((2, R, D), BF16)],
        "feed_backward", (W, W, W, a, b, inner, gf, hl, gs2, n1, r1, vec), prefetch=0)

def kd(slen, llen, xl, xs, w, small, q8, k, v, ctx, lse, ga, gs1, go, dxo, gbo, xb, dm, kt, gc, gqt, gk, gv, gat, xt, acc, sem):
    z = pl.program_id(0)
    m = lax.axis_index("mp")
    @pl.when(z == 0)
    def _():
        load_rows(m, xl, xs, xb, sem)
        distances(m, slen, llen, dm)
        acc[...] = gs1[...]
        gat[...] = ga[...].T
        xt[...] = xb[...].reshape(R, D).T
        gbo[...] = jnp.zeros_like(gbo)
    wz, sm = w.at[0, 0], small.at[0]
    gc[...] = nt(ga[...], wz[576:768, :]).astype(BF16)
    kt[...] = k[0].T
    attend_bwd(m, sm, q8.at[0], k.at[0], v.at[0], kt, gc, dm, lse.at[0], gqt, gk, gv)
    dq = gqt[...].astype(BF16).T
    dk = gk[...].astype(BF16)
    dv = gv[...].astype(BF16)
    gbo[z, 0:1, 0:192] = jnp.sum(dq.astype(F32), axis=0, keepdims=True)
    gbo[z, 1:2, 0:192] = jnp.sum(dv.astype(F32), axis=0, keepdims=True)
    acc[...] += nn(dq, wz[0:192, :]) + nn(dk, wz[192:384, :]) + nn(dv, wz[384:576, :])
    def wtile(rows):
        xr = xt[rows, :]
        go[0, 0, rows, :] = jnp.concatenate([nn(xr, dq), nn(xr, dk), nn(xr, dv), nn(gat[rows, :], ctx[0])], axis=1).astype(BF16)
    for i in range(6):
        wtile(slice(128 * i, 128 * i + 128))
    @pl.when(z == 3)
    def _():
        dxo[...] = acc[...].astype(BF16)

def run_kd(slen, llen, xl, xs, W, small, q8, k, v, ctx, lse, ga, gs1):
    rz = lambda: perz((R, E))
    rd = const((R, D))
    return call(kd, [ANY, ANY, part(0), perz((8, 256)), rz(), rz(), rz(), rz(), perz((8, R)), rd, rd],
        [(pl.BlockSpec((1, 1, D, D), lambda z, *_: (z, 0, 0, 0)), sds((4, 1, D, D), BF16)), (rd, sds((R, D), BF16)), (const((4, 8, 256)), sds((4, 8, 256), F32))],
        [pltpu.VMEM((5, 128, D), BF16), pltpu.VMEM((5, 512, 128), F32), pltpu.VMEM((E, R), BF16), pltpu.VMEM((R, E), BF16), pltpu.VMEM((E, R), F32), pltpu.VMEM((R, E), F32), pltpu.VMEM((R, E), F32),
         pltpu.VMEM((D, R), BF16), pltpu.VMEM((D, R), BF16), pltpu.VMEM((R, D), F32), pltpu.SemaphoreType.DMA],
        "attention_backward", (slen, llen, xl, xs, W, small, q8, k, v, ctx, lse, ga, gs1))

MESH = pl.DeviceIdType.MESH
GROUPS = ((0, 1), (1, 3))
PR = 96

def place():
    dp = lax.axis_index("dp"); z = lax.axis_index("mp")
    return dp, dp // 4, (dp // 2) % 2, dp % 2, z

def dpi(y, x, c):
    return (y * 2 + x) * 2 + c

def barrier_all(peers):
    b = pltpu.get_barrier_semaphore()
    for d in peers:
        pl.semaphore_signal(b, inc=1, device_id=d, device_id_type=MESH)
    pl.semaphore_wait(b, len(peers))

def ag_kernel(own, small, out, sout, stage, recv, send, loc, ss, sr):
    dp, y, x, c, z = place()
    xn, yn, cn = dpi(y, 1 - x, c), dpi(1 - y, x, c), dpi(y, x, 1 - c)
    dn = dpi(1 - y, 1 - x, c)
    barrier_all([(xn, z), (yn, z), (cn, z)] + [(dp, (z + k) % 4) for k in (1, 2, 3)])
    def sm(k): return pltpu.make_async_remote_copy(src_ref=small, dst_ref=sout.at[z], send_sem=ss.at[k], recv_sem=sr.at[z], device_id=(dp, (z + 1 + k) % 4), device_id_type=MESH)
    for k in range(3): sm(k).start()
    sout[z] = small[...]
    e = 1 - ((z + 1) // 2) % 2
    srcs = [z + 1 - 2 * (z % 2), e * ((z + 2) % 4) + (1 - e) * (3 - z), e * (3 - z) + (1 - e) * ((z + 2) % 4)]

    def rows(p, h):
        if h is None:
            return pl.ds(pl.multiple_of(p * PR, 32), PR)
        return pl.ds(pl.multiple_of(p * PR + h * (PR // 2), 16), PR // 2)
    def piece(s, g, p, h=None):
        a, n = GROUPS[g]
        return out.at[s, pl.ds(a, n), rows(p, h), :]
    def opiece(g, p):
        a, n = GROUPS[g]
        return own.at[pl.ds(a, n), rows(p, None), :]
    def cp(src, dst, s, g, k, r, dev):
        return pltpu.make_async_remote_copy(src_ref=src, dst_ref=dst, send_sem=send.at[s, g, k], recv_sem=recv.at[s, g, r], device_id=dev, device_id_type=MESH)
    def zsend(src, s, g):
        @pl.when((s <= z) & (z < 3))
        def _():
            cp(src, piece(s, g, dp), s, g, 0, 0, (dp, z + 1)).start()
        @pl.when((s >= z) & (z > 0))
        def _():
            cp(src, piece(s, g, dp), s, g, 1, 0, (dp, z - 1)).start()
    def zsend_wait(src, s, g):
        @pl.when((s <= z) & (z < 3))
        def _():
            cp(src, piece(s, g, dp), s, g, 0, 0, (dp, z + 1)).wait_send()
        @pl.when((s >= z) & (z > 0))
        def _():
            cp(src, piece(s, g, dp), s, g, 1, 0, (dp, z - 1)).wait_send()
    def simple(s, g):
        me, xp, yp, dg = dp, xn, yn, dn
        return dict(
            x=lambda: cp(piece(s, g, me), piece(s, g, me), s, g, 2, 1, (xn, z)),
            y=lambda: cp(piece(s, g, me), piece(s, g, me), s, g, 3, 2, (yn, z)),
            c=lambda: cp(piece(s, g, me), piece(s, g, me), s, g, 4, 3, (cn, z)),
            cx=lambda: cp(piece(s, g, xp), piece(s, g, xp), s, g, 5, 4, (cn, z)),
            cy=lambda: cp(piece(s, g, yp), piece(s, g, yp), s, g, 6, 5, (cn, z)),
            yf=lambda: cp(piece(s, g, xp, 0), piece(s, g, xp, 0), s, g, 7, 6, (yn, z)),
            xf=lambda: cp(piece(s, g, yp, 1), piece(s, g, yp, 1), s, g, 8, 7, (xn, z)),
            cd0=lambda: cp(piece(s, g, dg, 0), piece(s, g, dg, 0), s, g, 9, 8, (cn, z)),
            cd1=lambda: cp(piece(s, g, dg, 1), piece(s, g, dg, 1), s, g, 10, 9, (cn, z)),
        )
    def wrecv(ref, s, g, r):
        pltpu.make_async_remote_copy(src_ref=ref, dst_ref=ref, send_sem=send.at[s, g, 0], recv_sem=recv.at[s, g, r], device_id=(cn, z), device_id_type=MESH).wait_recv()
    def zarr(j, g):
        s = srcs[j]
        wrecv(piece(s, g, dp), s, g, 0)
        zsend(piece(s, g, dp), s, g)
        m = simple(s, g)
        m["x"]().start(); m["y"]().start(); m["c"]().start()
    def xyarr(j, g):
        s = srcs[j]; m = simple(s, g)
        wrecv(piece(s, g, xn), s, g, 1)
        m["yf"]().start(); m["cx"]().start()
        wrecv(piece(s, g, yn), s, g, 2)
        m["xf"]().start(); m["cy"]().start()
    def diag(j, g):
        s = srcs[j]; m = simple(s, g)
        wrecv(piece(s, g, dn, 0), s, g, 6)
        m["cd0"]().start()
        wrecv(piece(s, g, dn, 1), s, g, 7)
        m["cd1"]().start()
    def fin(j, g):
        s = srcs[j]; m = simple(s, g)
        zsend_wait(piece(s, g, dp), s, g)
        for k in ("x", "y", "c", "cx", "cy", "yf", "xf", "cd0", "cd1"):
            m[k]().wait_send()
        cdx, cdy, cdd = dpi(y, 1 - x, 1 - c), dpi(1 - y, x, 1 - c), dpi(1 - y, 1 - x, 1 - c)
        wrecv(piece(s, g, cn), s, g, 3)
        wrecv(piece(s, g, cdx), s, g, 4)
        wrecv(piece(s, g, cdy), s, g, 5)
        wrecv(piece(s, g, cdd, 0), s, g, 8)
        wrecv(piece(s, g, cdd, 1), s, g, 9)
    for g in (0, 1):
        zsend(opiece(g, dp), z, g)
    l1 = pltpu.make_async_copy(own, stage, loc.at[0]); l1.start()
    zarr(0, 0)
    zarr(0, 1)
    l1.wait()
    l2 = pltpu.make_async_copy(stage, out.at[z], loc.at[1]); l2.start()
    zarr(1, 0); xyarr(0, 0); zarr(1, 1)
    diag(0, 0); xyarr(0, 1)
    zarr(2, 0); xyarr(1, 0); zarr(2, 1)
    diag(0, 1); diag(1, 0); xyarr(1, 1)
    xyarr(2, 0); diag(2, 0); diag(1, 1); xyarr(2, 1); diag(2, 1)
    for g in (0, 1):
        zsend_wait(opiece(g, dp), z, g)
    for j in range(3):
        for g in (0, 1):
            fin(j, g)
    l2.wait()
    for k in range(3):
        sm(k).wait_send()
        pltpu.make_async_remote_copy(src_ref=small, dst_ref=sout.at[(z + 1 + k) % 4], send_sem=ss.at[k], recv_sem=sr.at[(z + 1 + k) % 4], device_id=(cn, z), device_id_type=MESH).wait_recv()

def gather_weights(own, small):
    A = pl.BlockSpec(memory_space=pl.ANY)
    V = pl.BlockSpec(memory_space=pltpu.VMEM)
    S = pltpu.SemaphoreType.DMA
    return pl.pallas_call(
        ag_kernel,
        out_shape=[jax.ShapeDtypeStruct((4, 4, 768, 768), jnp.bfloat16), jax.ShapeDtypeStruct((4, 8, 256), jnp.float32)],
        in_specs=[A, V], out_specs=[A, V],
        scratch_shapes=[pltpu.VMEM((4, 768, 768), jnp.bfloat16), S((4, 2, 10)), S((4, 2, 11)), S((2,)), S((3,)), S((4,))],
        compiler_params=pltpu.CompilerParams(collective_id=0, has_side_effects=True, vmem_limit_bytes=60 << 20),
        name="gather_weights",
    )(own, small)

ZO = (3, 0, 2, 1)

def far_order(z):
    e = 1 - ((z + 1) // 2) % 2
    return [z + 1 - 2 * (z % 2), e * ((z + 2) % 4) + (1 - e) * (3 - z), e * (3 - z) + (1 - e) * ((z + 2) % 4)]

def out_kernel(g1, g3, yin, dxin, vin, gout, yout, dxout, vout,
               r0, l0, rx, ry, rxy, ryx, rl, rr, stage, vr, vs,
               s0s, s0r, s0l, s1s, s1r, s2s, s2r, ys, yr, vsem_s, vsem_r, loc):
    dp, y, x, c, z = place()
    xn, yn, cn = dpi(y, 1 - x, c), dpi(1 - y, x, c), dpi(y, x, 1 - c)
    z1, z2 = z + 1 - 2 * (z % 2), (z + 2) % 4
    barrier_all([(xn, z), (yn, z), (cn, z)] + [(dp, (z + k) % 4) for k in (1, 2, 3)])

    def rows(p): return pl.ds(pl.multiple_of(p * PR, 32), PR)
    def rc(src, dst, ss, rs, dev):
        return pltpu.make_async_remote_copy(src_ref=src, dst_ref=dst, send_sem=ss, recv_sem=rs, device_id=dev, device_id_type=MESH)
    def st0(zz, q):
        p = dpi(q // 2, q % 2, 1 - c)
        return [rc(g1.at[zz, :, rows(p), :], r0.at[zz, q, pl.ds(0, 1)], s0s.at[zz, q, 0], s0r.at[zz, q, 0], (cn, z)),
                rc(g3.at[zz, :, rows(p), :], r0.at[zz, q, pl.ds(1, 3)], s0s.at[zz, q, 1], s0r.at[zz, q, 1], (cn, z))]
    def ld0(zz, q):
        p = dpi(q // 2, q % 2, c)
        return [pltpu.make_async_copy(g1.at[zz, :, rows(p), :], l0.at[zz, q, pl.ds(0, 1)], s0l.at[zz, q, 0]),
                pltpu.make_async_copy(g3.at[zz, :, rows(p), :], l0.at[zz, q, pl.ds(1, 3)], s0l.at[zz, q, 1])]
    order = far_order(z)
    def blk(s): return 4 * s + s // 3
    def yc(t, src, s, half, right):
        buf = (yout, dxout)[t]
        n, off = (4, 0) if half == 0 else (1, 4)
        dst = buf.at[pl.ds(blk(s) + off, n)]
        if src is None:
            src = dst
        else:
            src = src.at[pl.ds(off, n)]
        return rc(src, dst, ys.at[t, s, half, right], yr.at[t, s, half], (dp, z + 1 if right else z - 1))
    def ysend(t, src, s, act):
        for right in (1, 0):
            @pl.when((s <= z) & (z < 3) if right else (s >= z) & (z > 0))
            def _():
                getattr(yc(t, src, s, 0, right), act)()
                @pl.when(s == 2)
                def _():
                    getattr(yc(t, src, s, 1, right), act)()
    def yarr(t, j):
        s = order[j]
        yc(t, None, s, 0, 1).wait_recv()
        @pl.when(s == 2)
        def _():
            yc(t, None, s, 1, 1).wait_recv()
        ysend(t, None, s, "start")
    vpeer = [(cn, z), (xn, z), (yn, z), (dp, z1), (dp, z2)]
    def vstart(i): rc(vs.at[i], vr.at[i], vsem_s.at[i], vsem_r.at[i], vpeer[i]).start()
    def vstep(i):
        rc(vs.at[i], vr.at[i], vsem_s.at[i], vsem_r.at[i], vpeer[i]).wait_recv()
        tot = vs[i] + vr[i]
        if i < 4:
            vs[i + 1] = tot
            vstart(i + 1)
        else:
            vout[...] = tot

    for q in range(4):
        for d in st0(ZO[0], q): d.start()
        for d in ld0(ZO[0], q): d.start()
    for t, src in enumerate((yin, dxin)):
        ysend(t, src, z, "start")
    for zz in ZO[1:]:
        for q in range(4):
            for d in st0(zz, q): d.start()
            for d in ld0(zz, q): d.start()
    def own(t, which, way):
        n, off = (4, 0) if which == 0 else (1, 4)
        src = (yin, dxin)[t]
        dst = (yout, dxout)[t]
        if way == 0:
            return pltpu.make_async_copy(src.at[pl.ds(off, n)], stage.at[t, pl.ds(off, n)], loc.at[t, which, 0])
        return pltpu.make_async_copy(stage.at[t, pl.ds(off, n)], dst.at[pl.ds(blk(z) + off, n)], loc.at[t, which, 1])
    def ownall(fn):
        for t in (0, 1):
            fn(t, 0)
            @pl.when(z == 2)
            def _():
                fn(t, 1)
    ownall(lambda t, w: own(t, w, 0).start())
    vs[0] = vin[...]
    vstart(0)

    def addinto(dst, src):
        dst[...] = (dst[...].astype(F32) + src[...].astype(F32)).astype(BF16)
    def stage_a(zz):
        for q in range(4):
            for d in st0(zz, q): d.wait_recv()
            for d in ld0(zz, q): d.wait()
        def body(q, u):
            for t in range(4):
                addinto(l0.at[zz, q, t], r0.at[zz, q, t])
            return u
        lax.fori_loop(0, 4, body, 0)
        for k in range(2):
            s1x(zz, k).start(); s1y(zz, k).start()
    def s1x(zz, k):
        return rc(l0.at[zz, 2 * k + 1 - x, pl.ds(0, 2)], rx.at[zz, k], s1s.at[zz, k], s1r.at[zz, k], (xn, z))
    def s1y(zz, k):
        return rc(l0.at[zz, 2 * (1 - y) + k, pl.ds(2, 2)], ry.at[zz, k], s1s.at[zz, 2 + k], s1r.at[zz, 2 + k], (yn, z))
    def s1xy(zz):
        return rc(l0.at[zz, 2 * (1 - y) + x, pl.ds(0, 2)], rxy.at[zz], s1s.at[zz, 4], s1r.at[zz, 4], (yn, z))
    def s1yx(zz):
        return rc(l0.at[zz, 2 * y + 1 - x, pl.ds(2, 2)], ryx.at[zz], s1s.at[zz, 5], s1r.at[zz, 5], (xn, z))
    def stage_b(zz):
        for k in range(2):
            s1x(zz, k).wait_recv()
            for t in range(2):
                addinto(l0.at[zz, 2 * k + x, t], rx.at[zz, k, t])
        s1xy(zz).start()
        for k in range(2):
            s1y(zz, k).wait_recv()
            for t in range(2):
                addinto(l0.at[zz, 2 * y + k, 2 + t], ry.at[zz, k, t])
        s1yx(zz).start()
    def mine(zz): return l0.at[zz, 2 * y + x]
    def stage_c(zz):
        s1xy(zz).wait_recv()
        for t in range(2): addinto(mine(zz).at[t], rxy.at[zz, t])
        s1yx(zz).wait_recv()
        for t in range(2): addinto(mine(zz).at[2 + t], ryx.at[zz, t])
    def zs(zz, right):
        return rc(mine(zz), (rl if right else rr).at[zz], s2s.at[zz], s2r.at[zz, 0 if right else 1], (dp, z + 1 if right else z - 1))
    def stage_d(zz):
        @pl.when(z < zz)
        def _():
            @pl.when(z > 0)
            def _():
                zs(zz, True).wait_recv()
                for t in range(4): addinto(mine(zz).at[t], rl.at[zz, t])
            zs(zz, True).start()
        @pl.when(z > zz)
        def _():
            @pl.when(z < 3)
            def _():
                zs(zz, False).wait_recv()
                for t in range(4): addinto(mine(zz).at[t], rr.at[zz, t])
            zs(zz, False).start()
        @pl.when(z == zz)
        def _():
            for t in range(4): gout[t] = mine(zz)[t].astype(F32)
            if zz > 0:
                zs(zz, True).wait_recv()
                for t in range(4): gout[t] += rl[zz, t].astype(F32)
            if zz < 3:
                zs(zz, False).wait_recv()
                for t in range(4): gout[t] += rr[zz, t].astype(F32)
    A, B, C, Dd = stage_a, stage_b, stage_c, stage_d
    a, b, cc, d = ZO
    A(a); vstep(0); A(b); yarr(0, 0); B(a); vstep(1); A(cc); C(a); A(d)
    ownall(lambda t, w: (own(t, w, 0).wait(), own(t, w, 1).start()))
    vstep(2); yarr(0, 1); B(b); Dd(a); vstep(3); C(b); B(cc); yarr(0, 2); Dd(b); yarr(1, 0); C(cc); vstep(4); B(d); Dd(cc); C(d); yarr(1, 1); Dd(d); yarr(1, 2)
    for zz in ZO:
        for q in range(4):
            for dd in st0(zz, q): dd.wait_send()
        for k in range(2):
            s1x(zz, k).wait_send(); s1y(zz, k).wait_send()
        s1xy(zz).wait_send(); s1yx(zz).wait_send()
        @pl.when(z < zz)
        def _(): zs(zz, True).wait_send()
        @pl.when(z > zz)
        def _(): zs(zz, False).wait_send()
    for t, src in enumerate((yin, dxin)):
        ysend(t, src, z, "wait_send")
        for j in range(3):
            ysend(t, None, order[j], "wait_send")
    for i in range(5):
        rc(vs.at[i], vr.at[i], vsem_s.at[i], vsem_r.at[i], vpeer[i]).wait_send()
    ownall(lambda t, w: own(t, w, 1).wait())

def send_out(g1, g3, yv, dxv, vec):
    A = pl.BlockSpec(memory_space=pl.ANY)
    V = pl.BlockSpec(memory_space=pltpu.VMEM)
    S = pltpu.SemaphoreType.DMA
    b = lambda *s: pltpu.VMEM(s + (PR, 768), BF16)
    return pl.pallas_call(
        out_kernel,
        out_shape=[jax.ShapeDtypeStruct((4, PR, 768), F32), jax.ShapeDtypeStruct((17, 128, 768), BF16), jax.ShapeDtypeStruct((17, 128, 768), BF16), jax.ShapeDtypeStruct((8, 768), F32)],
        in_specs=[A, A, A, A, V], out_specs=[V, A, A, V],
        scratch_shapes=[b(4, 4, 4), b(4, 4, 4), b(4, 2, 2), b(4, 2, 2), b(4, 2), b(4, 2), b(4, 4), b(4, 4), pltpu.VMEM((2, 5, 128, 768), BF16),
                        pltpu.VMEM((5, 8, 768), F32), pltpu.VMEM((5, 8, 768), F32),
                        S((4, 4, 2)), S((4, 4, 2)), S((4, 4, 2)), S((4, 6)), S((4, 6)), S((4,)), S((4, 2)), S((2, 4, 2, 2)), S((2, 4, 2)), S((5,)), S((5,)), S((2, 2, 2))],
        compiler_params=pltpu.CompilerParams(collective_id=1, has_side_effects=True, vmem_limit_bytes=60 << 20),
        name="send_out",
    )(g1, g3, yv, dxv, vec)

def alibi_slopes(slope_index, head_total):
    power = 1 << head_total.bit_length() - 1
    f = slope_index.astype(F32)
    return jnp.where(slope_index < power, jnp.exp2(-8.0 * (f + 1.0) / power), jnp.exp2(-4.0 * (2.0 * (f - power) + 1.0) / power))
def prep(slope_index, w_qkv, b_qv, w_out, w_up, w_down):
    a = jnp.concatenate([jnp.transpose(w_qkv, (1, 2, 0)).reshape(576, D), w_out.T], 0)
    own = jnp.stack([a, w_up[:, 0], w_up[:, 1], w_down], 0)
    bt = jnp.transpose(b_qv, (1, 2, 0)).reshape(2, 192)
    sl = jnp.zeros((1, 192), F32).at[0, 0:3].set(alibi_slopes(slope_index, 12))
    small = jnp.pad(jnp.concatenate([bt, sl], 0), ((0, 5), (0, 64)))
    return own, small
def per_device(x_short, x_long, short_lengths, long_lengths, slope_index, w_qkv, b_qv, w_out, b_out, gain1, bias1, w_up, w_down, b_down, gain2, bias2, cot_short, cot_long):
    own, small = prep(slope_index, w_qkv, b_qv, w_out, w_up, w_down)
    W, S = gather_weights(own, small)
    vec = jnp.stack([b_out, gain1, bias1, b_down, gain2, bias2, bias2, bias2], 0)
    xl, cl = x_long.reshape(8, 128, D), cot_long.reshape(8, 128, D)
    q8, k, v, ctx, lse, n1, r1, hl = run_ka(short_lengths, long_lengths, xl, x_short, W, S, vec)
    a, b, inner, y, gf, gs2, vg2 = run_kb(cl, cot_short, W, hl, n1, vec)
    go3, ga, gs1, vg1 = run_kc(W, a, b, inner, gf, hl, gs2, n1, r1, vec)
    go1, dx, gb = run_kd(short_lengths, long_lengths, xl, x_short, W, S, q8, k, v, ctx, lse, ga, gs1)
    m, dpx = lax.axis_index("mp"), lax.axis_index("dp")
    gbr = jnp.transpose(gb[:, :2, :192], (1, 0, 2)).reshape(2, D)
    vsum = jnp.concatenate([vg2[:3], vg1[:3], gbr], 0)
    G, Y, DX, vs = send_out(go1, go3, y.reshape(5, 128, D), dx.reshape(5, 128, D), vsum)
    b = lax.dynamic_slice(vs[6:8].reshape(2, 12, 64), (0, 3 * m, 8 * dpx), (2, 3, 8))
    vs = lax.dynamic_slice(vs[:6], (0, 96 * dpx), (6, 96))
    gq = G[0][:, :576].reshape(-1, 3, 192)
    return (Y[8:], Y[:8].reshape(2, 512, D), DX[8:], DX[:8].reshape(2, 512, D), gq, jnp.transpose(b, (2, 0, 1)), G[0][:, 576:], vs[5], vs[3], vs[4], jnp.stack([G[1], G[2]], 1), G[3], vs[2], vs[0], vs[1])
def per_device_any(x_short, x_long, short_lengths, long_lengths, slope_index, w_qkv, b_qv, w_out, b_out, gain1, bias1, w_up, w_down, b_down, gain2, bias2, cot_short, cot_long):
    own, small = prep(slope_index, w_qkv, b_qv, w_out, w_up, w_down)
    W = lax.all_gather(own, "mp"); S = lax.all_gather(small, "mp")
    vec = jnp.stack([b_out, gain1, bias1, b_down, gain2, bias2, bias2, bias2], 0)
    xl, cl = x_long.reshape(8, 128, D), cot_long.reshape(8, 128, D)
    q8, k, v, ctx, lse, n1, r1, hl = run_ka(short_lengths, long_lengths, xl, x_short, W, S, vec)
    a, b, inner, y, gf, gs2, vg2 = run_kb(cl, cot_short, W, hl, n1, vec)
    go3, ga, gs1, vg1 = run_kc(W, a, b, inner, gf, hl, gs2, n1, r1, vec)
    go1, dx, gb = run_kd(short_lengths, long_lengths, xl, x_short, W, S, q8, k, v, ctx, lse, ga, gs1)
    m = lax.axis_index("mp")
    def spread(r):
        g = lax.all_gather(r, "mp")
        return jnp.concatenate([g[2], g[3][:512]], 0).reshape(9, 128, D), jnp.stack([g[0][:512], g[1][:512]], 0)
    ys, yl = spread(y); ds, dl = spread(dx)
    G = jnp.concatenate([go1, go3], 1).astype(F32)
    G = lax.psum_scatter(G, "mp", scatter_dimension=0, tiled=True)[0]
    G = lax.psum_scatter(G, "dp", scatter_dimension=1, tiled=True)
    vs = lax.psum(jnp.concatenate([vg2[:3], vg1[:3]], 0), "mp")
    vs = lax.psum_scatter(vs, "dp", scatter_dimension=1, tiled=True)
    gb = lax.psum_scatter(gb[:, :2, :192], "mp", scatter_dimension=0, tiled=True)[0]
    gb = jnp.transpose(gb.reshape(2, 3, 64), (2, 0, 1))
    gb = lax.psum_scatter(gb, "dp", scatter_dimension=0, tiled=True)
    gq = jnp.transpose(G[0][:, :576].reshape(-1, 3, 192), (0, 1, 2))
    return (ys, yl, ds, dl, gq, gb, G[0][:, 576:], vs[5], vs[3], vs[4], jnp.stack([G[1], G[2]], 1), G[3], vs[2], vs[0], vs[1])
def solution(mesh):
    fn = per_device if mesh.shape["dp"] == 8 else per_device_any
    d3 = P("dp", None, None)
    return jax.shard_map(fn, mesh=mesh,
        in_specs=(d3, d3, P("dp"), P("dp"), P("mp"), P(None, None, "mp"), P(None, None, "mp"), P(None, "mp"), P(), P(), P(), P(None, None, "mp"), P(None, "mp"), P(), P(), P(), d3, d3),
        out_specs=(d3, d3, d3, d3, P("dp", None, "mp"), P("dp", None, "mp"), P("dp", "mp"), P("dp"), P("dp"), P("dp"), P("dp", None, "mp"), P("dp", "mp"), P("dp"), P("dp"), P("dp")),
        check_vma=False)
```

```python
import functools
import math

import jax
import jax.numpy as jnp
from jax import lax
from jax.experimental import pallas as pl
from jax.experimental.pallas import tpu as pltpu
from jax.sharding import PartitionSpec as P

F32, BF16 = jnp.float32, jnp.bfloat16
R, D, E = 640, 768, 192
FAR = 1e30
VM = 60 << 20

def nn(a, b): return lax.dot_general(a, b, (((1,), (0,)), ((), ())), preferred_element_type=F32)
def nt(a, b): return lax.dot_general(a, b, (((1,), (1,)), ((), ())), preferred_element_type=F32)

def load_rows(m, long_ref, short_ref, buf, sem):
    @pl.when(m < 2)
    def _():
        c = pltpu.make_async_copy(long_ref.at[pl.ds(4 * m, 4)], buf.at[pl.ds(0, 4)], sem); c.start(); c.wait()
        buf[4] = jnp.zeros((128, D), BF16)
    @pl.when(m == 2)
    def _():
        c = pltpu.make_async_copy(short_ref.at[pl.ds(0, 5)], buf, sem); c.start(); c.wait()
    @pl.when(m == 3)
    def _():
        c = pltpu.make_async_copy(short_ref.at[pl.ds(5, 4)], buf.at[pl.ds(0, 4)], sem); c.start(); c.wait()
        buf[4] = jnp.zeros((128, D), BF16)

def distances(m, slen, llen, dm):
    @pl.when(m < 2)
    def _():
        n = llen[jnp.minimum(m, 1)]
        key = lax.broadcasted_iota(jnp.int32, (512, 128), 0)
        qry = lax.broadcasted_iota(jnp.int32, (512, 128), 1)
        for i in range(4):
            dist = jnp.abs(key - (qry + 128 * i)).astype(F32)
            dm[i] = jnp.where(key < n, dist, FAR)
    @pl.when(m >= 2)
    def _():
        key = lax.broadcasted_iota(jnp.int32, (128, 128), 0)
        qry = lax.broadcasted_iota(jnp.int32, (128, 128), 1)
        dist = jnp.abs(key - qry).astype(F32)
        for i in range(5):
            n = slen[jnp.minimum(5 * (m - 2) + i, 8)] if i == 4 else slen[jnp.maximum(5 * (m - 2), 0) + i]
            dm[i, 0:128, :] = jnp.where(key < n, dist, FAR)

def head_lanes(j):
    return lax.broadcasted_iota(jnp.int32, (1, E), 1) // 64 == j
def head_rows(j):
    return lax.broadcasted_iota(jnp.int32, (E, 1), 0) // 64 == j

def attend_fwd(m, small, q8, k, vt, dm, ct, lse):
    def block(i, keys, koff):
        cols = pl.ds(pl.multiple_of(i * 128, 128), 128)
        qi = q8[cols, :]
        kk = k[pl.ds(koff, keys), :]
        vv = vt[:, pl.ds(koff, keys)]
        d = dm[i, 0:keys, :]
        out = jnp.zeros((E, 128), F32)
        for j in range(3):
            s = nt(kk, jnp.where(head_lanes(j), qi, jnp.zeros_like(qi))) - small[2:3, j:j + 1] * d
            mx = jnp.max(s, axis=0, keepdims=True)
            ex = jnp.exp(s - mx)
            tot = jnp.sum(ex, axis=0, keepdims=True)
            p = (ex * (1.0 / tot)).astype(BF16)
            out = jnp.where(head_rows(j), nn(vv, p), out)
            lse[j:j + 1, cols] = mx + jnp.log(tot)
        ct[:, cols] = out.astype(BF16)
    @pl.when(m < 2)
    def _():
        lax.fori_loop(0, 4, lambda i, u: (block(i, 512, 0), u)[1], 0)
    @pl.when(m >= 2)
    def _():
        lax.fori_loop(0, 5, lambda i, u: (block(i, 128, pl.multiple_of(i * 128, 128)), u)[1], 0)

def attend_bwd(m, small, q8, k, v, kt, gc, dm, lse, gqt, gk, gv):
    gk[...] = jnp.zeros_like(gk)
    gv[...] = jnp.zeros_like(gv)
    def block(i, keys, koff):
        cols = pl.ds(pl.multiple_of(i * 128, 128), 128)
        rows = pl.ds(koff, keys)
        qi, gi = q8[cols, :], gc[cols, :]
        kk, vv, ktt = k[rows, :], v[rows, :], kt[:, rows]
        d = dm[i, 0:keys, :]
        oq = jnp.zeros((E, 128), F32)
        ok = jnp.zeros((keys, E), F32)
        ov = jnp.zeros((keys, E), F32)
        for j in range(3):
            hl = head_lanes(j)
            qj = jnp.where(hl, qi, jnp.zeros_like(qi))
            gj = jnp.where(hl, gi, jnp.zeros_like(gi))
            s = nt(kk, qj) - small[2:3, j:j + 1] * d
            p = jnp.exp(s - lse[j:j + 1, cols])
            gp = nt(vv, gj)
            ov = ov + nn(p.astype(BF16), gj)
            row = jnp.sum(p * gp, axis=0, keepdims=True)
            ds = (p * (gp - row)).astype(BF16)
            oq = jnp.where(head_rows(j), nn(ktt, ds), oq)
            ok = ok + nn(ds, qj)
        gqt[:, cols] = oq * 0.125
        gk[rows, :] += ok
        gv[rows, :] += ov
    @pl.when(m < 2)
    def _():
        lax.fori_loop(0, 4, lambda i, u: (block(i, 512, 0), u)[1], 0)
        gqt[:, 512:640] = jnp.zeros((E, 128), F32)
    @pl.when(m >= 2)
    def _():
        lax.fori_loop(0, 5, lambda i, u: (block(i, 128, pl.multiple_of(i * 128, 128)), u)[1], 0)

def norm_fwd(s):
    mean = jnp.mean(s, axis=1, keepdims=True)
    c = s - mean
    r = lax.rsqrt(jnp.mean(c * c, axis=1, keepdims=True) + 1e-12)
    return c * r, r

def norm_bwd(gn, normed, r):
    return r * (gn - jnp.mean(gn, axis=1, keepdims=True) - normed * jnp.mean(gn * normed, axis=1, keepdims=True))

def row_tiles(fn, tile=640):
    def body(i, u):
        fn(pl.ds(pl.multiple_of(i * tile, tile), tile)); return u
    lax.fori_loop(0, R // tile, body, 0)

def ka(slen, llen, xl, xs, w, small, vec, q8o, ko, vo, co, lseo, n1o, r1o, hlo, xb, dm, vt, ct, acc, sem):
    z = pl.program_id(0)
    m = lax.axis_index("mp")
    @pl.when(z == 0)
    def _():
        load_rows(m, xl, xs, xb, sem)
        distances(m, slen, llen, dm)
        ct[...] = jnp.zeros_like(ct)
        lseo[...] = jnp.zeros_like(lseo)
        acc[...] = jnp.zeros_like(acc)
    x = xb[...].reshape(R, D)
    wz, sm = w.at[0, 0], small.at[0]
    q8o[0] = ((nt(x, wz[0:192, :]) + sm[0:1, 0:192]).astype(BF16).astype(F32) * 0.125).astype(BF16)
    ko[0] = nt(x, wz[192:384, :]).astype(BF16)
    v = (nt(x, wz[384:576, :]) + sm[1:2, 0:192]).astype(BF16)
    vo[0] = v
    vt[...] = v.T
    attend_fwd(m, sm, q8o.at[0], ko.at[0], vt, dm, ct, lseo.at[0])
    co[0] = ct[...].T
    acc[...] += nn(co[0], wz[576:768, :]).astype(BF16).astype(F32)
    @pl.when(z == 3)
    def _():
        for i in range(5):
            rows = slice(128 * i, 128 * i + 128)
            s = xb[i].astype(F32) + acc[rows, :] + vec[0:1, :]
            n, r = norm_fwd(s)
            n1o[rows, :] = n
            r1o[rows, :] = jnp.broadcast_to(r, (128, 128))
            hlo[rows, :] = (n * vec[1:2, :] + vec[2:3, :]).astype(BF16)

def const(shape): return pl.BlockSpec(shape, lambda z, *_: (0,) * len(shape))
def perz(shape): return pl.BlockSpec((1,) + shape, lambda z, *_: (z,) + (0,) * len(shape))
ANY = pl.BlockSpec(memory_space=pl.ANY)
def sds(shape, dt): return jax.ShapeDtypeStruct(shape, dt)
def part(p): return pl.BlockSpec((1, 1, D, D), lambda z, *_: (z, p, 0, 0))

def call(kernel, in_specs, outs, scratch, name, args, grid=(4,), prefetch=2):
    return pl.pallas_call(
        kernel,
        grid_spec=pltpu.PrefetchScalarGridSpec(num_scalar_prefetch=prefetch, grid=grid, in_specs=in_specs,
            out_specs=[o[0] for o in outs], scratch_shapes=scratch),
        out_shape=[o[1] for o in outs],
        compiler_params=pltpu.CompilerParams(dimension_semantics=("arbitrary",), vmem_limit_bytes=VM),
        name=name)(*args)

def run_ka(slen, llen, xl, xs, W, small, vec):
    rz = lambda: (perz((R, E)), sds((4, R, E), BF16))
    return call(ka, [ANY, ANY, part(0), perz((8, 256)), const((8, D))],
        [rz(), rz(), rz(), rz(), (perz((8, R)), sds((4, 8, R), F32)), (const((R, D)), sds((R, D), F32)), (const((R, 128)), sds((R, 128), F32)), (const((R, D)), sds((R, D), BF16))],
        [pltpu.VMEM((5, 128, D), BF16), pltpu.VMEM((5, 512, 128), F32), pltpu.VMEM((E, R), BF16), pltpu.VMEM((E, R), BF16), pltpu.VMEM((R, D), F32), pltpu.SemaphoreType.DMA],
        "attention_forward", (slen, llen, xl, xs, W, small, vec))

def gelu_parts(g):
    cdf = 0.5 * (1.0 + lax.erf(g * (2.0 ** -0.5)))
    pdf = jnp.exp(-0.5 * g * g) * (1.0 / math.sqrt(2 * math.pi))
    return g * cdf, cdf + g * pdf

def kb(cl, cs, wg, wu, wd, hl, n1, vec, ao, bo, io, yo, gfo, gs2o, vgo, acc, cb, sem):
    z = pl.program_id(0)
    m = lax.axis_index("mp")
    @pl.when(z == 0)
    def _():
        load_rows(m, cl, cs, cb, sem)
        acc[...] = jnp.zeros_like(acc)
    def tile(rows):
        h = hl[rows, :]
        gate = nn(h, wg[0, 0])
        up = nn(h, wu[0, 0])
        a, slope = gelu_parts(gate)
        ao[0, rows, :] = a
        bo[0, rows, :] = up * slope
        inner = (a * up).astype(BF16)
        io[0, rows, :] = inner
        acc[rows, :] += nt(inner, wd[0, 0]).astype(BF16).astype(F32)
    row_tiles(tile)
    @pl.when(z == 3)
    def _():
        tot = [jnp.zeros((1, D), F32)] * 3
        for i in range(5):
            rows = slice(128 * i, 128 * i + 128)
            h1 = n1[rows, :] * vec[1:2, :] + vec[2:3, :]
            n, r = norm_fwd(h1 + acc[rows, :] + vec[3:4, :])
            yo[rows, :] = (n * vec[4:5, :] + vec[5:6, :]).astype(BF16)
            gy = cb[i].astype(F32)
            gs = norm_bwd(gy * vec[4:5, :], n, r)
            gs2o[rows, :] = gs
            gfo[rows, :] = gs.astype(BF16)
            tot = [tot[0] + jnp.sum(gy * n, axis=0, keepdims=True), tot[1] + jnp.sum(gy, axis=0, keepdims=True), tot[2] + jnp.sum(gs, axis=0, keepdims=True)]
        vgo[...] = jnp.concatenate(tot + [jnp.zeros((5, D), F32)], axis=0)

def run_kb(cl, cs, W, hl, n1, vec):
    z32 = lambda: (perz((R, D)), sds((4, R, D), F32))
    return call(kb, [ANY, ANY, part(1), part(2), part(3), const((R, D)), const((R, D)), const((8, D))],
        [z32(), z32(), (perz((R, D)), sds((4, R, D), BF16)), (const((R, D)), sds((R, D), BF16)), (const((R, D)), sds((R, D), BF16)), (const((R, D)), sds((R, D), F32)), (const((8, D)), sds((8, D), F32))],
        [pltpu.VMEM((R, D), F32), pltpu.VMEM((5, 128, D), BF16), pltpu.SemaphoreType.DMA],
        "feed_forward", (cl, cs, W, W, W, hl, n1, vec), prefetch=0)

def kc(wg, wu, wd, a, b, inner, gf, hl, gs2, n1, r1, vec, go, gs1o, vgo, acc, gft, hlt, gg):
    z = pl.program_id(0)
    @pl.when(z == 0)
    def _():
        acc[...] = gs2[...]
        gft[...] = gf[...].T
        hlt[...] = hl[...].T
    def tile(rows):
        gi = nn(gf[rows, :], wd[0, 0])
        g1 = (gi * b[0, rows, :]).astype(BF16)
        g2 = (gi * a[0, rows, :]).astype(BF16)
        gg[0, rows, :] = g1
        gg[1, rows, :] = g2
        acc[rows, :] += nt(g1, wg[0, 0]) + nt(g2, wu[0, 0])
    row_tiles(tile)
    def wtile(rows):
        go[0, 2, rows, :] = nn(gft[rows, :], inner[0]).astype(BF16)
        go[0, 0, rows, :] = nn(hlt[rows, :], gg[0]).astype(BF16)
        go[0, 1, rows, :] = nn(hlt[rows, :], gg[1]).astype(BF16)
    wtile(slice(0, D))
    @pl.when(z == 3)
    def _():
        tot = [jnp.zeros((1, D), F32)] * 3
        for i in range(5):
            rows = slice(128 * i, 128 * i + 128)
            gh, n = acc[rows, :], n1[rows, :]
            gs = norm_bwd(gh * vec[1:2, :], n, r1[rows, 0:1])
            gs1o[rows, :] = gs
            tot = [tot[0] + jnp.sum(gh * n, axis=0, keepdims=True), tot[1] + jnp.sum(gh, axis=0, keepdims=True), tot[2] + jnp.sum(gs, axis=0, keepdims=True)]
        vgo[...] = jnp.concatenate(tot + [jnp.zeros((5, D), F32)], axis=0)

def run_kc(W, a, b, inner, gf, hl, gs2, n1, r1, vec):
    c = lambda dt: const((R, D))
    return call(kc, [part(1), part(2), part(3), perz((R, D)), perz((R, D)), perz((R, D)), c(0), c(0), c(0), c(0), const((R, 128)), const((8, D))],
        [(pl.BlockSpec((1, 3, D, D), lambda z: (z, 0, 0, 0)), sds((4, 3, D, D), BF16)), (const((R, D)), sds((R, D), F32)), (const((8, D)), sds((8, D), F32))],
        [pltpu.VMEM((R, D), F32), pltpu.VMEM((D, R), BF16), pltpu.VMEM((D, R), BF16), pltpu.VMEM((2, R, D), BF16)],
        "feed_backward", (W, W, W, a, b, inner, gf, hl, gs2, n1, r1, vec), prefetch=0)

def kd(slen, llen, xl, xs, w, small, q8, k, v, ctx, lse, ga, gs1, go, dxo, gbo, xb, dm, kt, gc, gqt, gk, gv, gat, xt, acc, sem):
    z = pl.program_id(0)
    m = lax.axis_index("mp")
    @pl.when(z == 0)
    def _():
        load_rows(m, xl, xs, xb, sem)
        distances(m, slen, llen, dm)
        acc[...] = gs1[...]
        gat[...] = ga[...].T
        xt[...] = xb[...].reshape(R, D).T
        gbo[...] = jnp.zeros_like(gbo)
    wz, sm = w.at[0, 0], small.at[0]
    gc[...] = nt(ga[...], wz[576:768, :]).astype(BF16)
    kt[...] = k[0].T
    attend_bwd(m, sm, q8.at[0], k.at[0], v.at[0], kt, gc, dm, lse.at[0], gqt, gk, gv)
    dq = gqt[...].astype(BF16).T
    dk = gk[...].astype(BF16)
    dv = gv[...].astype(BF16)
    gbo[z, 0:1, 0:192] = jnp.sum(dq.astype(F32), axis=0, keepdims=True)
    gbo[z, 1:2, 0:192] = jnp.sum(dv.astype(F32), axis=0, keepdims=True)
    acc[...] += nn(dq, wz[0:192, :]) + nn(dk, wz[192:384, :]) + nn(dv, wz[384:576, :])
    def wtile(rows):
        xr = xt[rows, :]
        go[0, 0, rows, :] = jnp.concatenate([nn(xr, dq), nn(xr, dk), nn(xr, dv), nn(gat[rows, :], ctx[0])], axis=1).astype(BF16)
    for i in range(6):
        wtile(slice(128 * i, 128 * i + 128))
    @pl.when(z == 3)
    def _():
        dxo[...] = acc[...].astype(BF16)

def run_kd(slen, llen, xl, xs, W, small, q8, k, v, ctx, lse, ga, gs1):
    rz = lambda: perz((R, E))
    rd = const((R, D))
    return call(kd, [ANY, ANY, part(0), perz((8, 256)), rz(), rz(), rz(), rz(), perz((8, R)), rd, rd],
        [(pl.BlockSpec((1, 1, D, D), lambda z, *_: (z, 0, 0, 0)), sds((4, 1, D, D), BF16)), (rd, sds((R, D), BF16)), (const((4, 8, 256)), sds((4, 8, 256), F32))],
        [pltpu.VMEM((5, 128, D), BF16), pltpu.VMEM((5, 512, 128), F32), pltpu.VMEM((E, R), BF16), pltpu.VMEM((R, E), BF16), pltpu.VMEM((E, R), F32), pltpu.VMEM((R, E), F32), pltpu.VMEM((R, E), F32),
         pltpu.VMEM((D, R), BF16), pltpu.VMEM((D, R), BF16), pltpu.VMEM((R, D), F32), pltpu.SemaphoreType.DMA],
        "attention_backward", (slen, llen, xl, xs, W, small, q8, k, v, ctx, lse, ga, gs1))

MESH = pl.DeviceIdType.MESH
GROUPS = ((0, 1), (1, 3))
PR = 96

def place():
    dp = lax.axis_index("dp"); z = lax.axis_index("mp")
    return dp, dp // 4, (dp // 2) % 2, dp % 2, z

def dpi(y, x, c):
    return (y * 2 + x) * 2 + c

def barrier_all(peers):
    b = pltpu.get_barrier_semaphore()
    for d in peers:
        pl.semaphore_signal(b, inc=1, device_id=d, device_id_type=MESH)
    pl.semaphore_wait(b, len(peers))

def ag_kernel(own, small, out, sout, stage, recv, send, loc, ss, sr):
    dp, y, x, c, z = place()
    xn, yn, cn = dpi(y, 1 - x, c), dpi(1 - y, x, c), dpi(y, x, 1 - c)
    dn = dpi(1 - y, 1 - x, c)
    barrier_all([(xn, z), (yn, z), (cn, z)] + [(dp, (z + k) % 4) for k in (1, 2, 3)])
    def sm(k): return pltpu.make_async_remote_copy(src_ref=small, dst_ref=sout.at[z], send_sem=ss.at[k], recv_sem=sr.at[z], device_id=(dp, (z + 1 + k) % 4), device_id_type=MESH)
    for k in range(3): sm(k).start()
    sout[z] = small[...]
    e = 1 - ((z + 1) // 2) % 2
    srcs = [z + 1 - 2 * (z % 2), e * ((z + 2) % 4) + (1 - e) * (3 - z), e * (3 - z) + (1 - e) * ((z + 2) % 4)]

    def rows(p, h):
        if h is None:
            return pl.ds(pl.multiple_of(p * PR, 32), PR)
        return pl.ds(pl.multiple_of(p * PR + h * (PR // 2), 16), PR // 2)
    def piece(s, g, p, h=None):
        a, n = GROUPS[g]
        return out.at[s, pl.ds(a, n), rows(p, h), :]
    def opiece(g, p):
        a, n = GROUPS[g]
        return own.at[pl.ds(a, n), rows(p, None), :]
    def cp(src, dst, s, g, k, r, dev):
        return pltpu.make_async_remote_copy(src_ref=src, dst_ref=dst, send_sem=send.at[s, g, k], recv_sem=recv.at[s, g, r], device_id=dev, device_id_type=MESH)
    def zsend(src, s, g):
        @pl.when((s <= z) & (z < 3))
        def _():
            cp(src, piece(s, g, dp), s, g, 0, 0, (dp, z + 1)).start()
        @pl.when((s >= z) & (z > 0))
        def _():
            cp(src, piece(s, g, dp), s, g, 1, 0, (dp, z - 1)).start()
    def zsend_wait(src, s, g):
        @pl.when((s <= z) & (z < 3))
        def _():
            cp(src, piece(s, g, dp), s, g, 0, 0, (dp, z + 1)).wait_send()
        @pl.when((s >= z) & (z > 0))
        def _():
            cp(src, piece(s, g, dp), s, g, 1, 0, (dp, z - 1)).wait_send()
    def simple(s, g):
        me, xp, yp, dg = dp, xn, yn, dn
        return dict(
            x=lambda: cp(piece(s, g, me), piece(s, g, me), s, g, 2, 1, (xn, z)),
            y=lambda: cp(piece(s, g, me), piece(s, g, me), s, g, 3, 2, (yn, z)),
            c=lambda: cp(piece(s, g, me), piece(s, g, me), s, g, 4, 3, (cn, z)),
            cx=lambda: cp(piece(s, g, xp), piece(s, g, xp), s, g, 5, 4, (cn, z)),
            cy=lambda: cp(piece(s, g, yp), piece(s, g, yp), s, g, 6, 5, (cn, z)),
            yf=lambda: cp(piece(s, g, xp, 0), piece(s, g, xp, 0), s, g, 7, 6, (yn, z)),
            xf=lambda: cp(piece(s, g, yp, 1), piece(s, g, yp, 1), s, g, 8, 7, (xn, z)),
            cd0=lambda: cp(piece(s, g, dg, 0), piece(s, g, dg, 0), s, g, 9, 8, (cn, z)),
            cd1=lambda: cp(piece(s, g, dg, 1), piece(s, g, dg, 1), s, g, 10, 9, (cn, z)),
        )
    def wrecv(ref, s, g, r):
        pltpu.make_async_remote_copy(src_ref=ref, dst_ref=ref, send_sem=send.at[s, g, 0], recv_sem=recv.at[s, g, r], device_id=(cn, z), device_id_type=MESH).wait_recv()
    def zarr(j, g):
        s = srcs[j]
        wrecv(piece(s, g, dp), s, g, 0)
        zsend(piece(s, g, dp), s, g)
        m = simple(s, g)
        m["x"]().start(); m["y"]().start(); m["c"]().start()
    def xyarr(j, g):
        s = srcs[j]; m = simple(s, g)
        wrecv(piece(s, g, xn), s, g, 1)
        m["yf"]().start(); m["cx"]().start()
        wrecv(piece(s, g, yn), s, g, 2)
        m["xf"]().start(); m["cy"]().start()
    def diag(j, g):
        s = srcs[j]; m = simple(s, g)
        wrecv(piece(s, g, dn, 0), s, g, 6)
        m["cd0"]().start()
        wrecv(piece(s, g, dn, 1), s, g, 7)
        m["cd1"]().start()
    def fin(j, g):
        s = srcs[j]; m = simple(s, g)
        zsend_wait(piece(s, g, dp), s, g)
        for k in ("x", "y", "c", "cx", "cy", "yf", "xf", "cd0", "cd1"):
            m[k]().wait_send()
        cdx, cdy, cdd = dpi(y, 1 - x, 1 - c), dpi(1 - y, x, 1 - c), dpi(1 - y, 1 - x, 1 - c)
        wrecv(piece(s, g, cn), s, g, 3)
        wrecv(piece(s, g, cdx), s, g, 4)
        wrecv(piece(s, g, cdy), s, g, 5)
        wrecv(piece(s, g, cdd, 0), s, g, 8)
        wrecv(piece(s, g, cdd, 1), s, g, 9)
    for g in (0, 1):
        zsend(opiece(g, dp), z, g)
    l1 = pltpu.make_async_copy(own, stage, loc.at[0]); l1.start()
    zarr(0, 0)
    zarr(0, 1)
    l1.wait()
    l2 = pltpu.make_async_copy(stage, out.at[z], loc.at[1]); l2.start()
    zarr(1, 0); xyarr(0, 0); zarr(1, 1)
    diag(0, 0); xyarr(0, 1)
    zarr(2, 0); xyarr(1, 0); zarr(2, 1)
    diag(0, 1); diag(1, 0); xyarr(1, 1)
    xyarr(2, 0); diag(2, 0); diag(1, 1); xyarr(2, 1); diag(2, 1)
    for g in (0, 1):
        zsend_wait(opiece(g, dp), z, g)
    for j in range(3):
        for g in (0, 1):
            fin(j, g)
    l2.wait()
    for k in range(3):
        sm(k).wait_send()
        pltpu.make_async_remote_copy(src_ref=small, dst_ref=sout.at[(z + 1 + k) % 4], send_sem=ss.at[k], recv_sem=sr.at[(z + 1 + k) % 4], device_id=(cn, z), device_id_type=MESH).wait_recv()

def gather_weights(own, small):
    A = pl.BlockSpec(memory_space=pl.ANY)
    V = pl.BlockSpec(memory_space=pltpu.VMEM)
    S = pltpu.SemaphoreType.DMA
    return pl.pallas_call(
        ag_kernel,
        out_shape=[jax.ShapeDtypeStruct((4, 4, 768, 768), jnp.bfloat16), jax.ShapeDtypeStruct((4, 8, 256), jnp.float32)],
        in_specs=[A, V], out_specs=[A, V],
        scratch_shapes=[pltpu.VMEM((4, 768, 768), jnp.bfloat16), S((4, 2, 10)), S((4, 2, 11)), S((2,)), S((3,)), S((4,))],
        compiler_params=pltpu.CompilerParams(collective_id=0, has_side_effects=True, vmem_limit_bytes=60 << 20),
        name="gather_weights",
    )(own, small)

ZO = (3, 0, 2, 1)

def far_order(z):
    e = 1 - ((z + 1) // 2) % 2
    return [z + 1 - 2 * (z % 2), e * ((z + 2) % 4) + (1 - e) * (3 - z), e * (3 - z) + (1 - e) * ((z + 2) % 4)]

H = PR // 2

def zo(g):
    h, e = g // 2, g * (3 - g) // 2
    return (1 - e) * (3 - 2 * h) + e * 2 * h

def add_into(n, dst, src):
    def body(i, u):
        d, r = dst(i), src(i)
        d[...] = (d[...].astype(F32) + r[...].astype(F32)).astype(BF16)
        return u
    lax.fori_loop(0, n, body, 0)

def kx(slen, llen, xl, xs, w, small, q8, k, v, ctx, lse, gs1, g3, yin, vin, gout, yout, dxout, vout,
       xb, dm, kt, gc, gqt, gk, gv, ga, gat, xt, acc, gob, dxs, gbs, stage, vr, vs, l0,
       r03, rx3, ry3, rxy3, ryx3, rl3, rr3, r01, rx1, ry1, rxy1, ryx1, rl1, rr1,
       sem, s0s, s0r, s0l, s1s, s1r, s2s, s2r, ys, yr, vsem_s, vsem_r, loc):
    g = pl.program_id(0)
    dp, y, x, c, z = place()
    xn, yn, cn = dpi(y, 1 - x, c), dpi(1 - y, x, c), dpi(y, x, 1 - c)
    z1, z2 = z + 1 - 2 * (z % 2), (z + 2) % 4
    parts = (1, 3)
    r0, rx, ry, rxy, ryx, rl, rr = (r01, r03), (rx1, rx3), (ry1, ry3), (rxy1, rxy3), (ryx1, ryx3), (rl1, rl3), (rr1, rr3)
    def rows(p): return pl.ds(pl.multiple_of(p * PR, 32), PR)
    def rc(src, dst, ss, rs, dev):
        return pltpu.make_async_remote_copy(src_ref=src, dst_ref=dst, send_sem=ss, recv_sem=rs, device_id=dev, device_id_type=MESH)
    def blk(kd, zz, q):
        return l0.at[zz, q] if kd else gob.at[zz, :, rows(2 * q + c), :]
    def half(kd, zz, q, h):
        return l0.at[zz, q, :, pl.ds(h * H, H), :] if kd else gob.at[zz, :, pl.ds(pl.multiple_of((2 * q + c) * PR + h * H, 16), H), :]
    def st0(kd, zz, q):
        src = (g3 if kd else gob).at[zz, :, rows(2 * q + 1 - c), :]
        return rc(src, r0[kd].at[zz, q], s0s.at[kd, zz, q], s0r.at[kd, zz, q], (cn, z))
    def ld0(zz, q):
        return pltpu.make_async_copy(g3.at[zz, :, rows(2 * q + c), :], l0.at[zz, q], s0l.at[zz, q])
    def stage_0(kd, zz):
        for q in range(4):
            st0(kd, zz, q).start()
            if kd: ld0(zz, q).start()
    def stage_a(kd, zz):
        for q in range(4):
            st0(kd, zz, q).wait_recv()
            if kd: ld0(zz, q).wait()
        n = parts[kd]
        add_into(4 * n, lambda i: blk(kd, zz, i // n).at[i % n], lambda i: r0[kd].at[zz, i // n, i % n])
        for j in range(2):
            s1x(kd, zz, j).start(); s1y(kd, zz, j).start()
    def s1x(kd, zz, j):
        return rc(half(kd, zz, 2 * j + 1 - x, 0), rx[kd].at[zz, j], s1s.at[kd, zz, j], s1r.at[kd, zz, j], (xn, z))
    def s1y(kd, zz, j):
        return rc(half(kd, zz, 2 * (1 - y) + j, 1), ry[kd].at[zz, j], s1s.at[kd, zz, 2 + j], s1r.at[kd, zz, 2 + j], (yn, z))
    def s1xy(kd, zz):
        return rc(half(kd, zz, 2 * (1 - y) + x, 0), rxy[kd].at[zz], s1s.at[kd, zz, 4], s1r.at[kd, zz, 4], (yn, z))
    def s1yx(kd, zz):
        return rc(half(kd, zz, 2 * y + 1 - x, 1), ryx[kd].at[zz], s1s.at[kd, zz, 5], s1r.at[kd, zz, 5], (xn, z))
    def stage_b(kd, zz):
        n = parts[kd]
        for j in range(2): s1x(kd, zz, j).wait_recv()
        add_into(2 * n, lambda i: half(kd, zz, 2 * (i // n) + x, 0).at[i % n], lambda i: rx[kd].at[zz, i // n, i % n])
        s1xy(kd, zz).start()
        for j in range(2): s1y(kd, zz, j).wait_recv()
        add_into(2 * n, lambda i: half(kd, zz, 2 * y + i // n, 1).at[i % n], lambda i: ry[kd].at[zz, i // n, i % n])
        s1yx(kd, zz).start()
    def stage_c(kd, zz):
        n = parts[kd]
        s1xy(kd, zz).wait_recv()
        add_into(n, lambda i: half(kd, zz, 2 * y + x, 0).at[i], lambda i: rxy[kd].at[zz, i])
        s1yx(kd, zz).wait_recv()
        add_into(n, lambda i: half(kd, zz, 2 * y + x, 1).at[i], lambda i: ryx[kd].at[zz, i])
    def mine(kd, zz): return blk(kd, zz, 2 * y + x)
    def zs(kd, zz, right):
        return rc(mine(kd, zz), (rl if right else rr)[kd].at[zz], s2s.at[kd, zz], s2r.at[kd, zz, 0 if right else 1], (dp, z + 1 if right else z - 1))
    def stage_d(kd, zz, hop):
        n = parts[kd]
        if hop < zz:
            @pl.when(z == hop)
            def _():
                if hop > 0:
                    zs(kd, zz, True).wait_recv()
                    add_into(n, lambda i: mine(kd, zz).at[i], lambda i: rl[kd].at[zz, i])
                zs(kd, zz, True).start()
        if 3 - hop > zz:
            @pl.when(z == 3 - hop)
            def _():
                if hop > 0:
                    zs(kd, zz, False).wait_recv()
                    add_into(n, lambda i: mine(kd, zz).at[i], lambda i: rr[kd].at[zz, i])
                zs(kd, zz, False).start()
        if hop == max(zz, 3 - zz):
            @pl.when(z == zz)
            def _():
                if zz > 0: zs(kd, zz, True).wait_recv()
                if zz < 3: zs(kd, zz, False).wait_recv()
                def body(i, u):
                    t = mine(kd, zz)[i].astype(F32)
                    if zz > 0: t += rl[kd][zz, i].astype(F32)
                    if zz < 3: t += rr[kd][zz, i].astype(F32)
                    gout[kd + i] = t
                    return u
                lax.fori_loop(0, n, body, 0)
    order = far_order(z)
    def yb(s): return 4 * s + s // 3
    def yc(t, src, s, hf, right):
        n, off = (4, 0) if hf == 0 else (1, 4)
        dst = (yout, dxout)[t].at[pl.ds(yb(s) + off, n)]
        src = dst if src is None else src.at[pl.ds(off, n)]
        return rc(src, dst, ys.at[t, s, hf, right], yr.at[t, s, hf], (dp, z + 1 if right else z - 1))
    def ysend(t, src, s, act):
        for right in (1, 0):
            @pl.when((s <= z) & (z < 3) if right else (s >= z) & (z > 0))
            def _():
                getattr(yc(t, src, s, 0, right), act)()
                @pl.when(s == 2)
                def _():
                    getattr(yc(t, src, s, 1, right), act)()
    def yarr(t, j):
        s = order[j]
        yc(t, None, s, 0, 1).wait_recv()
        @pl.when(s == 2)
        def _():
            yc(t, None, s, 1, 1).wait_recv()
        ysend(t, None, s, "start")
    def own(t, hf, way):
        n, off = (4, 0) if hf == 0 else (1, 4)
        if way == 0:
            return pltpu.make_async_copy(yin.at[pl.ds(off, n)], stage.at[pl.ds(off, n)], loc.at[t, hf, 0])
        return pltpu.make_async_copy((stage, dxs)[t].at[pl.ds(off, n)], (yout, dxout)[t].at[pl.ds(yb(z) + off, n)], loc.at[t, hf, 1])
    def ownall(fn):
        fn(0)
        @pl.when(z == 2)
        def _():
            fn(1)
    vpeer = [(cn, z), (xn, z), (yn, z), (dp, z1), (dp, z2)]
    def vcopy(i): return rc(vs.at[i], vr.at[i], vsem_s.at[i], vsem_r.at[i], vpeer[i])
    def vstep(i):
        vcopy(i).wait_recv()
        tot = vs[i] + vr[i]
        if i < 4:
            vs[i + 1] = tot
            vcopy(i + 1).start()
        else:
            vout[...] = tot
    F, T, o = 1, 0, ZO
    def S0(kd, u): stage_0(kd, o[u])
    def A(kd, u): stage_a(kd, o[u])
    def B(kd, u): stage_b(kd, o[u])
    def C(kd, u): stage_c(kd, o[u])
    def Z(kd, u, hop): stage_d(kd, o[u], hop)

    @pl.when(g == 0)
    def _():
        barrier_all([(xn, z), (yn, z), (cn, z)] + [(dp, (z + j) % 4) for j in (1, 2, 3)])
        S0(F, 0)
        ysend(0, yin, z, "start")
        ownall(lambda h: own(0, h, 0).start())
        for j in (1, 2, 3): S0(F, j)
        cg = pltpu.make_async_copy(gs1, acc, sem.at[1]); cg.start()
        load_rows(z, xl, xs, xb, sem.at[0])
        distances(z, slen, llen, dm)
        xt[...] = xb[...].reshape(R, D).T
        gbs[...] = jnp.zeros_like(gbs)
        cg.wait()
        ga[...] = acc[...].astype(BF16)
        gat[...] = ga[...].T
        ownall(lambda h: (own(0, h, 0).wait(), own(0, h, 1).start()))
    wz, sm = w.at[0, 0], small.at[0]
    gc[...] = nt(ga[...], wz[576:768, :]).astype(BF16)
    kt[...] = k[0].T
    attend_bwd(z, sm, q8.at[0], k.at[0], v.at[0], kt, gc, dm, lse.at[0], gqt, gk, gv)
    @pl.when(g == 0)
    def _(): A(F, 0)
    @pl.when(g == 1)
    def _(): A(T, 0); B(F, 0)
    @pl.when(g == 2)
    def _(): A(T, 1); B(F, 1); C(F, 0); Z(F, 0, 0)
    @pl.when(g == 3)
    def _(): A(T, 2); B(F, 2); C(F, 1); Z(F, 0, 1); Z(F, 1, 0)
    zg = zo(g)
    dq = gqt[...].astype(BF16).T
    dk = gk[...].astype(BF16)
    dv = gv[...].astype(BF16)
    gbs[zg, 0:1, 0:192] = jnp.sum(dq.astype(F32), axis=0, keepdims=True)
    gbs[zg, 1:2, 0:192] = jnp.sum(dv.astype(F32), axis=0, keepdims=True)
    acc[...] += nn(dq, wz[0:192, :]) + nn(dk, wz[192:384, :]) + nn(dv, wz[384:576, :])
    @pl.when(g == 3)
    def _():
        for i in range(5):
            dxs[i] = acc[128 * i:128 * i + 128, :].astype(BF16)
        ysend(1, dxs, z, "start")
        ownall(lambda h: own(1, h, 1).start())
        vs[0] = vin[...]
        for i in range(4):
            vs[0, 6 + 2 * i:8 + 2 * i, 0:192] = gbs[i, 0:2, 0:192]
        vcopy(0).start()
    for i in range(6):
        rw = slice(128 * i, 128 * i + 128)
        gob[zg, 0, rw, :] = jnp.concatenate([nn(xt[rw, :], dq), nn(xt[rw, :], dk), nn(xt[rw, :], dv), nn(gat[rw, :], ctx[0])], axis=1).astype(BF16)
    @pl.when(g == 0)
    def _(): S0(T, 0); A(F, 1)
    @pl.when(g == 1)
    def _(): S0(T, 1); A(F, 2); yarr(0, 0)
    @pl.when(g == 2)
    def _(): S0(T, 2); A(F, 3); B(T, 0); yarr(0, 1)
    @pl.when(g == 3)
    def _():
        S0(T, 3); C(T, 0); B(T, 1); Z(T, 0, 0); yarr(0, 2); vstep(0); A(T, 3); Z(F, 0, 2); Z(F, 1, 1); B(F, 3); C(F, 2); Z(F, 2, 0)
        B(T, 2); C(T, 1); Z(T, 1, 0); Z(T, 0, 1); vstep(1); B(T, 3); yarr(1, 0); Z(F, 0, 3); Z(F, 1, 2); Z(F, 2, 1); C(F, 3); Z(F, 3, 0); vstep(2)
        C(T, 2); Z(T, 2, 0); C(T, 3); Z(T, 3, 0); Z(T, 0, 2); Z(T, 1, 1); yarr(1, 1); vstep(3); Z(F, 1, 3); Z(F, 2, 2); Z(F, 3, 1)
        Z(T, 1, 2); Z(T, 2, 1); Z(T, 3, 1); Z(T, 0, 3); Z(T, 1, 3); Z(F, 3, 2); Z(T, 2, 2); Z(T, 3, 2); vstep(4); yarr(1, 2)
        for kd in (0, 1):
            for zz in ZO:
                for q in range(4): st0(kd, zz, q).wait_send()
                for j in range(2):
                    s1x(kd, zz, j).wait_send(); s1y(kd, zz, j).wait_send()
                s1xy(kd, zz).wait_send(); s1yx(kd, zz).wait_send()
                @pl.when(z < zz)
                def _(): zs(kd, zz, True).wait_send()
                @pl.when(z > zz)
                def _(): zs(kd, zz, False).wait_send()
        for t, src in enumerate((yin, dxs)):
            ysend(t, src, z, "wait_send")
            for j in range(3):
                ysend(t, None, order[j], "wait_send")
            ownall(lambda h: own(t, h, 1).wait())
        for i in range(5): vcopy(i).wait_send()

def run_kx(slen, llen, xl, xs, W, small, q8, k, v, ctx, lse, gs1, g3, yv, vec):
    pz = lambda *s: pl.BlockSpec((1,) + s, lambda g, *_: (zo(g),) + (0,) * len(s))
    rz = lambda: pz(R, E)
    V, S = pltpu.VMEM, pltpu.SemaphoreType.DMA
    b = lambda *s: V(s + (PR, D), BF16)
    h = lambda *s: V(s + (H, D), BF16)
    bufs = lambda n: [b(4, 4, n), h(4, 2, n), h(4, 2, n), h(4, n), h(4, n), b(4, n), b(4, n)]
    scratch = [V((5, 128, D), BF16), V((5, 512, 128), F32), V((E, R), BF16), V((R, E), BF16), V((E, R), F32), V((R, E), F32), V((R, E), F32),
               V((R, D), BF16), V((D, R), BF16), V((D, R), BF16), V((R, D), F32), V((4, 1, D, D), BF16), V((5, 128, D), BF16), V((4, 8, 256), F32),
               V((5, 128, D), BF16), V((5, 16, D), F32), V((5, 16, D), F32), b(4, 4, 3)] + bufs(3) + bufs(1) + [
               S((2,)), S((2, 4, 4)), S((2, 4, 4)), S((4, 4)), S((2, 4, 6)), S((2, 4, 6)), S((2, 4)), S((2, 4, 2)), S((2, 4, 2, 2)), S((2, 4, 2)), S((5,)), S((5,)), S((2, 2, 2))]
    return pl.pallas_call(
        kx,
        grid_spec=pltpu.PrefetchScalarGridSpec(num_scalar_prefetch=2, grid=(4,),
            in_specs=[ANY, ANY, pl.BlockSpec((1, 1, D, D), lambda g, *_: (zo(g), 0, 0, 0)), pz(8, 256), rz(), rz(), rz(), rz(), pz(8, R), ANY, ANY, ANY, const((16, D))],
            out_specs=[const((4, PR, D)), ANY, ANY, const((16, D))], scratch_shapes=scratch),
        out_shape=[sds((4, PR, D), F32), sds((17, 128, D), BF16), sds((17, 128, D), BF16), sds((16, D), F32)],
        compiler_params=pltpu.CompilerParams(dimension_semantics=("arbitrary",), collective_id=1, has_side_effects=True, vmem_limit_bytes=VM),
        name="attention_backward_send")(slen, llen, xl, xs, W, small, q8, k, v, ctx, lse, gs1, g3, yv, vec)

def alibi_slopes(slope_index, head_total):
    power = 1 << head_total.bit_length() - 1
    f = slope_index.astype(F32)
    return jnp.where(slope_index < power, jnp.exp2(-8.0 * (f + 1.0) / power), jnp.exp2(-4.0 * (2.0 * (f - power) + 1.0) / power))
def prep(slope_index, w_qkv, b_qv, w_out, w_up, w_down):
    a = jnp.concatenate([jnp.transpose(w_qkv, (1, 2, 0)).reshape(576, D), w_out.T], 0)
    own = jnp.stack([a, w_up[:, 0], w_up[:, 1], w_down], 0)
    bt = jnp.transpose(b_qv, (1, 2, 0)).reshape(2, 192)
    sl = jnp.zeros((1, 192), F32).at[0, 0:3].set(alibi_slopes(slope_index, 12))
    small = jnp.pad(jnp.concatenate([bt, sl], 0), ((0, 5), (0, 64)))
    return own, small
def per_device(x_short, x_long, short_lengths, long_lengths, slope_index, w_qkv, b_qv, w_out, b_out, gain1, bias1, w_up, w_down, b_down, gain2, bias2, cot_short, cot_long):
    own, small = prep(slope_index, w_qkv, b_qv, w_out, w_up, w_down)
    W, S = gather_weights(own, small)
    vec = jnp.stack([b_out, gain1, bias1, b_down, gain2, bias2, bias2, bias2], 0)
    xl, cl = x_long.reshape(8, 128, D), cot_long.reshape(8, 128, D)
    q8, k, v, ctx, lse, n1, r1, hl = run_ka(short_lengths, long_lengths, xl, x_short, W, S, vec)
    a, b, inner, y, gf, gs2, vg2 = run_kb(cl, cot_short, W, hl, n1, vec)
    go3, gs1, vg1 = run_kc(W, a, b, inner, gf, hl, gs2, n1, r1, vec)
    m, dpx = lax.axis_index("mp"), lax.axis_index("dp")
    vsum = jnp.concatenate([vg2[:3], vg1[:3], jnp.zeros((10, D), F32)], 0)
    G, Y, DX, vs = run_kx(short_lengths, long_lengths, xl, x_short, W, S, q8, k, v, ctx, lse, gs1, go3, y.reshape(5, 128, D), vsum)
    b = lax.dynamic_slice(vs[6:14, :192].reshape(4, 2, 3, 64), (m, 0, 0, 8 * dpx), (1, 2, 3, 8))[0]
    vs = lax.dynamic_slice(vs[:6], (0, 96 * dpx), (6, 96))
    gq = G[0][:, :576].reshape(-1, 3, 192)
    return (Y[8:], Y[:8].reshape(2, 512, D), DX[8:], DX[:8].reshape(2, 512, D), gq, jnp.transpose(b, (2, 0, 1)), G[0][:, 576:], vs[5], vs[3], vs[4], jnp.stack([G[1], G[2]], 1), G[3], vs[2], vs[0], vs[1])
def per_device_any(x_short, x_long, short_lengths, long_lengths, slope_index, w_qkv, b_qv, w_out, b_out, gain1, bias1, w_up, w_down, b_down, gain2, bias2, cot_short, cot_long):
    own, small = prep(slope_index, w_qkv, b_qv, w_out, w_up, w_down)
    W = lax.all_gather(own, "mp"); S = lax.all_gather(small, "mp")
    vec = jnp.stack([b_out, gain1, bias1, b_down, gain2, bias2, bias2, bias2], 0)
    xl, cl = x_long.reshape(8, 128, D), cot_long.reshape(8, 128, D)
    q8, k, v, ctx, lse, n1, r1, hl = run_ka(short_lengths, long_lengths, xl, x_short, W, S, vec)
    a, b, inner, y, gf, gs2, vg2 = run_kb(cl, cot_short, W, hl, n1, vec)
    go3, gs1, vg1 = run_kc(W, a, b, inner, gf, hl, gs2, n1, r1, vec)
    go1, dx, gb = run_kd(short_lengths, long_lengths, xl, x_short, W, S, q8, k, v, ctx, lse, gs1.astype(BF16), gs1)
    m = lax.axis_index("mp")
    def spread(r):
        g = lax.all_gather(r, "mp")
        return jnp.concatenate([g[2], g[3][:512]], 0).reshape(9, 128, D), jnp.stack([g[0][:512], g[1][:512]], 0)
    ys, yl = spread(y); ds, dl = spread(dx)
    G = jnp.concatenate([go1, go3], 1).astype(F32)
    G = lax.psum_scatter(G, "mp", scatter_dimension=0, tiled=True)[0]
    G = lax.psum_scatter(G, "dp", scatter_dimension=1, tiled=True)
    vs = lax.psum(jnp.concatenate([vg2[:3], vg1[:3]], 0), "mp")
    vs = lax.psum_scatter(vs, "dp", scatter_dimension=1, tiled=True)
    gb = lax.psum_scatter(gb[:, :2, :192], "mp", scatter_dimension=0, tiled=True)[0]
    gb = jnp.transpose(gb.reshape(2, 3, 64), (2, 0, 1))
    gb = lax.psum_scatter(gb, "dp", scatter_dimension=0, tiled=True)
    gq = jnp.transpose(G[0][:, :576].reshape(-1, 3, 192), (0, 1, 2))
    return (ys, yl, ds, dl, gq, gb, G[0][:, 576:], vs[5], vs[3], vs[4], jnp.stack([G[1], G[2]], 1), G[3], vs[2], vs[0], vs[1])
def solution(mesh):
    fn = per_device if mesh.shape["dp"] == 8 else per_device_any
    d3 = P("dp", None, None)
    return jax.shard_map(fn, mesh=mesh,
        in_specs=(d3, d3, P("dp"), P("dp"), P("mp"), P(None, None, "mp"), P(None, None, "mp"), P(None, "mp"), P(), P(), P(), P(None, None, "mp"), P(None, "mp"), P(), P(), P(), d3, d3),
        out_specs=(d3, d3, d3, d3, P("dp", None, "mp"), P("dp", None, "mp"), P("dp", "mp"), P("dp"), P("dp"), P("dp"), P("dp", None, "mp"), P("dp", "mp"), P("dp"), P("dp"), P("dp")),
        check_vma=False)
```

```python
import functools
import math

import jax
import jax.numpy as jnp
from jax import lax
from jax.experimental import pallas as pl
from jax.experimental.pallas import tpu as pltpu
from jax.sharding import PartitionSpec as P

F32, BF16 = jnp.float32, jnp.bfloat16
R, D, E = 640, 768, 192
FAR = 1e30
VM = 60 << 20

def nn(a, b): return lax.dot_general(a, b, (((1,), (0,)), ((), ())), preferred_element_type=F32)
def nt(a, b): return lax.dot_general(a, b, (((1,), (1,)), ((), ())), preferred_element_type=F32)

def load_rows(m, long_ref, short_ref, buf, sem):
    @pl.when(m < 2)
    def _():
        c = pltpu.make_async_copy(long_ref.at[pl.ds(4 * m, 4)], buf.at[pl.ds(0, 4)], sem); c.start(); c.wait()
        buf[4] = jnp.zeros((128, D), BF16)
    @pl.when(m == 2)
    def _():
        c = pltpu.make_async_copy(short_ref.at[pl.ds(0, 5)], buf, sem); c.start(); c.wait()
    @pl.when(m == 3)
    def _():
        c = pltpu.make_async_copy(short_ref.at[pl.ds(5, 4)], buf.at[pl.ds(0, 4)], sem); c.start(); c.wait()
        buf[4] = jnp.zeros((128, D), BF16)

def distances(m, slen, llen, dm):
    @pl.when(m < 2)
    def _():
        n = llen[jnp.minimum(m, 1)]
        key = lax.broadcasted_iota(jnp.int32, (512, 128), 0)
        qry = lax.broadcasted_iota(jnp.int32, (512, 128), 1)
        for i in range(4):
            dist = jnp.abs(key - (qry + 128 * i)).astype(F32)
            dm[i] = jnp.where(key < n, dist, FAR)
    @pl.when(m >= 2)
    def _():
        key = lax.broadcasted_iota(jnp.int32, (128, 128), 0)
        qry = lax.broadcasted_iota(jnp.int32, (128, 128), 1)
        dist = jnp.abs(key - qry).astype(F32)
        for i in range(5):
            n = slen[jnp.minimum(5 * (m - 2) + i, 8)] if i == 4 else slen[jnp.maximum(5 * (m - 2), 0) + i]
            dm[i, 0:128, :] = jnp.where(key < n, dist, FAR)

def head_lanes(j):
    return lax.broadcasted_iota(jnp.int32, (1, E), 1) // 64 == j
def head_rows(j):
    return lax.broadcasted_iota(jnp.int32, (E, 1), 0) // 64 == j

def attend_fwd(m, small, q8, k, vt, dm, ct, lse, hook=lambda i: None):
    def block(i, keys, koff):
        cols = pl.ds(pl.multiple_of(i * 128, 128), 128)
        qi = q8[cols, :]
        kk = k[pl.ds(koff, keys), :]
        vv = vt[:, pl.ds(koff, keys)]
        d = dm[i, 0:keys, :]
        out = jnp.zeros((E, 128), F32)
        for j in range(3):
            s = nt(kk, jnp.where(head_lanes(j), qi, jnp.zeros_like(qi))) - small[2:3, j:j + 1] * d
            mx = jnp.max(s, axis=0, keepdims=True)
            ex = jnp.exp(s - mx)
            tot = jnp.sum(ex, axis=0, keepdims=True)
            p = (ex * (1.0 / tot)).astype(BF16)
            out = jnp.where(head_rows(j), nn(vv, p), out)
            lse[j:j + 1, cols] = mx + jnp.log(tot)
        ct[:, cols] = out.astype(BF16)
    @pl.when(m < 2)
    def _():
        lax.fori_loop(0, 4, lambda i, u: (block(i, 512, 0), hook(i), u)[2], 0)
    @pl.when(m >= 2)
    def _():
        lax.fori_loop(0, 5, lambda i, u: (block(i, 128, pl.multiple_of(i * 128, 128)), hook(i), u)[2], 0)

def attend_bwd(m, small, q8, k, v, kt, gc, dm, lse, gqt, gk, gv):
    gk[...] = jnp.zeros_like(gk)
    gv[...] = jnp.zeros_like(gv)
    def block(i, keys, koff):
        cols = pl.ds(pl.multiple_of(i * 128, 128), 128)
        rows = pl.ds(koff, keys)
        qi, gi = q8[cols, :], gc[cols, :]
        kk, vv, ktt = k[rows, :], v[rows, :], kt[:, rows]
        d = dm[i, 0:keys, :]
        oq = jnp.zeros((E, 128), F32)
        ok = jnp.zeros((keys, E), F32)
        ov = jnp.zeros((keys, E), F32)
        for j in range(3):
            hl = head_lanes(j)
            qj = jnp.where(hl, qi, jnp.zeros_like(qi))
            gj = jnp.where(hl, gi, jnp.zeros_like(gi))
            s = nt(kk, qj) - small[2:3, j:j + 1] * d
            p = jnp.exp(s - lse[j:j + 1, cols])
            gp = nt(vv, gj)
            ov = ov + nn(p.astype(BF16), gj)
            row = jnp.sum(p * gp, axis=0, keepdims=True)
            ds = (p * (gp - row)).astype(BF16)
            oq = jnp.where(head_rows(j), nn(ktt, ds), oq)
            ok = ok + nn(ds, qj)
        gqt[:, cols] = oq * 0.125
        gk[rows, :] += ok
        gv[rows, :] += ov
    @pl.when(m < 2)
    def _():
        lax.fori_loop(0, 4, lambda i, u: (block(i, 512, 0), u)[1], 0)
        gqt[:, 512:640] = jnp.zeros((E, 128), F32)
    @pl.when(m >= 2)
    def _():
        lax.fori_loop(0, 5, lambda i, u: (block(i, 128, pl.multiple_of(i * 128, 128)), u)[1], 0)

def norm_fwd(s):
    mean = jnp.mean(s, axis=1, keepdims=True)
    c = s - mean
    r = lax.rsqrt(jnp.mean(c * c, axis=1, keepdims=True) + 1e-12)
    return c * r, r

def norm_bwd(gn, normed, r):
    return r * (gn - jnp.mean(gn, axis=1, keepdims=True) - normed * jnp.mean(gn * normed, axis=1, keepdims=True))

def row_tiles(fn, tile=640):
    def body(i, u):
        fn(pl.ds(pl.multiple_of(i * tile, tile), tile)); return u
    lax.fori_loop(0, R // tile, body, 0)

def ka(slen, llen, xl, xs, w, small, vec, q8o, ko, vo, co, lseo, n1o, r1o, hlo, xb, dm, vt, ct, acc, sem):
    z = pl.program_id(0)
    m = lax.axis_index("mp")
    @pl.when(z == 0)
    def _():
        load_rows(m, xl, xs, xb, sem)
        distances(m, slen, llen, dm)
        ct[...] = jnp.zeros_like(ct)
        lseo[...] = jnp.zeros_like(lseo)
        acc[...] = jnp.zeros_like(acc)
    x = xb[...].reshape(R, D)
    wz, sm = w.at[0, 0], small.at[0]
    q8o[0] = ((nt(x, wz[0:192, :]) + sm[0:1, 0:192]).astype(BF16).astype(F32) * 0.125).astype(BF16)
    ko[0] = nt(x, wz[192:384, :]).astype(BF16)
    v = (nt(x, wz[384:576, :]) + sm[1:2, 0:192]).astype(BF16)
    vo[0] = v
    vt[...] = v.T
    attend_fwd(m, sm, q8o.at[0], ko.at[0], vt, dm, ct, lseo.at[0])
    co[0] = ct[...].T
    acc[...] += nn(co[0], wz[576:768, :]).astype(BF16).astype(F32)
    @pl.when(z == 3)
    def _():
        for i in range(5):
            rows = slice(128 * i, 128 * i + 128)
            s = xb[i].astype(F32) + acc[rows, :] + vec[0:1, :]
            n, r = norm_fwd(s)
            n1o[rows, :] = n
            r1o[rows, :] = jnp.broadcast_to(r, (128, 128))
            hlo[rows, :] = (n * vec[1:2, :] + vec[2:3, :]).astype(BF16)

def const(shape): return pl.BlockSpec(shape, lambda z, *_: (0,) * len(shape))
def perz(shape): return pl.BlockSpec((1,) + shape, lambda z, *_: (z,) + (0,) * len(shape))
ANY = pl.BlockSpec(memory_space=pl.ANY)
def sds(shape, dt): return jax.ShapeDtypeStruct(shape, dt)
def part(p): return pl.BlockSpec((1, 1, D, D), lambda z, *_: (z, p, 0, 0))

def call(kernel, in_specs, outs, scratch, name, args, grid=(4,), prefetch=2):
    return pl.pallas_call(
        kernel,
        grid_spec=pltpu.PrefetchScalarGridSpec(num_scalar_prefetch=prefetch, grid=grid, in_specs=in_specs,
            out_specs=[o[0] for o in outs], scratch_shapes=scratch),
        out_shape=[o[1] for o in outs],
        compiler_params=pltpu.CompilerParams(dimension_semantics=("arbitrary",), vmem_limit_bytes=VM),
        name=name)(*args)

def run_ka(slen, llen, xl, xs, W, small, vec):
    rz = lambda: (perz((R, E)), sds((4, R, E), BF16))
    return call(ka, [ANY, ANY, part(0), perz((8, 256)), const((8, D))],
        [rz(), rz(), rz(), rz(), (perz((8, R)), sds((4, 8, R), F32)), (const((R, D)), sds((R, D), F32)), (const((R, 128)), sds((R, 128), F32)), (const((R, D)), sds((R, D), BF16))],
        [pltpu.VMEM((5, 128, D), BF16), pltpu.VMEM((5, 512, 128), F32), pltpu.VMEM((E, R), BF16), pltpu.VMEM((E, R), BF16), pltpu.VMEM((R, D), F32), pltpu.SemaphoreType.DMA],
        "attention_forward", (slen, llen, xl, xs, W, small, vec))

def gelu_parts(g):
    cdf = 0.5 * (1.0 + lax.erf(g * (2.0 ** -0.5)))
    pdf = jnp.exp(-0.5 * g * g) * (1.0 / math.sqrt(2 * math.pi))
    return g * cdf, cdf + g * pdf

def kb(cl, cs, wg, wu, wd, hl, n1, vec, ao, bo, io, yo, gfo, gs2o, vgo, acc, cb, sem):
    z = pl.program_id(0)
    m = lax.axis_index("mp")
    @pl.when(z == 0)
    def _():
        load_rows(m, cl, cs, cb, sem)
        acc[...] = jnp.zeros_like(acc)
    def tile(rows):
        h = hl[rows, :]
        gate = nn(h, wg[0, 0])
        up = nn(h, wu[0, 0])
        a, slope = gelu_parts(gate)
        ao[0, rows, :] = a
        bo[0, rows, :] = up * slope
        inner = (a * up).astype(BF16)
        io[0, rows, :] = inner
        acc[rows, :] += nt(inner, wd[0, 0]).astype(BF16).astype(F32)
    row_tiles(tile)
    @pl.when(z == 3)
    def _():
        tot = [jnp.zeros((1, D), F32)] * 3
        for i in range(5):
            rows = slice(128 * i, 128 * i + 128)
            h1 = n1[rows, :] * vec[1:2, :] + vec[2:3, :]
            n, r = norm_fwd(h1 + acc[rows, :] + vec[3:4, :])
            yo[rows, :] = (n * vec[4:5, :] + vec[5:6, :]).astype(BF16)
            gy = cb[i].astype(F32)
            gs = norm_bwd(gy * vec[4:5, :], n, r)
            gs2o[rows, :] = gs
            gfo[rows, :] = gs.astype(BF16)
            tot = [tot[0] + jnp.sum(gy * n, axis=0, keepdims=True), tot[1] + jnp.sum(gy, axis=0, keepdims=True), tot[2] + jnp.sum(gs, axis=0, keepdims=True)]
        vgo[...] = jnp.concatenate(tot + [jnp.zeros((5, D), F32)], axis=0)

def run_kb(cl, cs, W, hl, n1, vec):
    z32 = lambda: (perz((R, D)), sds((4, R, D), F32))
    return call(kb, [ANY, ANY, part(1), part(2), part(3), const((R, D)), const((R, D)), const((8, D))],
        [z32(), z32(), (perz((R, D)), sds((4, R, D), BF16)), (const((R, D)), sds((R, D), BF16)), (const((R, D)), sds((R, D), BF16)), (const((R, D)), sds((R, D), F32)), (const((8, D)), sds((8, D), F32))],
        [pltpu.VMEM((R, D), F32), pltpu.VMEM((5, 128, D), BF16), pltpu.SemaphoreType.DMA],
        "feed_forward", (cl, cs, W, W, W, hl, n1, vec), prefetch=0)

def kc(wg, wu, wd, a, b, inner, gf, hl, gs2, n1, r1, vec, go, gs1o, vgo, acc, gft, hlt, gg):
    z = pl.program_id(0)
    @pl.when(z == 0)
    def _():
        acc[...] = gs2[...]
        gft[...] = gf[...].T
        hlt[...] = hl[...].T
    def tile(rows):
        gi = nn(gf[rows, :], wd[0, 0])
        g1 = (gi * b[0, rows, :]).astype(BF16)
        g2 = (gi * a[0, rows, :]).astype(BF16)
        gg[0, rows, :] = g1
        gg[1, rows, :] = g2
        acc[rows, :] += nt(g1, wg[0, 0]) + nt(g2, wu[0, 0])
    row_tiles(tile)
    def wtile(rows):
        go[0, 2, rows, :] = nn(gft[rows, :], inner[0]).astype(BF16)
        go[0, 0, rows, :] = nn(hlt[rows, :], gg[0]).astype(BF16)
        go[0, 1, rows, :] = nn(hlt[rows, :], gg[1]).astype(BF16)
    wtile(slice(0, D))
    @pl.when(z == 3)
    def _():
        tot = [jnp.zeros((1, D), F32)] * 3
        for i in range(5):
            rows = slice(128 * i, 128 * i + 128)
            gh, n = acc[rows, :], n1[rows, :]
            gs = norm_bwd(gh * vec[1:2, :], n, r1[rows, 0:1])
            gs1o[rows, :] = gs
            tot = [tot[0] + jnp.sum(gh * n, axis=0, keepdims=True), tot[1] + jnp.sum(gh, axis=0, keepdims=True), tot[2] + jnp.sum(gs, axis=0, keepdims=True)]
        vgo[...] = jnp.concatenate(tot + [jnp.zeros((5, D), F32)], axis=0)

def run_kc(W, a, b, inner, gf, hl, gs2, n1, r1, vec):
    c = lambda dt: const((R, D))
    return call(kc, [part(1), part(2), part(3), perz((R, D)), perz((R, D)), perz((R, D)), c(0), c(0), c(0), c(0), const((R, 128)), const((8, D))],
        [(pl.BlockSpec((1, 3, D, D), lambda z: (z, 0, 0, 0)), sds((4, 3, D, D), BF16)), (const((R, D)), sds((R, D), F32)), (const((8, D)), sds((8, D), F32))],
        [pltpu.VMEM((R, D), F32), pltpu.VMEM((D, R), BF16), pltpu.VMEM((D, R), BF16), pltpu.VMEM((2, R, D), BF16)],
        "feed_backward", (W, W, W, a, b, inner, gf, hl, gs2, n1, r1, vec), prefetch=0)

def kd(slen, llen, xl, xs, w, small, q8, k, v, ctx, lse, ga, gs1, go, dxo, gbo, xb, dm, kt, gc, gqt, gk, gv, gat, xt, acc, sem):
    z = pl.program_id(0)
    m = lax.axis_index("mp")
    @pl.when(z == 0)
    def _():
        load_rows(m, xl, xs, xb, sem)
        distances(m, slen, llen, dm)
        acc[...] = gs1[...]
        gat[...] = ga[...].T
        xt[...] = xb[...].reshape(R, D).T
        gbo[...] = jnp.zeros_like(gbo)
    wz, sm = w.at[0, 0], small.at[0]
    gc[...] = nt(ga[...], wz[576:768, :]).astype(BF16)
    kt[...] = k[0].T
    attend_bwd(m, sm, q8.at[0], k.at[0], v.at[0], kt, gc, dm, lse.at[0], gqt, gk, gv)
    dq = gqt[...].astype(BF16).T
    dk = gk[...].astype(BF16)
    dv = gv[...].astype(BF16)
    gbo[z, 0:1, 0:192] = jnp.sum(dq.astype(F32), axis=0, keepdims=True)
    gbo[z, 1:2, 0:192] = jnp.sum(dv.astype(F32), axis=0, keepdims=True)
    acc[...] += nn(dq, wz[0:192, :]) + nn(dk, wz[192:384, :]) + nn(dv, wz[384:576, :])
    def wtile(rows):
        xr = xt[rows, :]
        go[0, 0, rows, :] = jnp.concatenate([nn(xr, dq), nn(xr, dk), nn(xr, dv), nn(gat[rows, :], ctx[0])], axis=1).astype(BF16)
    for i in range(6):
        wtile(slice(128 * i, 128 * i + 128))
    @pl.when(z == 3)
    def _():
        dxo[...] = acc[...].astype(BF16)

def run_kd(slen, llen, xl, xs, W, small, q8, k, v, ctx, lse, ga, gs1):
    rz = lambda: perz((R, E))
    rd = const((R, D))
    return call(kd, [ANY, ANY, part(0), perz((8, 256)), rz(), rz(), rz(), rz(), perz((8, R)), rd, rd],
        [(pl.BlockSpec((1, 1, D, D), lambda z, *_: (z, 0, 0, 0)), sds((4, 1, D, D), BF16)), (rd, sds((R, D), BF16)), (const((4, 8, 256)), sds((4, 8, 256), F32))],
        [pltpu.VMEM((5, 128, D), BF16), pltpu.VMEM((5, 512, 128), F32), pltpu.VMEM((E, R), BF16), pltpu.VMEM((R, E), BF16), pltpu.VMEM((E, R), F32), pltpu.VMEM((R, E), F32), pltpu.VMEM((R, E), F32),
         pltpu.VMEM((D, R), BF16), pltpu.VMEM((D, R), BF16), pltpu.VMEM((R, D), F32), pltpu.SemaphoreType.DMA],
        "attention_backward", (slen, llen, xl, xs, W, small, q8, k, v, ctx, lse, ga, gs1))

MESH = pl.DeviceIdType.MESH
PR = 96

def place():
    dp = lax.axis_index("dp"); z = lax.axis_index("mp")
    return dp, dp // 4, (dp // 2) % 2, dp % 2, z

def dpi(y, x, c):
    return (y * 2 + x) * 2 + c

def barrier_all(peers):
    b = pltpu.get_barrier_semaphore()
    for d in peers:
        pl.semaphore_signal(b, inc=1, device_id=d, device_id_type=MESH)
    pl.semaphore_wait(b, len(peers))

def kg(slen, llen, own, small, xl, xs, vec, out, sout, q8o, ko, vo, co, lseo, n1o, r1o, hlo,
       stage, ssm, xb, dm, vt, ct, acc, wz, recv, send, loc, ss, sr, sem):
    g = pl.program_id(0)
    dp, y, x, c, z = place()
    xn, yn, cn = dpi(y, 1 - x, c), dpi(1 - y, x, c), dpi(y, x, 1 - c)
    dn = dpi(1 - y, 1 - x, c)
    def sm(j): return pltpu.make_async_remote_copy(src_ref=small, dst_ref=ssm.at[z], send_sem=ss.at[j], recv_sem=sr.at[z], device_id=(dp, (z + 1 + j) % 4), device_id_type=MESH)
    e = 1 - ((z + 1) // 2) % 2
    srcs = [z + 1 - 2 * (z % 2), e * ((z + 2) % 4) + (1 - e) * (3 - z), e * (3 - z) + (1 - e) * ((z + 2) % 4)]

    def rows(p, h):
        if h is None:
            return pl.ds(pl.multiple_of(p * PR, 32), PR)
        return pl.ds(pl.multiple_of(p * PR + h * (PR // 2), 16), PR // 2)
    def piece(s, g, p, h=None):
        return out.at[s, g, rows(p, h), :]
    def opiece(g, p):
        return own.at[g, rows(p, None), :]
    def cp(src, dst, s, g, k, r, dev):
        return pltpu.make_async_remote_copy(src_ref=src, dst_ref=dst, send_sem=send.at[s, g, k], recv_sem=recv.at[s, g, r], device_id=dev, device_id_type=MESH)
    def zsend(src, s, g):
        @pl.when((s <= z) & (z < 3))
        def _():
            cp(src, piece(s, g, dp), s, g, 0, 0, (dp, z + 1)).start()
        @pl.when((s >= z) & (z > 0))
        def _():
            cp(src, piece(s, g, dp), s, g, 1, 0, (dp, z - 1)).start()
    def zsend_wait(src, s, g):
        @pl.when((s <= z) & (z < 3))
        def _():
            cp(src, piece(s, g, dp), s, g, 0, 0, (dp, z + 1)).wait_send()
        @pl.when((s >= z) & (z > 0))
        def _():
            cp(src, piece(s, g, dp), s, g, 1, 0, (dp, z - 1)).wait_send()
    def simple(s, g):
        me, xp, yp, dg = dp, xn, yn, dn
        return dict(
            x=lambda: cp(piece(s, g, me), piece(s, g, me), s, g, 2, 1, (xn, z)),
            y=lambda: cp(piece(s, g, me), piece(s, g, me), s, g, 3, 2, (yn, z)),
            c=lambda: cp(piece(s, g, me), piece(s, g, me), s, g, 4, 3, (cn, z)),
            cx=lambda: cp(piece(s, g, xp), piece(s, g, xp), s, g, 5, 4, (cn, z)),
            cy=lambda: cp(piece(s, g, yp), piece(s, g, yp), s, g, 6, 5, (cn, z)),
            yf=lambda: cp(piece(s, g, xp, 0), piece(s, g, xp, 0), s, g, 7, 6, (yn, z)),
            xf=lambda: cp(piece(s, g, yp, 1), piece(s, g, yp, 1), s, g, 8, 7, (xn, z)),
            cd0=lambda: cp(piece(s, g, dg, 0), piece(s, g, dg, 0), s, g, 9, 8, (cn, z)),
            cd1=lambda: cp(piece(s, g, dg, 1), piece(s, g, dg, 1), s, g, 10, 9, (cn, z)),
        )
    def wrecv(ref, s, g, r):
        pltpu.make_async_remote_copy(src_ref=ref, dst_ref=ref, send_sem=send.at[s, g, 0], recv_sem=recv.at[s, g, r], device_id=(cn, z), device_id_type=MESH).wait_recv()
    def zarr(j, g):
        s = srcs[j]
        wrecv(piece(s, g, dp), s, g, 0)
        zsend(piece(s, g, dp), s, g)
        m = simple(s, g)
        m["x"]().start(); m["y"]().start(); m["c"]().start()
    def xyarr(j, g):
        s = srcs[j]; m = simple(s, g)
        wrecv(piece(s, g, xn), s, g, 1)
        m["yf"]().start(); m["cx"]().start()
        wrecv(piece(s, g, yn), s, g, 2)
        m["xf"]().start(); m["cy"]().start()
    def diag(j, g):
        s = srcs[j]; m = simple(s, g)
        wrecv(piece(s, g, dn, 0), s, g, 6)
        m["cd0"]().start()
        wrecv(piece(s, g, dn, 1), s, g, 7)
        m["cd1"]().start()
    def landed(j, g):
        s = srcs[j]
        cdx, cdy, cdd = dpi(y, 1 - x, 1 - c), dpi(1 - y, x, 1 - c), dpi(1 - y, 1 - x, 1 - c)
        wrecv(piece(s, g, cn), s, g, 3)
        wrecv(piece(s, g, cdx), s, g, 4)
        wrecv(piece(s, g, cdy), s, g, 5)
        wrecv(piece(s, g, cdd, 0), s, g, 8)
        wrecv(piece(s, g, cdd, 1), s, g, 9)
    def sent(j, g):
        s = srcs[j]; m = simple(s, g)
        zsend_wait(piece(s, g, dp), s, g)
        for k in ("x", "y", "c", "cx", "cy", "yf", "xf", "cd0", "cd1"):
            m[k]().wait_send()
    l1 = pltpu.make_async_copy(own, stage, loc.at[0])
    l2 = pltpu.make_async_copy(stage, out.at[z], loc.at[1])
    def fetch(j):
        landed(j, 0)
        cw = pltpu.make_async_copy(out.at[srcs[j], 0], wz, sem.at[1]); cw.start()
        pltpu.make_async_remote_copy(src_ref=small, dst_ref=ssm.at[srcs[j]], send_sem=ss.at[j], recv_sem=sr.at[srcs[j]], device_id=(cn, z), device_id_type=MESH).wait_recv()
        cw.wait()
    Z, XY, DG = zarr, xyarr, diag
    def mine(p): zsend(opiece(p, dp), z, p)
    def at(n, fn):
        @pl.when(g == n)
        def _(): fn()

    @pl.when(g == 0)
    def _():
        barrier_all([(xn, z), (yn, z), (cn, z)] + [(dp, (z + j) % 4) for j in (1, 2, 3)])
        mine(0); mine(2); mine(3)
        for j in range(3): sm(j).start()
        cw = pltpu.make_async_copy(own.at[0], wz, sem.at[1]); cw.start()
        l1.start()
        ssm[z] = small[...]
        load_rows(z, xl, xs, xb, sem.at[0])
        distances(z, slen, llen, dm)
        ct[...] = jnp.zeros_like(ct)
        lseo[...] = jnp.zeros_like(lseo)
        acc[...] = jnp.zeros_like(acc)
        cw.wait()
        Z(0, 0); mine(1)
    zz = jnp.where(g == 0, z, jnp.where(g == 1, srcs[0], jnp.where(g == 2, srcs[1], srcs[2])))
    xv = xb[...].reshape(R, D)
    bs = ssm.at[zz]
    q8o[zz] = ((nt(xv, wz[0:192, :]) + bs[0:1, 0:192]).astype(BF16).astype(F32) * 0.125).astype(BF16)
    ko[zz] = nt(xv, wz[192:384, :]).astype(BF16)
    v = (nt(xv, wz[384:576, :]) + bs[1:2, 0:192]).astype(BF16)
    vo[zz] = v
    vt[...] = v.T
    at(0, lambda: Z(0, 2))
    at(1, lambda: XY(0, 3))
    at(3, lambda: DG(0, 3))
    def hook(i):
        def on(n, j, fn):
            @pl.when((g == n) & (i == j))
            def _(): fn()
        on(0, 0, lambda: (Z(0, 3), XY(0, 0), Z(1, 0), Z(2, 0)))
        on(0, 1, lambda: Z(0, 1))
        on(0, 2, lambda: (DG(0, 0), XY(1, 0)))
        on(0, 3, lambda: (XY(0, 2), Z(1, 3)))
        on(1, 0, lambda: Z(2, 2))
        on(1, 2, lambda: (DG(1, 0), Z(1, 2)))
        on(2, 0, lambda: Z(2, 1))
        on(2, 1, lambda: XY(1, 3))
        on(2, 3, lambda: (Z(2, 3), XY(1, 2)))
        on(3, 1, lambda: (XY(1, 1), XY(2, 3)))
    attend_fwd(z, bs, q8o.at[zz], ko.at[zz], vt, dm, ct, lseo.at[zz], hook)
    cv = ct[...].T
    co[zz] = cv
    acc[...] += nn(cv, wz[576:768, :]).astype(BF16).astype(F32)
    at(0, lambda: (l1.wait(), l2.start(), XY(2, 0), fetch(0), Z(1, 1),))
    at(1, lambda: (fetch(1), DG(2, 0),))
    at(2, lambda: (fetch(2), XY(2, 2), XY(0, 1),))
    @pl.when(g == 3)
    def _():
        XY(2, 1); DG(2, 2)
        sout[...] = ssm[...]
        for i in range(5):
            rw = slice(128 * i, 128 * i + 128)
            s = xb[i].astype(F32) + acc[rw, :] + vec[0:1, :]
            n, r = norm_fwd(s)
            n1o[rw, :] = n
            r1o[rw, :] = jnp.broadcast_to(r, (128, 128))
            hlo[rw, :] = (n * vec[1:2, :] + vec[2:3, :]).astype(BF16)
        DG(1, 2); DG(0, 1); DG(1, 1); DG(2, 3); DG(0, 2); DG(1, 3); DG(2, 1)
        for h in range(4):
            zsend_wait(opiece(h, dp), z, h)
        for j in range(3):
            sm(j).wait_send()
            for p in range(4): sent(j, p)
            for p in (1, 2, 3): landed(j, p)
        l2.wait()

def run_kg(slen, llen, own, small, xl, xs, vec):
    V, S = pltpu.VMEM, pltpu.SemaphoreType.DMA
    o = lambda *s: const(s)
    rz = lambda: sds((4, R, E), BF16)
    return pl.pallas_call(
        kg,
        grid_spec=pltpu.PrefetchScalarGridSpec(num_scalar_prefetch=2, grid=(4,),
            in_specs=[ANY, o(8, 256), ANY, ANY, o(8, D)],
            out_specs=[ANY, o(4, 8, 256), o(4, R, E), o(4, R, E), o(4, R, E), o(4, R, E), o(4, 8, R), o(R, D), o(R, 128), o(R, D)],
            scratch_shapes=[V((4, D, D), BF16), V((4, 8, 256), F32), V((5, 128, D), BF16), V((5, 512, 128), F32), V((E, R), BF16), V((E, R), BF16), V((R, D), F32), V((D, D), BF16),
                            S((4, 4, 10)), S((4, 4, 11)), S((2,)), S((3,)), S((4,)), S((2,))]),
        out_shape=[sds((4, 4, D, D), BF16), sds((4, 8, 256), F32), rz(), rz(), rz(), rz(), sds((4, 8, R), F32), sds((R, D), F32), sds((R, 128), F32), sds((R, D), BF16)],
        compiler_params=pltpu.CompilerParams(dimension_semantics=("arbitrary",), collective_id=0, has_side_effects=True, vmem_limit_bytes=VM),
        name="gather_attention_forward")(slen, llen, own, small, xl, xs, vec)

ZO = (3, 0, 2, 1)

def far_order(z):
    e = 1 - ((z + 1) // 2) % 2
    return [z + 1 - 2 * (z % 2), e * ((z + 2) % 4) + (1 - e) * (3 - z), e * (3 - z) + (1 - e) * ((z + 2) % 4)]

H = PR // 2

def zo(g):
    h, e = g // 2, g * (3 - g) // 2
    return (1 - e) * (3 - 2 * h) + e * 2 * h

def add_into(n, dst, src):
    def body(i, u):
        d, r = dst(i), src(i)
        d[...] = (d[...].astype(F32) + r[...].astype(F32)).astype(BF16)
        return u
    lax.fori_loop(0, n, body, 0)

def kx(slen, llen, xl, xs, w, small, q8, k, v, ctx, lse, gs1, g3, yin, vin, gout, yout, dxout, vout,
       xb, dm, kt, gc, gqt, gk, gv, ga, gat, xt, acc, gob, dxs, gbs, stage, vr, vs, l0,
       r03, rx3, ry3, rxy3, ryx3, rl3, rr3, r01, rx1, ry1, rxy1, ryx1, rl1, rr1,
       sem, s0s, s0r, s0l, s1s, s1r, s2s, s2r, ys, yr, vsem_s, vsem_r, loc):
    g = pl.program_id(0)
    dp, y, x, c, z = place()
    xn, yn, cn = dpi(y, 1 - x, c), dpi(1 - y, x, c), dpi(y, x, 1 - c)
    z1, z2 = z + 1 - 2 * (z % 2), (z + 2) % 4
    parts = (1, 3)
    r0, rx, ry, rxy, ryx, rl, rr = (r01, r03), (rx1, rx3), (ry1, ry3), (rxy1, rxy3), (ryx1, ryx3), (rl1, rl3), (rr1, rr3)
    def rows(p): return pl.ds(pl.multiple_of(p * PR, 32), PR)
    def rc(src, dst, ss, rs, dev):
        return pltpu.make_async_remote_copy(src_ref=src, dst_ref=dst, send_sem=ss, recv_sem=rs, device_id=dev, device_id_type=MESH)
    def blk(kd, zz, q):
        return l0.at[zz, q] if kd else gob.at[zz, :, rows(2 * q + c), :]
    def half(kd, zz, q, h):
        return l0.at[zz, q, :, pl.ds(h * H, H), :] if kd else gob.at[zz, :, pl.ds(pl.multiple_of((2 * q + c) * PR + h * H, 16), H), :]
    def st0(kd, zz, q):
        src = (g3 if kd else gob).at[zz, :, rows(2 * q + 1 - c), :]
        return rc(src, r0[kd].at[zz, q], s0s.at[kd, zz, q], s0r.at[kd, zz, q], (cn, z))
    def ld0(zz, q):
        return pltpu.make_async_copy(g3.at[zz, :, rows(2 * q + c), :], l0.at[zz, q], s0l.at[zz, q])
    def stage_0(kd, zz):
        for q in range(4):
            st0(kd, zz, q).start()
            if kd: ld0(zz, q).start()
    def stage_a(kd, zz):
        for q in range(4):
            st0(kd, zz, q).wait_recv()
            if kd: ld0(zz, q).wait()
        n = parts[kd]
        add_into(4 * n, lambda i: blk(kd, zz, i // n).at[i % n], lambda i: r0[kd].at[zz, i // n, i % n])
        for j in range(2):
            s1x(kd, zz, j).start(); s1y(kd, zz, j).start()
    def s1x(kd, zz, j):
        return rc(half(kd, zz, 2 * j + 1 - x, 0), rx[kd].at[zz, j], s1s.at[kd, zz, j], s1r.at[kd, zz, j], (xn, z))
    def s1y(kd, zz, j):
        return rc(half(kd, zz, 2 * (1 - y) + j, 1), ry[kd].at[zz, j], s1s.at[kd, zz, 2 + j], s1r.at[kd, zz, 2 + j], (yn, z))
    def s1xy(kd, zz):
        return rc(half(kd, zz, 2 * (1 - y) + x, 0), rxy[kd].at[zz], s1s.at[kd, zz, 4], s1r.at[kd, zz, 4], (yn, z))
    def s1yx(kd, zz):
        return rc(half(kd, zz, 2 * y + 1 - x, 1), ryx[kd].at[zz], s1s.at[kd, zz, 5], s1r.at[kd, zz, 5], (xn, z))
    def stage_b(kd, zz):
        n = parts[kd]
        for j in range(2): s1x(kd, zz, j).wait_recv()
        add_into(2 * n, lambda i: half(kd, zz, 2 * (i // n) + x, 0).at[i % n], lambda i: rx[kd].at[zz, i // n, i % n])
        s1xy(kd, zz).start()
        for j in range(2): s1y(kd, zz, j).wait_recv()
        add_into(2 * n, lambda i: half(kd, zz, 2 * y + i // n, 1).at[i % n], lambda i: ry[kd].at[zz, i // n, i % n])
        s1yx(kd, zz).start()
    def stage_c(kd, zz):
        n = parts[kd]
        s1xy(kd, zz).wait_recv()
        add_into(n, lambda i: half(kd, zz, 2 * y + x, 0).at[i], lambda i: rxy[kd].at[zz, i])
        s1yx(kd, zz).wait_recv()
        add_into(n, lambda i: half(kd, zz, 2 * y + x, 1).at[i], lambda i: ryx[kd].at[zz, i])
    def mine(kd, zz): return blk(kd, zz, 2 * y + x)
    def zs(kd, zz, right):
        return rc(mine(kd, zz), (rl if right else rr)[kd].at[zz], s2s.at[kd, zz], s2r.at[kd, zz, 0 if right else 1], (dp, z + 1 if right else z - 1))
    def stage_d(kd, zz, hop):
        n = parts[kd]
        if hop < zz:
            @pl.when(z == hop)
            def _():
                if hop > 0:
                    zs(kd, zz, True).wait_recv()
                    add_into(n, lambda i: mine(kd, zz).at[i], lambda i: rl[kd].at[zz, i])
                zs(kd, zz, True).start()
        if 3 - hop > zz:
            @pl.when(z == 3 - hop)
            def _():
                if hop > 0:
                    zs(kd, zz, False).wait_recv()
                    add_into(n, lambda i: mine(kd, zz).at[i], lambda i: rr[kd].at[zz, i])
                zs(kd, zz, False).start()
        if hop == max(zz, 3 - zz):
            @pl.when(z == zz)
            def _():
                if zz > 0: zs(kd, zz, True).wait_recv()
                if zz < 3: zs(kd, zz, False).wait_recv()
                def body(i, u):
                    t = mine(kd, zz)[i].astype(F32)
                    if zz > 0: t += rl[kd][zz, i].astype(F32)
                    if zz < 3: t += rr[kd][zz, i].astype(F32)
                    gout[kd + i] = t
                    return u
                lax.fori_loop(0, n, body, 0)
    order = far_order(z)
    def yb(s): return 4 * s + s // 3
    def yc(t, src, s, hf, right):
        n, off = (4, 0) if hf == 0 else (1, 4)
        dst = (yout, dxout)[t].at[pl.ds(yb(s) + off, n)]
        src = dst if src is None else src.at[pl.ds(off, n)]
        return rc(src, dst, ys.at[t, s, hf, right], yr.at[t, s, hf], (dp, z + 1 if right else z - 1))
    def ysend(t, src, s, act):
        for right in (1, 0):
            @pl.when((s <= z) & (z < 3) if right else (s >= z) & (z > 0))
            def _():
                getattr(yc(t, src, s, 0, right), act)()
                @pl.when(s == 2)
                def _():
                    getattr(yc(t, src, s, 1, right), act)()
    def yarr(t, j):
        s = order[j]
        yc(t, None, s, 0, 1).wait_recv()
        @pl.when(s == 2)
        def _():
            yc(t, None, s, 1, 1).wait_recv()
        ysend(t, None, s, "start")
    def own(t, hf, way):
        n, off = (4, 0) if hf == 0 else (1, 4)
        if way == 0:
            return pltpu.make_async_copy(yin.at[pl.ds(off, n)], stage.at[pl.ds(off, n)], loc.at[t, hf, 0])
        return pltpu.make_async_copy((stage, dxs)[t].at[pl.ds(off, n)], (yout, dxout)[t].at[pl.ds(yb(z) + off, n)], loc.at[t, hf, 1])
    def ownall(fn):
        fn(0)
        @pl.when(z == 2)
        def _():
            fn(1)
    vpeer = [(cn, z), (xn, z), (yn, z), (dp, z1), (dp, z2)]
    def vcopy(i): return rc(vs.at[i], vr.at[i], vsem_s.at[i], vsem_r.at[i], vpeer[i])
    def vstep(i):
        vcopy(i).wait_recv()
        tot = vs[i] + vr[i]
        if i < 4:
            vs[i + 1] = tot
            vcopy(i + 1).start()
        else:
            vout[...] = tot
    F, T, o = 1, 0, ZO
    def S0(kd, u): stage_0(kd, o[u])
    def A(kd, u): stage_a(kd, o[u])
    def B(kd, u): stage_b(kd, o[u])
    def C(kd, u): stage_c(kd, o[u])
    def Z(kd, u, hop): stage_d(kd, o[u], hop)

    @pl.when(g == 0)
    def _():
        barrier_all([(xn, z), (yn, z), (cn, z)] + [(dp, (z + j) % 4) for j in (1, 2, 3)])
        S0(F, 0)
        ysend(0, yin, z, "start")
        ownall(lambda h: own(0, h, 0).start())
        for j in (1, 2, 3): S0(F, j)
        cg = pltpu.make_async_copy(gs1, acc, sem.at[1]); cg.start()
        load_rows(z, xl, xs, xb, sem.at[0])
        distances(z, slen, llen, dm)
        xt[...] = xb[...].reshape(R, D).T
        gbs[...] = jnp.zeros_like(gbs)
        cg.wait()
        ga[...] = acc[...].astype(BF16)
        gat[...] = ga[...].T
        ownall(lambda h: (own(0, h, 0).wait(), own(0, h, 1).start()))
    wz, sm = w.at[0, 0], small.at[0]
    gc[...] = nt(ga[...], wz[576:768, :]).astype(BF16)
    kt[...] = k[0].T
    attend_bwd(z, sm, q8.at[0], k.at[0], v.at[0], kt, gc, dm, lse.at[0], gqt, gk, gv)
    @pl.when(g == 0)
    def _(): A(F, 0)
    @pl.when(g == 1)
    def _(): A(T, 0); B(F, 0)
    @pl.when(g == 2)
    def _(): A(T, 1); B(F, 1); C(F, 0); Z(F, 0, 0)
    @pl.when(g == 3)
    def _(): A(T, 2); B(F, 2); C(F, 1); Z(F, 0, 1); Z(F, 1, 0)
    zg = zo(g)
    dq = gqt[...].astype(BF16).T
    dk = gk[...].astype(BF16)
    dv = gv[...].astype(BF16)
    gbs[zg, 0:1, 0:192] = jnp.sum(dq.astype(F32), axis=0, keepdims=True)
    gbs[zg, 1:2, 0:192] = jnp.sum(dv.astype(F32), axis=0, keepdims=True)
    acc[...] += nn(dq, wz[0:192, :]) + nn(dk, wz[192:384, :]) + nn(dv, wz[384:576, :])
    @pl.when(g == 3)
    def _():
        for i in range(5):
            dxs[i] = acc[128 * i:128 * i + 128, :].astype(BF16)
        ysend(1, dxs, z, "start")
        ownall(lambda h: own(1, h, 1).start())
        vs[0] = vin[...]
        for i in range(4):
            vs[0, 6 + 2 * i:8 + 2 * i, 0:192] = gbs[i, 0:2, 0:192]
        vcopy(0).start()
    for i in range(6):
        rw = slice(128 * i, 128 * i + 128)
        gob[zg, 0, rw, :] = jnp.concatenate([nn(xt[rw, :], dq), nn(xt[rw, :], dk), nn(xt[rw, :], dv), nn(gat[rw, :], ctx[0])], axis=1).astype(BF16)
    @pl.when(g == 0)
    def _(): S0(T, 0); A(F, 1)
    @pl.when(g == 1)
    def _(): S0(T, 1); A(F, 2); yarr(0, 0)
    @pl.when(g == 2)
    def _(): S0(T, 2); A(F, 3); B(T, 0); yarr(0, 1)
    @pl.when(g == 3)
    def _():
        S0(T, 3); C(T, 0); B(T, 1); Z(T, 0, 0); yarr(0, 2); vstep(0); A(T, 3); Z(F, 0, 2); Z(F, 1, 1); B(F, 3); C(F, 2); Z(F, 2, 0)
        B(T, 2); C(T, 1); Z(T, 1, 0); Z(T, 0, 1); vstep(1); B(T, 3); yarr(1, 0); Z(F, 0, 3); Z(F, 1, 2); Z(F, 2, 1); C(F, 3); Z(F, 3, 0); vstep(2)
        C(T, 2); Z(T, 2, 0); C(T, 3); Z(T, 3, 0); Z(T, 0, 2); Z(T, 1, 1); yarr(1, 1); vstep(3); Z(F, 1, 3); Z(F, 2, 2); Z(F, 3, 1)
        Z(T, 1, 2); Z(T, 2, 1); Z(T, 3, 1); Z(T, 0, 3); Z(T, 1, 3); Z(F, 3, 2); Z(T, 2, 2); Z(T, 3, 2); vstep(4); yarr(1, 2)
        for kd in (0, 1):
            for zz in ZO:
                for q in range(4): st0(kd, zz, q).wait_send()
                for j in range(2):
                    s1x(kd, zz, j).wait_send(); s1y(kd, zz, j).wait_send()
                s1xy(kd, zz).wait_send(); s1yx(kd, zz).wait_send()
                @pl.when(z < zz)
                def _(): zs(kd, zz, True).wait_send()
                @pl.when(z > zz)
                def _(): zs(kd, zz, False).wait_send()
        for t, src in enumerate((yin, dxs)):
            ysend(t, src, z, "wait_send")
            for j in range(3):
                ysend(t, None, order[j], "wait_send")
            ownall(lambda h: own(t, h, 1).wait())
        for i in range(5): vcopy(i).wait_send()

def run_kx(slen, llen, xl, xs, W, small, q8, k, v, ctx, lse, gs1, g3, yv, vec):
    pz = lambda *s: pl.BlockSpec((1,) + s, lambda g, *_: (zo(g),) + (0,) * len(s))
    rz = lambda: pz(R, E)
    V, S = pltpu.VMEM, pltpu.SemaphoreType.DMA
    b = lambda *s: V(s + (PR, D), BF16)
    h = lambda *s: V(s + (H, D), BF16)
    bufs = lambda n: [b(4, 4, n), h(4, 2, n), h(4, 2, n), h(4, n), h(4, n), b(4, n), b(4, n)]
    scratch = [V((5, 128, D), BF16), V((5, 512, 128), F32), V((E, R), BF16), V((R, E), BF16), V((E, R), F32), V((R, E), F32), V((R, E), F32),
               V((R, D), BF16), V((D, R), BF16), V((D, R), BF16), V((R, D), F32), V((4, 1, D, D), BF16), V((5, 128, D), BF16), V((4, 8, 256), F32),
               V((5, 128, D), BF16), V((5, 16, D), F32), V((5, 16, D), F32), b(4, 4, 3)] + bufs(3) + bufs(1) + [
               S((2,)), S((2, 4, 4)), S((2, 4, 4)), S((4, 4)), S((2, 4, 6)), S((2, 4, 6)), S((2, 4)), S((2, 4, 2)), S((2, 4, 2, 2)), S((2, 4, 2)), S((5,)), S((5,)), S((2, 2, 2))]
    return pl.pallas_call(
        kx,
        grid_spec=pltpu.PrefetchScalarGridSpec(num_scalar_prefetch=2, grid=(4,),
            in_specs=[ANY, ANY, pl.BlockSpec((1, 1, D, D), lambda g, *_: (zo(g), 0, 0, 0)), pz(8, 256), rz(), rz(), rz(), rz(), pz(8, R), ANY, ANY, ANY, const((16, D))],
            out_specs=[const((4, PR, D)), ANY, ANY, const((16, D))], scratch_shapes=scratch),
        out_shape=[sds((4, PR, D), F32), sds((17, 128, D), BF16), sds((17, 128, D), BF16), sds((16, D), F32)],
        compiler_params=pltpu.CompilerParams(dimension_semantics=("arbitrary",), collective_id=1, has_side_effects=True, vmem_limit_bytes=VM),
        name="attention_backward_send")(slen, llen, xl, xs, W, small, q8, k, v, ctx, lse, gs1, g3, yv, vec)

def alibi_slopes(slope_index, head_total):
    power = 1 << head_total.bit_length() - 1
    f = slope_index.astype(F32)
    return jnp.where(slope_index < power, jnp.exp2(-8.0 * (f + 1.0) / power), jnp.exp2(-4.0 * (2.0 * (f - power) + 1.0) / power))
def prep(slope_index, w_qkv, b_qv, w_out, w_up, w_down):
    a = jnp.concatenate([jnp.transpose(w_qkv, (1, 2, 0)).reshape(576, D), w_out.T], 0)
    own = jnp.stack([a, w_up[:, 0], w_up[:, 1], w_down], 0)
    bt = jnp.transpose(b_qv, (1, 2, 0)).reshape(2, 192)
    sl = jnp.zeros((1, 192), F32).at[0, 0:3].set(alibi_slopes(slope_index, 12))
    small = jnp.pad(jnp.concatenate([bt, sl], 0), ((0, 5), (0, 64)))
    return own, small
def per_device(x_short, x_long, short_lengths, long_lengths, slope_index, w_qkv, b_qv, w_out, b_out, gain1, bias1, w_up, w_down, b_down, gain2, bias2, cot_short, cot_long):
    own, small = prep(slope_index, w_qkv, b_qv, w_out, w_up, w_down)
    vec = jnp.stack([b_out, gain1, bias1, b_down, gain2, bias2, bias2, bias2], 0)
    xl, cl = x_long.reshape(8, 128, D), cot_long.reshape(8, 128, D)
    W, S, q8, k, v, ctx, lse, n1, r1, hl = run_kg(short_lengths, long_lengths, own, small, xl, x_short, vec)
    a, b, inner, y, gf, gs2, vg2 = run_kb(cl, cot_short, W, hl, n1, vec)
    go3, gs1, vg1 = run_kc(W, a, b, inner, gf, hl, gs2, n1, r1, vec)
    m, dpx = lax.axis_index("mp"), lax.axis_index("dp")
    vsum = jnp.concatenate([vg2[:3], vg1[:3], jnp.zeros((10, D), F32)], 0)
    G, Y, DX, vs = run_kx(short_lengths, long_lengths, xl, x_short, W, S, q8, k, v, ctx, lse, gs1, go3, y.reshape(5, 128, D), vsum)
    b = lax.dynamic_slice(vs[6:14, :192].reshape(4, 2, 3, 64), (m, 0, 0, 8 * dpx), (1, 2, 3, 8))[0]
    vs = lax.dynamic_slice(vs[:6], (0, 96 * dpx), (6, 96))
    gq = G[0][:, :576].reshape(-1, 3, 192)
    return (Y[8:], Y[:8].reshape(2, 512, D), DX[8:], DX[:8].reshape(2, 512, D), gq, jnp.transpose(b, (2, 0, 1)), G[0][:, 576:], vs[5], vs[3], vs[4], jnp.stack([G[1], G[2]], 1), G[3], vs[2], vs[0], vs[1])
def per_device_any(x_short, x_long, short_lengths, long_lengths, slope_index, w_qkv, b_qv, w_out, b_out, gain1, bias1, w_up, w_down, b_down, gain2, bias2, cot_short, cot_long):
    own, small = prep(slope_index, w_qkv, b_qv, w_out, w_up, w_down)
    W = lax.all_gather(own, "mp"); S = lax.all_gather(small, "mp")
    vec = jnp.stack([b_out, gain1, bias1, b_down, gain2, bias2, bias2, bias2], 0)
    xl, cl = x_long.reshape(8, 128, D), cot_long.reshape(8, 128, D)
    q8, k, v, ctx, lse, n1, r1, hl = run_ka(short_lengths, long_lengths, xl, x_short, W, S, vec)
    a, b, inner, y, gf, gs2, vg2 = run_kb(cl, cot_short, W, hl, n1, vec)
    go3, gs1, vg1 = run_kc(W, a, b, inner, gf, hl, gs2, n1, r1, vec)
    go1, dx, gb = run_kd(short_lengths, long_lengths, xl, x_short, W, S, q8, k, v, ctx, lse, gs1.astype(BF16), gs1)
    m = lax.axis_index("mp")
    def spread(r):
        g = lax.all_gather(r, "mp")
        return jnp.concatenate([g[2], g[3][:512]], 0).reshape(9, 128, D), jnp.stack([g[0][:512], g[1][:512]], 0)
    ys, yl = spread(y); ds, dl = spread(dx)
    G = jnp.concatenate([go1, go3], 1).astype(F32)
    G = lax.psum_scatter(G, "mp", scatter_dimension=0, tiled=True)[0]
    G = lax.psum_scatter(G, "dp", scatter_dimension=1, tiled=True)
    vs = lax.psum(jnp.concatenate([vg2[:3], vg1[:3]], 0), "mp")
    vs = lax.psum_scatter(vs, "dp", scatter_dimension=1, tiled=True)
    gb = lax.psum_scatter(gb[:, :2, :192], "mp", scatter_dimension=0, tiled=True)[0]
    gb = jnp.transpose(gb.reshape(2, 3, 64), (2, 0, 1))
    gb = lax.psum_scatter(gb, "dp", scatter_dimension=0, tiled=True)
    gq = jnp.transpose(G[0][:, :576].reshape(-1, 3, 192), (0, 1, 2))
    return (ys, yl, ds, dl, gq, gb, G[0][:, 576:], vs[5], vs[3], vs[4], jnp.stack([G[1], G[2]], 1), G[3], vs[2], vs[0], vs[1])
def solution(mesh):
    fn = per_device if mesh.shape["dp"] == 8 else per_device_any
    d3 = P("dp", None, None)
    return jax.shard_map(fn, mesh=mesh,
        in_specs=(d3, d3, P("dp"), P("dp"), P("mp"), P(None, None, "mp"), P(None, None, "mp"), P(None, "mp"), P(), P(), P(), P(None, None, "mp"), P(None, "mp"), P(), P(), P(), d3, d3),
        out_specs=(d3, d3, d3, d3, P("dp", None, "mp"), P("dp", None, "mp"), P("dp", "mp"), P("dp"), P("dp"), P("dp"), P("dp", None, "mp"), P("dp", "mp"), P("dp"), P("dp"), P("dp")),
        check_vma=False)
```

```python
import functools
import math

import jax
import jax.numpy as jnp
from jax import lax
from jax.experimental import pallas as pl
from jax.experimental.pallas import tpu as pltpu
from jax.sharding import PartitionSpec as P

F32, BF16 = jnp.float32, jnp.bfloat16
R, D, E = 640, 768, 192
FAR = 1e30
VM = 60 << 20

def nn(a, b): return lax.dot_general(a, b, (((1,), (0,)), ((), ())), preferred_element_type=F32)
def nt(a, b): return lax.dot_general(a, b, (((1,), (1,)), ((), ())), preferred_element_type=F32)

def load_rows(m, long_ref, short_ref, buf, sem):
    @pl.when(m < 2)
    def _():
        c = pltpu.make_async_copy(long_ref.at[pl.ds(4 * m, 4)], buf.at[pl.ds(0, 4)], sem); c.start(); c.wait()
        buf[4] = jnp.zeros((128, D), BF16)
    @pl.when(m == 2)
    def _():
        c = pltpu.make_async_copy(short_ref.at[pl.ds(0, 5)], buf, sem); c.start(); c.wait()
    @pl.when(m == 3)
    def _():
        c = pltpu.make_async_copy(short_ref.at[pl.ds(5, 4)], buf.at[pl.ds(0, 4)], sem); c.start(); c.wait()
        buf[4] = jnp.zeros((128, D), BF16)

def distances(m, slen, llen, dm):
    @pl.when(m < 2)
    def _():
        n = llen[jnp.minimum(m, 1)]
        key = lax.broadcasted_iota(jnp.int32, (512, 128), 0)
        qry = lax.broadcasted_iota(jnp.int32, (512, 128), 1)
        for i in range(4):
            dist = jnp.abs(key - (qry + 128 * i)).astype(F32)
            dm[i] = jnp.where(key < n, dist, FAR)
    @pl.when(m >= 2)
    def _():
        key = lax.broadcasted_iota(jnp.int32, (128, 128), 0)
        qry = lax.broadcasted_iota(jnp.int32, (128, 128), 1)
        dist = jnp.abs(key - qry).astype(F32)
        for i in range(5):
            n = slen[jnp.minimum(5 * (m - 2) + i, 8)] if i == 4 else slen[jnp.maximum(5 * (m - 2), 0) + i]
            dm[i, 0:128, :] = jnp.where(key < n, dist, FAR)

def head_lanes(j):
    return lax.broadcasted_iota(jnp.int32, (1, E), 1) // 64 == j
def head_rows(j):
    return lax.broadcasted_iota(jnp.int32, (E, 1), 0) // 64 == j

def attend_fwd(m, small, q8, k, vt, dm, ct, lse, hook=lambda i: None):
    def block(i, keys, koff):
        cols = pl.ds(pl.multiple_of(i * 128, 128), 128)
        qi = q8[cols, :]
        kk = k[pl.ds(koff, keys), :]
        vv = vt[:, pl.ds(koff, keys)]
        d = dm[i, 0:keys, :]
        out = jnp.zeros((E, 128), F32)
        for j in range(3):
            s = nt(kk, jnp.where(head_lanes(j), qi, jnp.zeros_like(qi))) - small[2:3, j:j + 1] * d
            mx = jnp.max(s, axis=0, keepdims=True)
            ex = jnp.exp(s - mx)
            tot = jnp.sum(ex, axis=0, keepdims=True)
            p = (ex * (1.0 / tot)).astype(BF16)
            out = jnp.where(head_rows(j), nn(vv, p), out)
            lse[j:j + 1, cols] = mx + jnp.log(tot)
        ct[:, cols] = out.astype(BF16)
    @pl.when(m < 2)
    def _():
        lax.fori_loop(0, 4, lambda i, u: (block(i, 512, 0), hook(i), u)[2], 0)
    @pl.when(m >= 2)
    def _():
        lax.fori_loop(0, 5, lambda i, u: (block(i, 128, pl.multiple_of(i * 128, 128)), hook(i), u)[2], 0)

def attend_bwd(m, small, q8, k, v, kt, gc, dm, lse, gqt, gk, gv, hook=lambda i: None):
    gk[...] = jnp.zeros_like(gk)
    gv[...] = jnp.zeros_like(gv)
    def block(i, keys, koff):
        cols = pl.ds(pl.multiple_of(i * 128, 128), 128)
        rows = pl.ds(koff, keys)
        qi, gi = q8[cols, :], gc[cols, :]
        kk, vv, ktt = k[rows, :], v[rows, :], kt[:, rows]
        d = dm[i, 0:keys, :]
        oq = jnp.zeros((E, 128), F32)
        ok = jnp.zeros((keys, E), F32)
        ov = jnp.zeros((keys, E), F32)
        for j in range(3):
            hl = head_lanes(j)
            qj = jnp.where(hl, qi, jnp.zeros_like(qi))
            gj = jnp.where(hl, gi, jnp.zeros_like(gi))
            s = nt(kk, qj) - small[2:3, j:j + 1] * d
            p = jnp.exp(s - lse[j:j + 1, cols])
            gp = nt(vv, gj)
            ov = ov + nn(p.astype(BF16), gj)
            row = jnp.sum(p * gp, axis=0, keepdims=True)
            ds = (p * (gp - row)).astype(BF16)
            oq = jnp.where(head_rows(j), nn(ktt, ds), oq)
            ok = ok + nn(ds, qj)
        gqt[:, cols] = oq * 0.125
        gk[rows, :] += ok
        gv[rows, :] += ov
    @pl.when(m < 2)
    def _():
        lax.fori_loop(0, 4, lambda i, u: (block(i, 512, 0), hook(i), u)[2], 0)
        gqt[:, 512:640] = jnp.zeros((E, 128), F32)
    @pl.when(m >= 2)
    def _():
        lax.fori_loop(0, 5, lambda i, u: (block(i, 128, pl.multiple_of(i * 128, 128)), hook(i), u)[2], 0)

def norm_fwd(s):
    mean = jnp.mean(s, axis=1, keepdims=True)
    c = s - mean
    r = lax.rsqrt(jnp.mean(c * c, axis=1, keepdims=True) + 1e-12)
    return c * r, r

def norm_bwd(gn, normed, r):
    return r * (gn - jnp.mean(gn, axis=1, keepdims=True) - normed * jnp.mean(gn * normed, axis=1, keepdims=True))

def row_tiles(fn, tile=640):
    def body(i, u):
        fn(pl.ds(pl.multiple_of(i * tile, tile), tile)); return u
    lax.fori_loop(0, R // tile, body, 0)

def ka(slen, llen, xl, xs, w, small, vec, q8o, ko, vo, co, lseo, n1o, r1o, hlo, xb, dm, vt, ct, acc, sem):
    z = pl.program_id(0)
    m = lax.axis_index("mp")
    @pl.when(z == 0)
    def _():
        load_rows(m, xl, xs, xb, sem)
        distances(m, slen, llen, dm)
        ct[...] = jnp.zeros_like(ct)
        lseo[...] = jnp.zeros_like(lseo)
        acc[...] = jnp.zeros_like(acc)
    x = xb[...].reshape(R, D)
    wz, sm = w.at[0, 0], small.at[0]
    q8o[0] = ((nt(x, wz[0:192, :]) + sm[0:1, 0:192]).astype(BF16).astype(F32) * 0.125).astype(BF16)
    ko[0] = nt(x, wz[192:384, :]).astype(BF16)
    v = (nt(x, wz[384:576, :]) + sm[1:2, 0:192]).astype(BF16)
    vo[0] = v
    vt[...] = v.T
    attend_fwd(m, sm, q8o.at[0], ko.at[0], vt, dm, ct, lseo.at[0])
    co[0] = ct[...].T
    acc[...] += nn(co[0], wz[576:768, :]).astype(BF16).astype(F32)
    @pl.when(z == 3)
    def _():
        for i in range(5):
            rows = slice(128 * i, 128 * i + 128)
            s = xb[i].astype(F32) + acc[rows, :] + vec[0:1, :]
            n, r = norm_fwd(s)
            n1o[rows, :] = n
            r1o[rows, :] = jnp.broadcast_to(r, (128, 128))
            hlo[rows, :] = (n * vec[1:2, :] + vec[2:3, :]).astype(BF16)

def const(shape): return pl.BlockSpec(shape, lambda z, *_: (0,) * len(shape))
def perz(shape): return pl.BlockSpec((1,) + shape, lambda z, *_: (z,) + (0,) * len(shape))
ANY = pl.BlockSpec(memory_space=pl.ANY)
def sds(shape, dt): return jax.ShapeDtypeStruct(shape, dt)
def part(p): return pl.BlockSpec((1, 1, D, D), lambda z, *_: (z, p, 0, 0))

def call(kernel, in_specs, outs, scratch, name, args, grid=(4,), prefetch=2):
    return pl.pallas_call(
        kernel,
        grid_spec=pltpu.PrefetchScalarGridSpec(num_scalar_prefetch=prefetch, grid=grid, in_specs=in_specs,
            out_specs=[o[0] for o in outs], scratch_shapes=scratch),
        out_shape=[o[1] for o in outs],
        compiler_params=pltpu.CompilerParams(dimension_semantics=("arbitrary",), vmem_limit_bytes=VM),
        name=name)(*args)

def run_ka(slen, llen, xl, xs, W, small, vec):
    rz = lambda: (perz((R, E)), sds((4, R, E), BF16))
    return call(ka, [ANY, ANY, part(0), perz((8, 256)), const((8, D))],
        [rz(), rz(), rz(), rz(), (perz((8, R)), sds((4, 8, R), F32)), (const((R, D)), sds((R, D), F32)), (const((R, 128)), sds((R, 128), F32)), (const((R, D)), sds((R, D), BF16))],
        [pltpu.VMEM((5, 128, D), BF16), pltpu.VMEM((5, 512, 128), F32), pltpu.VMEM((E, R), BF16), pltpu.VMEM((E, R), BF16), pltpu.VMEM((R, D), F32), pltpu.SemaphoreType.DMA],
        "attention_forward", (slen, llen, xl, xs, W, small, vec))

def gelu_parts(g):
    cdf = 0.5 * (1.0 + lax.erf(g * (2.0 ** -0.5)))
    pdf = jnp.exp(-0.5 * g * g) * (1.0 / math.sqrt(2 * math.pi))
    return g * cdf, cdf + g * pdf

def kb(cl, cs, wg, wu, wd, hl, n1, vec, ao, bo, io, yo, gfo, gs2o, vgo, acc, cb, sem):
    z = pl.program_id(0)
    m = lax.axis_index("mp")
    @pl.when(z == 0)
    def _():
        load_rows(m, cl, cs, cb, sem)
        acc[...] = jnp.zeros_like(acc)
    def tile(rows):
        h = hl[rows, :]
        gate = nn(h, wg[0, 0])
        up = nn(h, wu[0, 0])
        a, slope = gelu_parts(gate)
        ao[0, rows, :] = a
        bo[0, rows, :] = up * slope
        inner = (a * up).astype(BF16)
        io[0, rows, :] = inner
        acc[rows, :] += nt(inner, wd[0, 0]).astype(BF16).astype(F32)
    row_tiles(tile)
    @pl.when(z == 3)
    def _():
        tot = [jnp.zeros((1, D), F32)] * 3
        for i in range(5):
            rows = slice(128 * i, 128 * i + 128)
            h1 = n1[rows, :] * vec[1:2, :] + vec[2:3, :]
            n, r = norm_fwd(h1 + acc[rows, :] + vec[3:4, :])
            yo[rows, :] = (n * vec[4:5, :] + vec[5:6, :]).astype(BF16)
            gy = cb[i].astype(F32)
            gs = norm_bwd(gy * vec[4:5, :], n, r)
            gs2o[rows, :] = gs
            gfo[rows, :] = gs.astype(BF16)
            tot = [tot[0] + jnp.sum(gy * n, axis=0, keepdims=True), tot[1] + jnp.sum(gy, axis=0, keepdims=True), tot[2] + jnp.sum(gs, axis=0, keepdims=True)]
        vgo[...] = jnp.concatenate(tot + [jnp.zeros((5, D), F32)], axis=0)

def run_kb(cl, cs, W, hl, n1, vec):
    z32 = lambda: (perz((R, D)), sds((4, R, D), F32))
    return call(kb, [ANY, ANY, part(1), part(2), part(3), const((R, D)), const((R, D)), const((8, D))],
        [z32(), z32(), (perz((R, D)), sds((4, R, D), BF16)), (const((R, D)), sds((R, D), BF16)), (const((R, D)), sds((R, D), BF16)), (const((R, D)), sds((R, D), F32)), (const((8, D)), sds((8, D), F32))],
        [pltpu.VMEM((R, D), F32), pltpu.VMEM((5, 128, D), BF16), pltpu.SemaphoreType.DMA],
        "feed_forward", (cl, cs, W, W, W, hl, n1, vec), prefetch=0)

def kc(wg, wu, wd, a, b, inner, gf, hl, gs2, n1, r1, vec, go, gs1o, vgo, acc, gft, hlt, gg):
    z = pl.program_id(0)
    @pl.when(z == 0)
    def _():
        acc[...] = gs2[...]
        gft[...] = gf[...].T
        hlt[...] = hl[...].T
    def tile(rows):
        gi = nn(gf[rows, :], wd[0, 0])
        g1 = (gi * b[0, rows, :]).astype(BF16)
        g2 = (gi * a[0, rows, :]).astype(BF16)
        gg[0, rows, :] = g1
        gg[1, rows, :] = g2
        acc[rows, :] += nt(g1, wg[0, 0]) + nt(g2, wu[0, 0])
    row_tiles(tile)
    def wtile(rows):
        go[0, 2, rows, :] = nn(gft[rows, :], inner[0]).astype(BF16)
        go[0, 0, rows, :] = nn(hlt[rows, :], gg[0]).astype(BF16)
        go[0, 1, rows, :] = nn(hlt[rows, :], gg[1]).astype(BF16)
    wtile(slice(0, D))
    @pl.when(z == 3)
    def _():
        tot = [jnp.zeros((1, D), F32)] * 3
        for i in range(5):
            rows = slice(128 * i, 128 * i + 128)
            gh, n = acc[rows, :], n1[rows, :]
            gs = norm_bwd(gh * vec[1:2, :], n, r1[rows, 0:1])
            gs1o[rows, :] = gs
            tot = [tot[0] + jnp.sum(gh * n, axis=0, keepdims=True), tot[1] + jnp.sum(gh, axis=0, keepdims=True), tot[2] + jnp.sum(gs, axis=0, keepdims=True)]
        vgo[...] = jnp.concatenate(tot + [jnp.zeros((5, D), F32)], axis=0)

def run_kc(W, a, b, inner, gf, hl, gs2, n1, r1, vec):
    c = lambda dt: const((R, D))
    return call(kc, [part(1), part(2), part(3), perz((R, D)), perz((R, D)), perz((R, D)), c(0), c(0), c(0), c(0), const((R, 128)), const((8, D))],
        [(pl.BlockSpec((1, 3, D, D), lambda z: (z, 0, 0, 0)), sds((4, 3, D, D), BF16)), (const((R, D)), sds((R, D), F32)), (const((8, D)), sds((8, D), F32))],
        [pltpu.VMEM((R, D), F32), pltpu.VMEM((D, R), BF16), pltpu.VMEM((D, R), BF16), pltpu.VMEM((2, R, D), BF16)],
        "feed_backward", (W, W, W, a, b, inner, gf, hl, gs2, n1, r1, vec), prefetch=0)

def kd(slen, llen, xl, xs, w, small, q8, k, v, ctx, lse, ga, gs1, go, dxo, gbo, xb, dm, kt, gc, gqt, gk, gv, gat, xt, acc, sem):
    z = pl.program_id(0)
    m = lax.axis_index("mp")
    @pl.when(z == 0)
    def _():
        load_rows(m, xl, xs, xb, sem)
        distances(m, slen, llen, dm)
        acc[...] = gs1[...]
        gat[...] = ga[...].T
        xt[...] = xb[...].reshape(R, D).T
        gbo[...] = jnp.zeros_like(gbo)
    wz, sm = w.at[0, 0], small.at[0]
    gc[...] = nt(ga[...], wz[576:768, :]).astype(BF16)
    kt[...] = k[0].T
    attend_bwd(m, sm, q8.at[0], k.at[0], v.at[0], kt, gc, dm, lse.at[0], gqt, gk, gv)
    dq = gqt[...].astype(BF16).T
    dk = gk[...].astype(BF16)
    dv = gv[...].astype(BF16)
    gbo[z, 0:1, 0:192] = jnp.sum(dq.astype(F32), axis=0, keepdims=True)
    gbo[z, 1:2, 0:192] = jnp.sum(dv.astype(F32), axis=0, keepdims=True)
    acc[...] += nn(dq, wz[0:192, :]) + nn(dk, wz[192:384, :]) + nn(dv, wz[384:576, :])
    def wtile(rows):
        xr = xt[rows, :]
        go[0, 0, rows, :] = jnp.concatenate([nn(xr, dq), nn(xr, dk), nn(xr, dv), nn(gat[rows, :], ctx[0])], axis=1).astype(BF16)
    for i in range(6):
        wtile(slice(128 * i, 128 * i + 128))
    @pl.when(z == 3)
    def _():
        dxo[...] = acc[...].astype(BF16)

def run_kd(slen, llen, xl, xs, W, small, q8, k, v, ctx, lse, ga, gs1):
    rz = lambda: perz((R, E))
    rd = const((R, D))
    return call(kd, [ANY, ANY, part(0), perz((8, 256)), rz(), rz(), rz(), rz(), perz((8, R)), rd, rd],
        [(pl.BlockSpec((1, 1, D, D), lambda z, *_: (z, 0, 0, 0)), sds((4, 1, D, D), BF16)), (rd, sds((R, D), BF16)), (const((4, 8, 256)), sds((4, 8, 256), F32))],
        [pltpu.VMEM((5, 128, D), BF16), pltpu.VMEM((5, 512, 128), F32), pltpu.VMEM((E, R), BF16), pltpu.VMEM((R, E), BF16), pltpu.VMEM((E, R), F32), pltpu.VMEM((R, E), F32), pltpu.VMEM((R, E), F32),
         pltpu.VMEM((D, R), BF16), pltpu.VMEM((D, R), BF16), pltpu.VMEM((R, D), F32), pltpu.SemaphoreType.DMA],
        "attention_backward", (slen, llen, xl, xs, W, small, q8, k, v, ctx, lse, ga, gs1))

MESH = pl.DeviceIdType.MESH
PR = 96

def place():
    dp = lax.axis_index("dp"); z = lax.axis_index("mp")
    return dp, dp // 4, (dp // 2) % 2, dp % 2, z

def dpi(y, x, c):
    return (y * 2 + x) * 2 + c

def barrier_all(peers):
    b = pltpu.get_barrier_semaphore()
    for d in peers:
        pl.semaphore_signal(b, inc=1, device_id=d, device_id_type=MESH)
    pl.semaphore_wait(b, len(peers))

def kg(slen, llen, own, small, xl, xs, vec, out, sout, q8o, ko, vo, co, lseo, n1o, r1o, hlo,
       stage, ssm, xb, dm, vt, ct, acc, wz, recv, send, loc, ss, sr, sem):
    g = pl.program_id(0)
    dp, y, x, c, z = place()
    xn, yn, cn = dpi(y, 1 - x, c), dpi(1 - y, x, c), dpi(y, x, 1 - c)
    dn = dpi(1 - y, 1 - x, c)
    def sm(j): return pltpu.make_async_remote_copy(src_ref=small, dst_ref=ssm.at[z], send_sem=ss.at[j], recv_sem=sr.at[z], device_id=(dp, (z + 1 + j) % 4), device_id_type=MESH)
    e = 1 - ((z + 1) // 2) % 2
    srcs = [z + 1 - 2 * (z % 2), e * ((z + 2) % 4) + (1 - e) * (3 - z), e * (3 - z) + (1 - e) * ((z + 2) % 4)]

    def rows(p, h):
        if h is None:
            return pl.ds(pl.multiple_of(p * PR, 32), PR)
        return pl.ds(pl.multiple_of(p * PR + h * (PR // 2), 16), PR // 2)
    def piece(s, g, p, h=None):
        return out.at[s, g, rows(p, h), :]
    def opiece(g, p):
        return own.at[g, rows(p, None), :]
    def cp(src, dst, s, g, k, r, dev):
        return pltpu.make_async_remote_copy(src_ref=src, dst_ref=dst, send_sem=send.at[s, g, k], recv_sem=recv.at[s, g, r], device_id=dev, device_id_type=MESH)
    def zsend(src, s, g):
        @pl.when((s <= z) & (z < 3))
        def _():
            cp(src, piece(s, g, dp), s, g, 0, 0, (dp, z + 1)).start()
        @pl.when((s >= z) & (z > 0))
        def _():
            cp(src, piece(s, g, dp), s, g, 1, 0, (dp, z - 1)).start()
    def zsend_wait(src, s, g):
        @pl.when((s <= z) & (z < 3))
        def _():
            cp(src, piece(s, g, dp), s, g, 0, 0, (dp, z + 1)).wait_send()
        @pl.when((s >= z) & (z > 0))
        def _():
            cp(src, piece(s, g, dp), s, g, 1, 0, (dp, z - 1)).wait_send()
    def simple(s, g):
        me, xp, yp, dg = dp, xn, yn, dn
        return dict(
            x=lambda: cp(piece(s, g, me), piece(s, g, me), s, g, 2, 1, (xn, z)),
            y=lambda: cp(piece(s, g, me), piece(s, g, me), s, g, 3, 2, (yn, z)),
            c=lambda: cp(piece(s, g, me), piece(s, g, me), s, g, 4, 3, (cn, z)),
            cx=lambda: cp(piece(s, g, xp), piece(s, g, xp), s, g, 5, 4, (cn, z)),
            cy=lambda: cp(piece(s, g, yp), piece(s, g, yp), s, g, 6, 5, (cn, z)),
            yf=lambda: cp(piece(s, g, xp, 0), piece(s, g, xp, 0), s, g, 7, 6, (yn, z)),
            xf=lambda: cp(piece(s, g, yp, 1), piece(s, g, yp, 1), s, g, 8, 7, (xn, z)),
            cd0=lambda: cp(piece(s, g, dg, 0), piece(s, g, dg, 0), s, g, 9, 8, (cn, z)),
            cd1=lambda: cp(piece(s, g, dg, 1), piece(s, g, dg, 1), s, g, 10, 9, (cn, z)),
        )
    def wrecv(ref, s, g, r):
        pltpu.make_async_remote_copy(src_ref=ref, dst_ref=ref, send_sem=send.at[s, g, 0], recv_sem=recv.at[s, g, r], device_id=(cn, z), device_id_type=MESH).wait_recv()
    def zarr(j, g):
        s = srcs[j]
        wrecv(piece(s, g, dp), s, g, 0)
        zsend(piece(s, g, dp), s, g)
        m = simple(s, g)
        m["x"]().start(); m["y"]().start(); m["c"]().start()
    def xyarr(j, g):
        s = srcs[j]; m = simple(s, g)
        wrecv(piece(s, g, xn), s, g, 1)
        m["yf"]().start(); m["cx"]().start()
        wrecv(piece(s, g, yn), s, g, 2)
        m["xf"]().start(); m["cy"]().start()
    def diag(j, g):
        s = srcs[j]; m = simple(s, g)
        wrecv(piece(s, g, dn, 0), s, g, 6)
        m["cd0"]().start()
        wrecv(piece(s, g, dn, 1), s, g, 7)
        m["cd1"]().start()
    def landed(j, g):
        s = srcs[j]
        cdx, cdy, cdd = dpi(y, 1 - x, 1 - c), dpi(1 - y, x, 1 - c), dpi(1 - y, 1 - x, 1 - c)
        wrecv(piece(s, g, cn), s, g, 3)
        wrecv(piece(s, g, cdx), s, g, 4)
        wrecv(piece(s, g, cdy), s, g, 5)
        wrecv(piece(s, g, cdd, 0), s, g, 8)
        wrecv(piece(s, g, cdd, 1), s, g, 9)
    def sent(j, g):
        s = srcs[j]; m = simple(s, g)
        zsend_wait(piece(s, g, dp), s, g)
        for k in ("x", "y", "c", "cx", "cy", "yf", "xf", "cd0", "cd1"):
            m[k]().wait_send()
    l1 = pltpu.make_async_copy(own, stage, loc.at[0])
    l2 = pltpu.make_async_copy(stage, out.at[z], loc.at[1])
    def fetch(j):
        landed(j, 0)
        cw = pltpu.make_async_copy(out.at[srcs[j], 0], wz, sem.at[1]); cw.start()
        pltpu.make_async_remote_copy(src_ref=small, dst_ref=ssm.at[srcs[j]], send_sem=ss.at[j], recv_sem=sr.at[srcs[j]], device_id=(cn, z), device_id_type=MESH).wait_recv()
        cw.wait()
    Z, XY, DG = zarr, xyarr, diag
    def mine(p): zsend(opiece(p, dp), z, p)
    def at(n, fn):
        @pl.when(g == n)
        def _(): fn()

    @pl.when(g == 0)
    def _():
        barrier_all([(xn, z), (yn, z), (cn, z)] + [(dp, (z + j) % 4) for j in (1, 2, 3)])
        mine(0); mine(2); mine(3)
        for j in range(3): sm(j).start()
        cw = pltpu.make_async_copy(own.at[0], wz, sem.at[1]); cw.start()
        l1.start()
        ssm[z] = small[...]
        load_rows(z, xl, xs, xb, sem.at[0])
        distances(z, slen, llen, dm)
        ct[...] = jnp.zeros_like(ct)
        lseo[...] = jnp.zeros_like(lseo)
        acc[...] = jnp.zeros_like(acc)
        cw.wait()
        Z(0, 0); mine(1)
    zz = jnp.where(g == 0, z, jnp.where(g == 1, srcs[0], jnp.where(g == 2, srcs[1], srcs[2])))
    xv = xb[...].reshape(R, D)
    bs = ssm.at[zz]
    q8o[zz] = ((nt(xv, wz[0:192, :]) + bs[0:1, 0:192]).astype(BF16).astype(F32) * 0.125).astype(BF16)
    ko[zz] = nt(xv, wz[192:384, :]).astype(BF16)
    v = (nt(xv, wz[384:576, :]) + bs[1:2, 0:192]).astype(BF16)
    vo[zz] = v
    vt[...] = v.T
    at(0, lambda: Z(0, 2))
    at(1, lambda: XY(0, 3))
    at(3, lambda: DG(0, 3))
    def hook(i):
        def on(n, j, fn):
            @pl.when((g == n) & (i == j))
            def _(): fn()
        on(0, 0, lambda: (Z(0, 3), XY(0, 0), Z(1, 0), Z(2, 0)))
        on(0, 1, lambda: Z(0, 1))
        on(0, 2, lambda: (DG(0, 0), XY(1, 0)))
        on(0, 3, lambda: (XY(0, 2), Z(1, 3)))
        on(1, 0, lambda: Z(2, 2))
        on(1, 2, lambda: (DG(1, 0), Z(1, 2)))
        on(2, 0, lambda: Z(2, 1))
        on(2, 1, lambda: XY(1, 3))
        on(2, 3, lambda: (Z(2, 3), XY(1, 2)))
        on(3, 1, lambda: (XY(1, 1), XY(2, 3)))
    attend_fwd(z, bs, q8o.at[zz], ko.at[zz], vt, dm, ct, lseo.at[zz], hook)
    cv = ct[...].T
    co[zz] = cv
    acc[...] += nn(cv, wz[576:768, :]).astype(BF16).astype(F32)
    at(0, lambda: (l1.wait(), l2.start(), XY(2, 0), fetch(0), Z(1, 1),))
    at(1, lambda: (fetch(1), DG(2, 0),))
    at(2, lambda: (fetch(2), XY(2, 2), XY(0, 1),))
    @pl.when(g == 3)
    def _():
        XY(2, 1); DG(2, 2)
        sout[...] = ssm[...]
        for i in range(5):
            rw = slice(128 * i, 128 * i + 128)
            s = xb[i].astype(F32) + acc[rw, :] + vec[0:1, :]
            n, r = norm_fwd(s)
            n1o[rw, :] = n
            r1o[rw, :] = jnp.broadcast_to(r, (128, 128))
            hlo[rw, :] = (n * vec[1:2, :] + vec[2:3, :]).astype(BF16)
        DG(1, 2); DG(0, 1); DG(1, 1); DG(2, 3); DG(0, 2); DG(1, 3); DG(2, 1)
        for h in range(4):
            zsend_wait(opiece(h, dp), z, h)
        for j in range(3):
            sm(j).wait_send()
            for p in range(4): sent(j, p)
            for p in (1, 2, 3): landed(j, p)
        l2.wait()

def run_kg(slen, llen, own, small, xl, xs, vec):
    V, S = pltpu.VMEM, pltpu.SemaphoreType.DMA
    o = lambda *s: const(s)
    rz = lambda: sds((4, R, E), BF16)
    return pl.pallas_call(
        kg,
        grid_spec=pltpu.PrefetchScalarGridSpec(num_scalar_prefetch=2, grid=(4,),
            in_specs=[ANY, o(8, 256), ANY, ANY, o(8, D)],
            out_specs=[ANY, o(4, 8, 256), o(4, R, E), o(4, R, E), o(4, R, E), o(4, R, E), o(4, 8, R), o(R, D), o(R, 128), o(R, D)],
            scratch_shapes=[V((4, D, D), BF16), V((4, 8, 256), F32), V((5, 128, D), BF16), V((5, 512, 128), F32), V((E, R), BF16), V((E, R), BF16), V((R, D), F32), V((D, D), BF16),
                            S((4, 4, 10)), S((4, 4, 11)), S((2,)), S((3,)), S((4,)), S((2,))]),
        out_shape=[sds((4, 4, D, D), BF16), sds((4, 8, 256), F32), rz(), rz(), rz(), rz(), sds((4, 8, R), F32), sds((R, D), F32), sds((R, 128), F32), sds((R, D), BF16)],
        compiler_params=pltpu.CompilerParams(dimension_semantics=("arbitrary",), collective_id=0, has_side_effects=True, vmem_limit_bytes=VM),
        name="gather_attention_forward")(slen, llen, own, small, xl, xs, vec)

ZO = (3, 0, 2, 1)

def far_order(z):
    e = 1 - ((z + 1) // 2) % 2
    return [z + 1 - 2 * (z % 2), e * ((z + 2) % 4) + (1 - e) * (3 - z), e * (3 - z) + (1 - e) * ((z + 2) % 4)]

H = PR // 2

def zo(g):
    h, e = g // 2, g * (3 - g) // 2
    return (1 - e) * (3 - 2 * h) + e * 2 * h

def add_into(n, dst, src):
    def body(i, u):
        d, r = dst(i), src(i)
        d[...] = (d[...].astype(F32) + r[...].astype(F32)).astype(BF16)
        return u
    lax.fori_loop(0, n, body, 0)

def kx(slen, llen, xl, xs, w, small, q8, k, v, ctx, lse, gs1, g3, yin, vin, gout, yout, dxout, vout,
       xb, dm, kt, gc, gqt, gk, gv, ga, gat, xt, acc, gob, dxs, gbs, stage, vr, vs, l0,
       r03, rx3, ry3, rxy3, ryx3, rl3, rr3, r01, rx1, ry1, rxy1, ryx1, rl1, rr1,
       sem, s0s, s0r, s0l, s1s, s1r, s2s, s2r, ys, yr, vsem_s, vsem_r, loc):
    g = pl.program_id(0)
    dp, y, x, c, z = place()
    xn, yn, cn = dpi(y, 1 - x, c), dpi(1 - y, x, c), dpi(y, x, 1 - c)
    z1, z2 = z + 1 - 2 * (z % 2), (z + 2) % 4
    parts = (1, 3)
    r0, rx, ry, rxy, ryx, rl, rr = (r01, r03), (rx1, rx3), (ry1, ry3), (rxy1, rxy3), (ryx1, ryx3), (rl1, rl3), (rr1, rr3)
    def rows(p): return pl.ds(pl.multiple_of(p * PR, 32), PR)
    def rc(src, dst, ss, rs, dev):
        return pltpu.make_async_remote_copy(src_ref=src, dst_ref=dst, send_sem=ss, recv_sem=rs, device_id=dev, device_id_type=MESH)
    def blk(kd, zz, q):
        return l0.at[zz, q] if kd else gob.at[zz, :, rows(2 * q + c), :]
    def half(kd, zz, q, h):
        return l0.at[zz, q, :, pl.ds(h * H, H), :] if kd else gob.at[zz, :, pl.ds(pl.multiple_of((2 * q + c) * PR + h * H, 16), H), :]
    def st0(kd, zz, q):
        src = (g3 if kd else gob).at[zz, :, rows(2 * q + 1 - c), :]
        return rc(src, r0[kd].at[zz, q], s0s.at[kd, zz, q], s0r.at[kd, zz, q], (cn, z))
    def ld0(zz, q):
        return pltpu.make_async_copy(g3.at[zz, :, rows(2 * q + c), :], l0.at[zz, q], s0l.at[zz, q])
    def stage_0(kd, zz):
        for q in range(4):
            st0(kd, zz, q).start()
            if kd: ld0(zz, q).start()
    def stage_a(kd, zz):
        for q in range(4):
            st0(kd, zz, q).wait_recv()
            if kd: ld0(zz, q).wait()
        n = parts[kd]
        add_into(4 * n, lambda i: blk(kd, zz, i // n).at[i % n], lambda i: r0[kd].at[zz, i // n, i % n])
        for j in range(2):
            s1x(kd, zz, j).start(); s1y(kd, zz, j).start()
    def s1x(kd, zz, j):
        return rc(half(kd, zz, 2 * j + 1 - x, 0), rx[kd].at[zz, j], s1s.at[kd, zz, j], s1r.at[kd, zz, j], (xn, z))
    def s1y(kd, zz, j):
        return rc(half(kd, zz, 2 * (1 - y) + j, 1), ry[kd].at[zz, j], s1s.at[kd, zz, 2 + j], s1r.at[kd, zz, 2 + j], (yn, z))
    def s1xy(kd, zz):
        return rc(half(kd, zz, 2 * (1 - y) + x, 0), rxy[kd].at[zz], s1s.at[kd, zz, 4], s1r.at[kd, zz, 4], (yn, z))
    def s1yx(kd, zz):
        return rc(half(kd, zz, 2 * y + 1 - x, 1), ryx[kd].at[zz], s1s.at[kd, zz, 5], s1r.at[kd, zz, 5], (xn, z))
    def stage_b(kd, zz):
        n = parts[kd]
        for j in range(2): s1x(kd, zz, j).wait_recv()
        add_into(2 * n, lambda i: half(kd, zz, 2 * (i // n) + x, 0).at[i % n], lambda i: rx[kd].at[zz, i // n, i % n])
        s1xy(kd, zz).start()
        for j in range(2): s1y(kd, zz, j).wait_recv()
        add_into(2 * n, lambda i: half(kd, zz, 2 * y + i // n, 1).at[i % n], lambda i: ry[kd].at[zz, i // n, i % n])
        s1yx(kd, zz).start()
    def stage_c(kd, zz):
        n = parts[kd]
        s1xy(kd, zz).wait_recv()
        add_into(n, lambda i: half(kd, zz, 2 * y + x, 0).at[i], lambda i: rxy[kd].at[zz, i])
        s1yx(kd, zz).wait_recv()
        add_into(n, lambda i: half(kd, zz, 2 * y + x, 1).at[i], lambda i: ryx[kd].at[zz, i])
    def mine(kd, zz): return blk(kd, zz, 2 * y + x)
    def zs(kd, zz, right):
        return rc(mine(kd, zz), (rl if right else rr)[kd].at[zz], s2s.at[kd, zz], s2r.at[kd, zz, 0 if right else 1], (dp, z + 1 if right else z - 1))
    def stage_d(kd, zz, hop):
        n = parts[kd]
        if hop < zz:
            @pl.when(z == hop)
            def _():
                if hop > 0:
                    zs(kd, zz, True).wait_recv()
                    add_into(n, lambda i: mine(kd, zz).at[i], lambda i: rl[kd].at[zz, i])
                zs(kd, zz, True).start()
        if 3 - hop > zz:
            @pl.when(z == 3 - hop)
            def _():
                if hop > 0:
                    zs(kd, zz, False).wait_recv()
                    add_into(n, lambda i: mine(kd, zz).at[i], lambda i: rr[kd].at[zz, i])
                zs(kd, zz, False).start()
        if hop == max(zz, 3 - zz):
            @pl.when(z == zz)
            def _():
                if zz > 0: zs(kd, zz, True).wait_recv()
                if zz < 3: zs(kd, zz, False).wait_recv()
                def body(i, u):
                    t = mine(kd, zz)[i].astype(F32)
                    if zz > 0: t += rl[kd][zz, i].astype(F32)
                    if zz < 3: t += rr[kd][zz, i].astype(F32)
                    gout[kd + i] = t
                    return u
                lax.fori_loop(0, n, body, 0)
    order = far_order(z)
    def yb(s): return 4 * s + s // 3
    CHUNKS = ((2, 0), (2, 2), (1, 4))
    def yc(t, src, s, h, right):
        n, off = CHUNKS[h]
        dst = (yout, dxout)[t].at[pl.ds(yb(s) + off, n)]
        src = dst if src is None else src.at[pl.ds(off, n)]
        return rc(src, dst, ys.at[t, s, h, right], yr.at[t, s, h], (dp, z + 1 if right else z - 1))
    def ysend(t, src, s, act, hs=(0, 1, 2)):
        for h in hs:
            for right in (1, 0):
                go = (s <= z) & (z < 3) if right else (s >= z) & (z > 0)
                @pl.when(go & (s == 2) if h == 2 else go)
                def _():
                    getattr(yc(t, src, s, h, right), act)()
    def yarr(t, j, h):
        s = order[j]
        if h == 2:
            @pl.when(s == 2)
            def _():
                yc(t, None, s, h, 1).wait_recv()
        else:
            yc(t, None, s, h, 1).wait_recv()
        ysend(t, None, s, "start", (h,))
    def own(t, hf, way):
        n, off = (4, 0) if hf == 0 else (1, 4)
        if way == 0:
            return pltpu.make_async_copy(yin.at[pl.ds(off, n)], stage.at[pl.ds(off, n)], loc.at[t, hf, 0])
        return pltpu.make_async_copy((stage, dxs)[t].at[pl.ds(off, n)], (yout, dxout)[t].at[pl.ds(yb(z) + off, n)], loc.at[t, hf, 1])
    def ownall(fn):
        fn(0)
        @pl.when(z == 2)
        def _():
            fn(1)
    vpeer = [(dp, z1), (dp, z2), (cn, z), (xn, z), (yn, z)]
    def vcopy(i): return rc(vs.at[i], vr.at[i], vsem_s.at[i], vsem_r.at[i], vpeer[i])
    def vstep(i):
        vcopy(i).wait_recv()
        tot = vs[i] + vr[i]
        if i < 4:
            vs[i + 1] = tot
            vcopy(i + 1).start()
        else:
            vout[...] = tot
    F, T, o = 1, 0, ZO
    def S0(kd, u): stage_0(kd, o[u])
    def A(kd, u): stage_a(kd, o[u])
    def B(kd, u): stage_b(kd, o[u])
    def C(kd, u): stage_c(kd, o[u])
    def Z(kd, u, hop): stage_d(kd, o[u], hop)

    @pl.when(g == 0)
    def _():
        barrier_all([(xn, z), (yn, z), (cn, z)] + [(dp, (z + j) % 4) for j in (1, 2, 3)])
        S0(F, 0)
        ysend(0, yin, z, "start")
        ownall(lambda h: own(0, h, 0).start())
        for j in (1, 2, 3): S0(F, j)
        cg = pltpu.make_async_copy(gs1, acc, sem.at[1]); cg.start()
        load_rows(z, xl, xs, xb, sem.at[0])
        distances(z, slen, llen, dm)
        xt[...] = xb[...].reshape(R, D).T
        gbs[...] = jnp.zeros_like(gbs)
        cg.wait()
        ga[...] = acc[...].astype(BF16)
        gat[...] = ga[...].T
        ownall(lambda h: (own(0, h, 0).wait(), own(0, h, 1).start()))
        yarr(0, 2, 2)
    wz, sm = w.at[0, 0], small.at[0]
    gc[...] = nt(ga[...], wz[576:768, :]).astype(BF16)
    kt[...] = k[0].T
    @pl.when(g == 2)
    def _():
        yarr(0, 2, 0)
    @pl.when(g == 3)
    def _():
        yarr(0, 2, 1)
    def hook(i):
        def on(n, j, fn):
            @pl.when((g == n) & (i == j))
            def _(): fn()
        on(0, 0, lambda: A(F, 0))
        on(0, 1, lambda: yarr(0, 0, 0))
        on(0, 3, lambda: A(F, 1))
        on(1, 0, lambda: yarr(0, 0, 1))
        on(1, 2, lambda: yarr(0, 1, 1))
        on(1, 3, lambda: B(F, 0))
        on(2, 2, lambda: (A(T, 0), C(F, 0), Z(F, 0, 0)))
    attend_bwd(z, sm, q8.at[0], k.at[0], v.at[0], kt, gc, dm, lse.at[0], gqt, gk, gv, hook)
    @pl.when(g == 0)
    def _():
        yarr(0, 1, 0)
    zg = zo(g)
    dq = gqt[...].astype(BF16).T
    dk = gk[...].astype(BF16)
    dv = gv[...].astype(BF16)
    gbs[zg, 0:1, 0:192] = jnp.sum(dq.astype(F32), axis=0, keepdims=True)
    gbs[zg, 1:2, 0:192] = jnp.sum(dv.astype(F32), axis=0, keepdims=True)
    acc[...] += nn(dq, wz[0:192, :]) + nn(dk, wz[192:384, :]) + nn(dv, wz[384:576, :])
    def X():
        for i in range(5):
            dxs[i] = acc[128 * i:128 * i + 128, :].astype(BF16)
        vs[0] = vin[...]
        for i in range(4):
            vs[0, 6 + 2 * i:8 + 2 * i, 0:192] = gbs[i, 0:2, 0:192]
        vcopy(0).start()
        ysend(1, dxs, z, "start")
        ownall(lambda h: own(1, h, 1).start())
    @pl.when(g == 1)
    def _():
        yarr(1, 2, 2)
    @pl.when(g == 2)
    def _():
        C(F, 1); Z(F, 1, 0); yarr(0, 1, 2); A(F, 2)
    @pl.when(g == 3)
    def _():
        X(); B(F, 2); A(T, 1)
    for i in range(6):
        rw = slice(128 * i, 128 * i + 128)
        gob[zg, 0, rw, :] = jnp.concatenate([nn(xt[rw, :], dq), nn(xt[rw, :], dk), nn(xt[rw, :], dv), nn(gat[rw, :], ctx[0])], axis=1).astype(BF16)
    @pl.when(g == 0)
    def _():
        S0(T, 0)
    @pl.when(g == 1)
    def _():
        B(F, 1); S0(T, 1)
    @pl.when(g == 2)
    def _():
        S0(T, 2)
    @pl.when(g == 3)
    def _():
        A(F, 3); C(F, 2); Z(F, 1, 1); S0(T, 3); Z(F, 2, 0); Z(F, 0, 1); vstep(0); B(T, 1); B(T, 0)
        yarr(1, 1, 1); B(F, 3); A(T, 2); A(T, 3); C(T, 1); C(T, 0); Z(T, 0, 0); Z(T, 1, 0); yarr(1, 0, 0)
        yarr(1, 0, 2); yarr(1, 1, 0); C(F, 3); Z(F, 0, 2); Z(F, 1, 2); yarr(0, 0, 2); yarr(1, 0, 1); Z(F, 3, 0); vstep(1)
        B(T, 2); yarr(1, 1, 2); C(T, 2); Z(F, 0, 3); Z(T, 2, 0); Z(T, 1, 1); B(T, 3); C(T, 3); vstep(2)
        Z(F, 1, 3); yarr(1, 2, 1); Z(F, 3, 1); Z(T, 0, 1); Z(T, 3, 0); vstep(3); Z(T, 0, 2); Z(T, 0, 3); Z(T, 1, 2)
        Z(T, 1, 3); Z(F, 2, 1); yarr(1, 2, 0); Z(T, 2, 1); Z(F, 3, 2); Z(F, 2, 2); vstep(4); Z(T, 2, 2); Z(T, 3, 2)
        Z(T, 3, 1)
        for kd in (0, 1):
            for zz in ZO:
                for q in range(4): st0(kd, zz, q).wait_send()
                for j in range(2):
                    s1x(kd, zz, j).wait_send(); s1y(kd, zz, j).wait_send()
                s1xy(kd, zz).wait_send(); s1yx(kd, zz).wait_send()
                @pl.when(z < zz)
                def _(): zs(kd, zz, True).wait_send()
                @pl.when(z > zz)
                def _(): zs(kd, zz, False).wait_send()
        for t, src in enumerate((yin, dxs)):
            ysend(t, src, z, "wait_send")
            for j in range(3):
                ysend(t, None, order[j], "wait_send")
            ownall(lambda h: own(t, h, 1).wait())
        for i in range(5): vcopy(i).wait_send()

def run_kx(slen, llen, xl, xs, W, small, q8, k, v, ctx, lse, gs1, g3, yv, vec):
    pz = lambda *s: pl.BlockSpec((1,) + s, lambda g, *_: (zo(g),) + (0,) * len(s))
    rz = lambda: pz(R, E)
    V, S = pltpu.VMEM, pltpu.SemaphoreType.DMA
    b = lambda *s: V(s + (PR, D), BF16)
    h = lambda *s: V(s + (H, D), BF16)
    bufs = lambda n: [b(4, 4, n), h(4, 2, n), h(4, 2, n), h(4, n), h(4, n), b(4, n), b(4, n)]
    scratch = [V((5, 128, D), BF16), V((5, 512, 128), F32), V((E, R), BF16), V((R, E), BF16), V((E, R), F32), V((R, E), F32), V((R, E), F32),
               V((R, D), BF16), V((D, R), BF16), V((D, R), BF16), V((R, D), F32), V((4, 1, D, D), BF16), V((5, 128, D), BF16), V((4, 8, 256), F32),
               V((5, 128, D), BF16), V((5, 16, D), F32), V((5, 16, D), F32), b(4, 4, 3)] + bufs(3) + bufs(1) + [
               S((2,)), S((2, 4, 4)), S((2, 4, 4)), S((4, 4)), S((2, 4, 6)), S((2, 4, 6)), S((2, 4)), S((2, 4, 2)), S((2, 4, 3, 2)), S((2, 4, 3)), S((5,)), S((5,)), S((2, 2, 2))]
    return pl.pallas_call(
        kx,
        grid_spec=pltpu.PrefetchScalarGridSpec(num_scalar_prefetch=2, grid=(4,),
            in_specs=[ANY, ANY, pl.BlockSpec((1, 1, D, D), lambda g, *_: (zo(g), 0, 0, 0)), pz(8, 256), rz(), rz(), rz(), rz(), pz(8, R), ANY, ANY, ANY, const((16, D))],
            out_specs=[const((4, PR, D)), ANY, ANY, const((16, D))], scratch_shapes=scratch),
        out_shape=[sds((4, PR, D), F32), sds((17, 128, D), BF16), sds((17, 128, D), BF16), sds((16, D), F32)],
        compiler_params=pltpu.CompilerParams(dimension_semantics=("arbitrary",), collective_id=1, has_side_effects=True, vmem_limit_bytes=VM),
        name="attention_backward_send")(slen, llen, xl, xs, W, small, q8, k, v, ctx, lse, gs1, g3, yv, vec)

def alibi_slopes(slope_index, head_total):
    power = 1 << head_total.bit_length() - 1
    f = slope_index.astype(F32)
    return jnp.where(slope_index < power, jnp.exp2(-8.0 * (f + 1.0) / power), jnp.exp2(-4.0 * (2.0 * (f - power) + 1.0) / power))
def prep(slope_index, w_qkv, b_qv, w_out, w_up, w_down):
    a = jnp.concatenate([jnp.transpose(w_qkv, (1, 2, 0)).reshape(576, D), w_out.T], 0)
    own = jnp.stack([a, w_up[:, 0], w_up[:, 1], w_down], 0)
    bt = jnp.transpose(b_qv, (1, 2, 0)).reshape(2, 192)
    sl = jnp.zeros((1, 192), F32).at[0, 0:3].set(alibi_slopes(slope_index, 12))
    small = jnp.pad(jnp.concatenate([bt, sl], 0), ((0, 5), (0, 64)))
    return own, small
def per_device(x_short, x_long, short_lengths, long_lengths, slope_index, w_qkv, b_qv, w_out, b_out, gain1, bias1, w_up, w_down, b_down, gain2, bias2, cot_short, cot_long):
    own, small = prep(slope_index, w_qkv, b_qv, w_out, w_up, w_down)
    vec = jnp.stack([b_out, gain1, bias1, b_down, gain2, bias2, bias2, bias2], 0)
    xl, cl = x_long.reshape(8, 128, D), cot_long.reshape(8, 128, D)
    W, S, q8, k, v, ctx, lse, n1, r1, hl = run_kg(short_lengths, long_lengths, own, small, xl, x_short, vec)
    a, b, inner, y, gf, gs2, vg2 = run_kb(cl, cot_short, W, hl, n1, vec)
    go3, gs1, vg1 = run_kc(W, a, b, inner, gf, hl, gs2, n1, r1, vec)
    m, dpx = lax.axis_index("mp"), lax.axis_index("dp")
    vsum = jnp.concatenate([vg2[:3], vg1[:3], jnp.zeros((10, D), F32)], 0)
    G, Y, DX, vs = run_kx(short_lengths, long_lengths, xl, x_short, W, S, q8, k, v, ctx, lse, gs1, go3, y.reshape(5, 128, D), vsum)
    b = lax.dynamic_slice(vs[6:14, :192].reshape(4, 2, 3, 64), (m, 0, 0, 8 * dpx), (1, 2, 3, 8))[0]
    vs = lax.dynamic_slice(vs[:6], (0, 96 * dpx), (6, 96))
    gq = G[0][:, :576].reshape(-1, 3, 192)
    return (Y[8:], Y[:8].reshape(2, 512, D), DX[8:], DX[:8].reshape(2, 512, D), gq, jnp.transpose(b, (2, 0, 1)), G[0][:, 576:], vs[5], vs[3], vs[4], jnp.stack([G[1], G[2]], 1), G[3], vs[2], vs[0], vs[1])
def per_device_any(x_short, x_long, short_lengths, long_lengths, slope_index, w_qkv, b_qv, w_out, b_out, gain1, bias1, w_up, w_down, b_down, gain2, bias2, cot_short, cot_long):
    own, small = prep(slope_index, w_qkv, b_qv, w_out, w_up, w_down)
    W = lax.all_gather(own, "mp"); S = lax.all_gather(small, "mp")
    vec = jnp.stack([b_out, gain1, bias1, b_down, gain2, bias2, bias2, bias2], 0)
    xl, cl = x_long.reshape(8, 128, D), cot_long.reshape(8, 128, D)
    q8, k, v, ctx, lse, n1, r1, hl = run_ka(short_lengths, long_lengths, xl, x_short, W, S, vec)
    a, b, inner, y, gf, gs2, vg2 = run_kb(cl, cot_short, W, hl, n1, vec)
    go3, gs1, vg1 = run_kc(W, a, b, inner, gf, hl, gs2, n1, r1, vec)
    go1, dx, gb = run_kd(short_lengths, long_lengths, xl, x_short, W, S, q8, k, v, ctx, lse, gs1.astype(BF16), gs1)
    m = lax.axis_index("mp")
    def spread(r):
        g = lax.all_gather(r, "mp")
        return jnp.concatenate([g[2], g[3][:512]], 0).reshape(9, 128, D), jnp.stack([g[0][:512], g[1][:512]], 0)
    ys, yl = spread(y); ds, dl = spread(dx)
    G = jnp.concatenate([go1, go3], 1).astype(F32)
    G = lax.psum_scatter(G, "mp", scatter_dimension=0, tiled=True)[0]
    G = lax.psum_scatter(G, "dp", scatter_dimension=1, tiled=True)
    vs = lax.psum(jnp.concatenate([vg2[:3], vg1[:3]], 0), "mp")
    vs = lax.psum_scatter(vs, "dp", scatter_dimension=1, tiled=True)
    gb = lax.psum_scatter(gb[:, :2, :192], "mp", scatter_dimension=0, tiled=True)[0]
    gb = jnp.transpose(gb.reshape(2, 3, 64), (2, 0, 1))
    gb = lax.psum_scatter(gb, "dp", scatter_dimension=0, tiled=True)
    gq = jnp.transpose(G[0][:, :576].reshape(-1, 3, 192), (0, 1, 2))
    return (ys, yl, ds, dl, gq, gb, G[0][:, 576:], vs[5], vs[3], vs[4], jnp.stack([G[1], G[2]], 1), G[3], vs[2], vs[0], vs[1])
def solution(mesh):
    fn = per_device if mesh.shape["dp"] == 8 else per_device_any
    d3 = P("dp", None, None)
    return jax.shard_map(fn, mesh=mesh,
        in_specs=(d3, d3, P("dp"), P("dp"), P("mp"), P(None, None, "mp"), P(None, None, "mp"), P(None, "mp"), P(), P(), P(), P(None, None, "mp"), P(None, "mp"), P(), P(), P(), d3, d3),
        out_specs=(d3, d3, d3, d3, P("dp", None, "mp"), P("dp", None, "mp"), P("dp", "mp"), P("dp"), P("dp"), P("dp"), P("dp", None, "mp"), P("dp", "mp"), P("dp"), P("dp"), P("dp")),
        check_vma=False)
```

```python
import functools
import math

import jax
import jax.numpy as jnp
from jax import lax
from jax.experimental import pallas as pl
from jax.experimental.pallas import tpu as pltpu
from jax.sharding import PartitionSpec as P

F32, BF16 = jnp.float32, jnp.bfloat16
R, D, E = 640, 768, 192
FAR = 1e30
VM = 60 << 20

def nn(a, b): return lax.dot_general(a, b, (((1,), (0,)), ((), ())), preferred_element_type=F32)
def nt(a, b): return lax.dot_general(a, b, (((1,), (1,)), ((), ())), preferred_element_type=F32)

def load_rows(m, long_ref, short_ref, buf, sem):
    @pl.when(m < 2)
    def _():
        c = pltpu.make_async_copy(long_ref.at[pl.ds(4 * m, 4)], buf.at[pl.ds(0, 4)], sem); c.start(); c.wait()
        buf[4] = jnp.zeros((128, D), BF16)
    @pl.when(m == 2)
    def _():
        c = pltpu.make_async_copy(short_ref.at[pl.ds(0, 5)], buf, sem); c.start(); c.wait()
    @pl.when(m == 3)
    def _():
        c = pltpu.make_async_copy(short_ref.at[pl.ds(5, 4)], buf.at[pl.ds(0, 4)], sem); c.start(); c.wait()
        buf[4] = jnp.zeros((128, D), BF16)

def distances(m, slen, llen, dm):
    @pl.when(m < 2)
    def _():
        n = llen[jnp.minimum(m, 1)]
        key = lax.broadcasted_iota(jnp.int32, (512, 128), 0)
        qry = lax.broadcasted_iota(jnp.int32, (512, 128), 1)
        for i in range(4):
            dist = jnp.abs(key - (qry + 128 * i)).astype(F32)
            dm[i] = jnp.where(key < n, dist, FAR)
    @pl.when(m >= 2)
    def _():
        key = lax.broadcasted_iota(jnp.int32, (128, 128), 0)
        qry = lax.broadcasted_iota(jnp.int32, (128, 128), 1)
        dist = jnp.abs(key - qry).astype(F32)
        for i in range(5):
            n = slen[jnp.minimum(5 * (m - 2) + i, 8)] if i == 4 else slen[jnp.maximum(5 * (m - 2), 0) + i]
            dm[i, 0:128, :] = jnp.where(key < n, dist, FAR)

def head_lanes(j):
    return lax.broadcasted_iota(jnp.int32, (1, E), 1) // 64 == j
def head_rows(j):
    return lax.broadcasted_iota(jnp.int32, (E, 1), 0) // 64 == j

def attend_fwd(m, small, q8, k, vt, dm, ct, lse, hook=lambda i: None):
    def block(i, keys, koff):
        cols = pl.ds(pl.multiple_of(i * 128, 128), 128)
        qi = q8[cols, :]
        kk = k[pl.ds(koff, keys), :]
        vv = vt[:, pl.ds(koff, keys)]
        d = dm[i, 0:keys, :]
        out = jnp.zeros((E, 128), F32)
        for j in range(3):
            s = nt(kk, jnp.where(head_lanes(j), qi, jnp.zeros_like(qi))) - small[2:3, j:j + 1] * d
            mx = jnp.max(s, axis=0, keepdims=True)
            ex = jnp.exp(s - mx)
            tot = jnp.sum(ex, axis=0, keepdims=True)
            p = (ex * (1.0 / tot)).astype(BF16)
            out = jnp.where(head_rows(j), nn(vv, p), out)
            lse[j:j + 1, cols] = mx + jnp.log(tot)
        ct[:, cols] = out.astype(BF16)
    @pl.when(m < 2)
    def _():
        lax.fori_loop(0, 4, lambda i, u: (block(i, 512, 0), hook(i), u)[2], 0)
    @pl.when(m >= 2)
    def _():
        lax.fori_loop(0, 5, lambda i, u: (block(i, 128, pl.multiple_of(i * 128, 128)), hook(i), u)[2], 0)

def attend_bwd(m, small, q8, k, v, kt, gc, dm, lse, gqt, gk, gv, hook=lambda i: None):
    gk[...] = jnp.zeros_like(gk)
    gv[...] = jnp.zeros_like(gv)
    def block(i, keys, koff):
        cols = pl.ds(pl.multiple_of(i * 128, 128), 128)
        rows = pl.ds(koff, keys)
        qi, gi = q8[cols, :], gc[cols, :]
        kk, vv, ktt = k[rows, :], v[rows, :], kt[:, rows]
        d = dm[i, 0:keys, :]
        oq = jnp.zeros((E, 128), F32)
        ok = jnp.zeros((keys, E), F32)
        ov = jnp.zeros((keys, E), F32)
        for j in range(3):
            hl = head_lanes(j)
            qj = jnp.where(hl, qi, jnp.zeros_like(qi))
            gj = jnp.where(hl, gi, jnp.zeros_like(gi))
            s = nt(kk, qj) - small[2:3, j:j + 1] * d
            p = jnp.exp(s - lse[j:j + 1, cols])
            gp = nt(vv, gj)
            ov = ov + nn(p.astype(BF16), gj)
            row = jnp.sum(p * gp, axis=0, keepdims=True)
            ds = (p * (gp - row)).astype(BF16)
            oq = jnp.where(head_rows(j), nn(ktt, ds), oq)
            ok = ok + nn(ds, qj)
        gqt[:, cols] = oq * 0.125
        gk[rows, :] += ok
        gv[rows, :] += ov
    @pl.when(m < 2)
    def _():
        lax.fori_loop(0, 4, lambda i, u: (block(i, 512, 0), hook(i), u)[2], 0)
        gqt[:, 512:640] = jnp.zeros((E, 128), F32)
    @pl.when(m >= 2)
    def _():
        lax.fori_loop(0, 5, lambda i, u: (block(i, 128, pl.multiple_of(i * 128, 128)), hook(i), u)[2], 0)

def norm_fwd(s):
    mean = jnp.mean(s, axis=1, keepdims=True)
    c = s - mean
    r = lax.rsqrt(jnp.mean(c * c, axis=1, keepdims=True) + 1e-12)
    return c * r, r

def norm_bwd(gn, normed, r):
    return r * (gn - jnp.mean(gn, axis=1, keepdims=True) - normed * jnp.mean(gn * normed, axis=1, keepdims=True))

def row_tiles(fn, tile=640):
    def body(i, u):
        fn(pl.ds(pl.multiple_of(i * tile, tile), tile)); return u
    lax.fori_loop(0, R // tile, body, 0)

def ka(slen, llen, xl, xs, w, small, vec, q8o, ko, vo, co, lseo, n1o, r1o, hlo, xb, dm, vt, ct, acc, sem):
    z = pl.program_id(0)
    m = lax.axis_index("mp")
    @pl.when(z == 0)
    def _():
        load_rows(m, xl, xs, xb, sem)
        distances(m, slen, llen, dm)
        ct[...] = jnp.zeros_like(ct)
        lseo[...] = jnp.zeros_like(lseo)
        acc[...] = jnp.zeros_like(acc)
    x = xb[...].reshape(R, D)
    wz, sm = w.at[0, 0], small.at[0]
    q8o[0] = ((nt(x, wz[0:192, :]) + sm[0:1, 0:192]).astype(BF16).astype(F32) * 0.125).astype(BF16)
    ko[0] = nt(x, wz[192:384, :]).astype(BF16)
    v = (nt(x, wz[384:576, :]) + sm[1:2, 0:192]).astype(BF16)
    vo[0] = v
    vt[...] = v.T
    attend_fwd(m, sm, q8o.at[0], ko.at[0], vt, dm, ct, lseo.at[0])
    co[0] = ct[...].T
    acc[...] += nn(co[0], wz[576:768, :]).astype(BF16).astype(F32)
    @pl.when(z == 3)
    def _():
        for i in range(5):
            rows = slice(128 * i, 128 * i + 128)
            s = xb[i].astype(F32) + acc[rows, :] + vec[0:1, :]
            n, r = norm_fwd(s)
            n1o[rows, :] = n
            r1o[rows, :] = jnp.broadcast_to(r, (128, 128))
            hlo[rows, :] = (n * vec[1:2, :] + vec[2:3, :]).astype(BF16)

def const(shape): return pl.BlockSpec(shape, lambda z, *_: (0,) * len(shape))
def perz(shape): return pl.BlockSpec((1,) + shape, lambda z, *_: (z,) + (0,) * len(shape))
ANY = pl.BlockSpec(memory_space=pl.ANY)
def sds(shape, dt): return jax.ShapeDtypeStruct(shape, dt)
def part(p): return pl.BlockSpec((1, 1, D, D), lambda z, *_: (z, p, 0, 0))

def call(kernel, in_specs, outs, scratch, name, args, grid=(4,), prefetch=2):
    return pl.pallas_call(
        kernel,
        grid_spec=pltpu.PrefetchScalarGridSpec(num_scalar_prefetch=prefetch, grid=grid, in_specs=in_specs,
            out_specs=[o[0] for o in outs], scratch_shapes=scratch),
        out_shape=[o[1] for o in outs],
        compiler_params=pltpu.CompilerParams(dimension_semantics=("arbitrary",), vmem_limit_bytes=VM),
        name=name)(*args)

def run_ka(slen, llen, xl, xs, W, small, vec):
    rz = lambda: (perz((R, E)), sds((4, R, E), BF16))
    return call(ka, [ANY, ANY, part(0), perz((8, 256)), const((8, D))],
        [rz(), rz(), rz(), rz(), (perz((8, R)), sds((4, 8, R), F32)), (const((R, D)), sds((R, D), F32)), (const((R, 128)), sds((R, 128), F32)), (const((R, D)), sds((R, D), BF16))],
        [pltpu.VMEM((5, 128, D), BF16), pltpu.VMEM((5, 512, 128), F32), pltpu.VMEM((E, R), BF16), pltpu.VMEM((E, R), BF16), pltpu.VMEM((R, D), F32), pltpu.SemaphoreType.DMA],
        "attention_forward", (slen, llen, xl, xs, W, small, vec))

def gelu_parts(g):
    cdf = 0.5 * (1.0 + lax.erf(g * (2.0 ** -0.5)))
    pdf = jnp.exp(-0.5 * g * g) * (1.0 / math.sqrt(2 * math.pi))
    return g * cdf, cdf + g * pdf

def kb(cl, cs, wg, wu, wd, hl, n1, vec, ao, bo, io, yo, gfo, gs2o, vgo, acc, cb, sem):
    z = pl.program_id(0)
    m = lax.axis_index("mp")
    @pl.when(z == 0)
    def _():
        load_rows(m, cl, cs, cb, sem)
        acc[...] = jnp.zeros_like(acc)
    def tile(rows):
        h = hl[rows, :]
        gate = nn(h, wg[0, 0])
        up = nn(h, wu[0, 0])
        a, slope = gelu_parts(gate)
        ao[0, rows, :] = a
        bo[0, rows, :] = up * slope
        inner = (a * up).astype(BF16)
        io[0, rows, :] = inner
        acc[rows, :] += nt(inner, wd[0, 0]).astype(BF16).astype(F32)
    row_tiles(tile)
    @pl.when(z == 3)
    def _():
        tot = [jnp.zeros((1, D), F32)] * 3
        for i in range(5):
            rows = slice(128 * i, 128 * i + 128)
            h1 = n1[rows, :] * vec[1:2, :] + vec[2:3, :]
            n, r = norm_fwd(h1 + acc[rows, :] + vec[3:4, :])
            yo[rows, :] = (n * vec[4:5, :] + vec[5:6, :]).astype(BF16)
            gy = cb[i].astype(F32)
            gs = norm_bwd(gy * vec[4:5, :], n, r)
            gs2o[rows, :] = gs
            gfo[rows, :] = gs.astype(BF16)
            tot = [tot[0] + jnp.sum(gy * n, axis=0, keepdims=True), tot[1] + jnp.sum(gy, axis=0, keepdims=True), tot[2] + jnp.sum(gs, axis=0, keepdims=True)]
        vgo[...] = jnp.concatenate(tot + [jnp.zeros((5, D), F32)], axis=0)

def run_kb(cl, cs, W, hl, n1, vec):
    z32 = lambda: (perz((R, D)), sds((4, R, D), F32))
    return call(kb, [ANY, ANY, part(1), part(2), part(3), const((R, D)), const((R, D)), const((8, D))],
        [z32(), z32(), (perz((R, D)), sds((4, R, D), BF16)), (const((R, D)), sds((R, D), BF16)), (const((R, D)), sds((R, D), BF16)), (const((R, D)), sds((R, D), F32)), (const((8, D)), sds((8, D), F32))],
        [pltpu.VMEM((R, D), F32), pltpu.VMEM((5, 128, D), BF16), pltpu.SemaphoreType.DMA],
        "feed_forward", (cl, cs, W, W, W, hl, n1, vec), prefetch=0)

def kc(wg, wu, wd, a, b, inner, gf, hl, gs2, n1, r1, vec, go, gs1o, vgo, acc, gft, hlt, gg):
    z = pl.program_id(0)
    @pl.when(z == 0)
    def _():
        acc[...] = gs2[...]
        gft[...] = gf[...].T
        hlt[...] = hl[...].T
    def tile(rows):
        gi = nn(gf[rows, :], wd[0, 0])
        g1 = (gi * b[0, rows, :]).astype(BF16)
        g2 = (gi * a[0, rows, :]).astype(BF16)
        gg[0, rows, :] = g1
        gg[1, rows, :] = g2
        acc[rows, :] += nt(g1, wg[0, 0]) + nt(g2, wu[0, 0])
    row_tiles(tile)
    def wtile(rows):
        go[0, 2, rows, :] = nn(gft[rows, :], inner[0]).astype(BF16)
        go[0, 0, rows, :] = nn(hlt[rows, :], gg[0]).astype(BF16)
        go[0, 1, rows, :] = nn(hlt[rows, :], gg[1]).astype(BF16)
    wtile(slice(0, D))
    @pl.when(z == 3)
    def _():
        tot = [jnp.zeros((1, D), F32)] * 3
        for i in range(5):
            rows = slice(128 * i, 128 * i + 128)
            gh, n = acc[rows, :], n1[rows, :]
            gs = norm_bwd(gh * vec[1:2, :], n, r1[rows, 0:1])
            gs1o[rows, :] = gs
            tot = [tot[0] + jnp.sum(gh * n, axis=0, keepdims=True), tot[1] + jnp.sum(gh, axis=0, keepdims=True), tot[2] + jnp.sum(gs, axis=0, keepdims=True)]
        vgo[...] = jnp.concatenate(tot + [jnp.zeros((5, D), F32)], axis=0)

def run_kc(W, a, b, inner, gf, hl, gs2, n1, r1, vec):
    c = lambda dt: const((R, D))
    return call(kc, [part(1), part(2), part(3), perz((R, D)), perz((R, D)), perz((R, D)), c(0), c(0), c(0), c(0), const((R, 128)), const((8, D))],
        [(pl.BlockSpec((1, 3, D, D), lambda z: (z, 0, 0, 0)), sds((4, 3, D, D), BF16)), (const((R, D)), sds((R, D), F32)), (const((8, D)), sds((8, D), F32))],
        [pltpu.VMEM((R, D), F32), pltpu.VMEM((D, R), BF16), pltpu.VMEM((D, R), BF16), pltpu.VMEM((2, R, D), BF16)],
        "feed_backward", (W, W, W, a, b, inner, gf, hl, gs2, n1, r1, vec), prefetch=0)

def kd(slen, llen, xl, xs, w, small, q8, k, v, ctx, lse, ga, gs1, go, dxo, gbo, xb, dm, kt, gc, gqt, gk, gv, gat, xt, acc, sem):
    z = pl.program_id(0)
    m = lax.axis_index("mp")
    @pl.when(z == 0)
    def _():
        load_rows(m, xl, xs, xb, sem)
        distances(m, slen, llen, dm)
        acc[...] = gs1[...]
        gat[...] = ga[...].T
        xt[...] = xb[...].reshape(R, D).T
        gbo[...] = jnp.zeros_like(gbo)
    wz, sm = w.at[0, 0], small.at[0]
    gc[...] = nt(ga[...], wz[576:768, :]).astype(BF16)
    kt[...] = k[0].T
    attend_bwd(m, sm, q8.at[0], k.at[0], v.at[0], kt, gc, dm, lse.at[0], gqt, gk, gv)
    dq = gqt[...].astype(BF16).T
    dk = gk[...].astype(BF16)
    dv = gv[...].astype(BF16)
    gbo[z, 0:1, 0:192] = jnp.sum(dq.astype(F32), axis=0, keepdims=True)
    gbo[z, 1:2, 0:192] = jnp.sum(dv.astype(F32), axis=0, keepdims=True)
    acc[...] += nn(dq, wz[0:192, :]) + nn(dk, wz[192:384, :]) + nn(dv, wz[384:576, :])
    def wtile(rows):
        xr = xt[rows, :]
        go[0, 0, rows, :] = jnp.concatenate([nn(xr, dq), nn(xr, dk), nn(xr, dv), nn(gat[rows, :], ctx[0])], axis=1).astype(BF16)
    for i in range(6):
        wtile(slice(128 * i, 128 * i + 128))
    @pl.when(z == 3)
    def _():
        dxo[...] = acc[...].astype(BF16)

def run_kd(slen, llen, xl, xs, W, small, q8, k, v, ctx, lse, ga, gs1):
    rz = lambda: perz((R, E))
    rd = const((R, D))
    return call(kd, [ANY, ANY, part(0), perz((8, 256)), rz(), rz(), rz(), rz(), perz((8, R)), rd, rd],
        [(pl.BlockSpec((1, 1, D, D), lambda z, *_: (z, 0, 0, 0)), sds((4, 1, D, D), BF16)), (rd, sds((R, D), BF16)), (const((4, 8, 256)), sds((4, 8, 256), F32))],
        [pltpu.VMEM((5, 128, D), BF16), pltpu.VMEM((5, 512, 128), F32), pltpu.VMEM((E, R), BF16), pltpu.VMEM((R, E), BF16), pltpu.VMEM((E, R), F32), pltpu.VMEM((R, E), F32), pltpu.VMEM((R, E), F32),
         pltpu.VMEM((D, R), BF16), pltpu.VMEM((D, R), BF16), pltpu.VMEM((R, D), F32), pltpu.SemaphoreType.DMA],
        "attention_backward", (slen, llen, xl, xs, W, small, q8, k, v, ctx, lse, ga, gs1))

MESH = pl.DeviceIdType.MESH
PR = 96

def place():
    dp = lax.axis_index("dp"); z = lax.axis_index("mp")
    return dp, dp // 4, (dp // 2) % 2, dp % 2, z

def dpi(y, x, c):
    return (y * 2 + x) * 2 + c

def barrier_all(peers):
    b = pltpu.get_barrier_semaphore()
    for d in peers:
        pl.semaphore_signal(b, inc=1, device_id=d, device_id_type=MESH)
    pl.semaphore_wait(b, len(peers))

def kg(slen, llen, own, small, xl, xs, cl, cs, vec, out, sout, q8o, ko, vo, co, lseo, n1o, r1o, hlo, ao, bo, io, yo, gfo, gs2o, vgo,
       ssm, xb, dm, vt, ct, acc, wz, wf, ab, bb, ib, recv, send, loc, ss, sr, sem, lsem, osem):
    g = pl.program_id(0)
    dp, y, x, c, z = place()
    xn, yn, cn = dpi(y, 1 - x, c), dpi(1 - y, x, c), dpi(y, x, 1 - c)
    dn = dpi(1 - y, 1 - x, c)
    def sm(j): return pltpu.make_async_remote_copy(src_ref=small, dst_ref=ssm.at[z], send_sem=ss.at[j], recv_sem=sr.at[z], device_id=(dp, (z + 1 + j) % 4), device_id_type=MESH)
    e = 1 - ((z + 1) // 2) % 2
    srcs = [z + 1 - 2 * (z % 2), e * ((z + 2) % 4) + (1 - e) * (3 - z), e * (3 - z) + (1 - e) * ((z + 2) % 4)]

    def rows(p, h):
        if h is None:
            return pl.ds(pl.multiple_of(p * PR, 32), PR)
        return pl.ds(pl.multiple_of(p * PR + h * (PR // 2), 16), PR // 2)
    def piece(s, g, p, h=None):
        return out.at[s, g, rows(p, h), :]
    def opiece(g, p):
        return own.at[g, rows(p, None), :]
    def cp(src, dst, s, g, k, r, dev):
        return pltpu.make_async_remote_copy(src_ref=src, dst_ref=dst, send_sem=send.at[s, g, k], recv_sem=recv.at[s, g, r], device_id=dev, device_id_type=MESH)
    def zsend(src, s, g):
        @pl.when((s <= z) & (z < 3))
        def _():
            cp(src, piece(s, g, dp), s, g, 0, 0, (dp, z + 1)).start()
        @pl.when((s >= z) & (z > 0))
        def _():
            cp(src, piece(s, g, dp), s, g, 1, 0, (dp, z - 1)).start()
    def zsend_wait(src, s, g):
        @pl.when((s <= z) & (z < 3))
        def _():
            cp(src, piece(s, g, dp), s, g, 0, 0, (dp, z + 1)).wait_send()
        @pl.when((s >= z) & (z > 0))
        def _():
            cp(src, piece(s, g, dp), s, g, 1, 0, (dp, z - 1)).wait_send()
    def simple(s, g):
        me, xp, yp, dg = dp, xn, yn, dn
        return dict(
            x=lambda: cp(piece(s, g, me), piece(s, g, me), s, g, 2, 1, (xn, z)),
            y=lambda: cp(piece(s, g, me), piece(s, g, me), s, g, 3, 2, (yn, z)),
            c=lambda: cp(piece(s, g, me), piece(s, g, me), s, g, 4, 3, (cn, z)),
            cx=lambda: cp(piece(s, g, xp), piece(s, g, xp), s, g, 5, 4, (cn, z)),
            cy=lambda: cp(piece(s, g, yp), piece(s, g, yp), s, g, 6, 5, (cn, z)),
            yf=lambda: cp(piece(s, g, xp, 0), piece(s, g, xp, 0), s, g, 7, 6, (yn, z)),
            xf=lambda: cp(piece(s, g, yp, 1), piece(s, g, yp, 1), s, g, 8, 7, (xn, z)),
            cd0=lambda: cp(piece(s, g, dg, 0), piece(s, g, dg, 0), s, g, 9, 8, (cn, z)),
            cd1=lambda: cp(piece(s, g, dg, 1), piece(s, g, dg, 1), s, g, 10, 9, (cn, z)),
        )
    def wrecv(ref, s, g, r):
        pltpu.make_async_remote_copy(src_ref=ref, dst_ref=ref, send_sem=send.at[s, g, 0], recv_sem=recv.at[s, g, r], device_id=(cn, z), device_id_type=MESH).wait_recv()
    def zarr(j, g):
        s = srcs[j]
        wrecv(piece(s, g, dp), s, g, 0)
        zsend(piece(s, g, dp), s, g)
        m = simple(s, g)
        m["x"]().start(); m["y"]().start(); m["c"]().start()
    def xyarr(j, g):
        s = srcs[j]; m = simple(s, g)
        wrecv(piece(s, g, xn), s, g, 1)
        m["yf"]().start(); m["cx"]().start()
        wrecv(piece(s, g, yn), s, g, 2)
        m["xf"]().start(); m["cy"]().start()
    def diag(j, g):
        s = srcs[j]; m = simple(s, g)
        wrecv(piece(s, g, dn, 0), s, g, 6)
        m["cd0"]().start()
        wrecv(piece(s, g, dn, 1), s, g, 7)
        m["cd1"]().start()
    def landed(j, g):
        s = srcs[j]
        cdx, cdy, cdd = dpi(y, 1 - x, 1 - c), dpi(1 - y, x, 1 - c), dpi(1 - y, 1 - x, 1 - c)
        wrecv(piece(s, g, cn), s, g, 3)
        wrecv(piece(s, g, cdx), s, g, 4)
        wrecv(piece(s, g, cdy), s, g, 5)
        wrecv(piece(s, g, cdd, 0), s, g, 8)
        wrecv(piece(s, g, cdd, 1), s, g, 9)
    def sent(j, g):
        s = srcs[j]; m = simple(s, g)
        zsend_wait(piece(s, g, dp), s, g)
        for k in ("x", "y", "c", "cx", "cy", "yf", "xf", "cd0", "cd1"):
            m[k]().wait_send()
    l0 = pltpu.make_async_copy(wz, out.at[z, 0], loc.at[0])
    l1 = pltpu.make_async_copy(own.at[pl.ds(1, 3)], wf.at[0], lsem.at[0])
    l2 = pltpu.make_async_copy(wf.at[0], out.at[z, pl.ds(1, 3)], loc.at[1])
    def fetch(j):
        landed(j, 0)
        cw = pltpu.make_async_copy(out.at[srcs[j], 0], wz, sem.at[1]); cw.start()
        pltpu.make_async_remote_copy(src_ref=small, dst_ref=ssm.at[srcs[j]], send_sem=ss.at[j], recv_sem=sr.at[srcs[j]], device_id=(cn, z), device_id_type=MESH).wait_recv()
        cw.wait()
    def fcopy(j): return pltpu.make_async_copy(out.at[srcs[j], pl.ds(1, 3)], wf.at[(j + 1) % 2], lsem.at[(j + 1) % 2])
    def load(j):
        for p in (1, 2, 3): landed(j, p)
        fcopy(j).start()
    blocks = [z] + srcs
    def stores(n):
        return [pltpu.make_async_copy(f.at[n % 2], t.at[blocks[n]], osem.at[i, n % 2]) for i, (f, t) in enumerate(((ab, ao), (bb, bo), (ib, io)))]
    Z, XY, DG = zarr, xyarr, diag
    def mine(p): zsend(opiece(p, dp), z, p)

    @pl.when(g == 0)
    def _():
        barrier_all([(xn, z), (yn, z), (cn, z)] + [(dp, (z + j) % 4) for j in (1, 2, 3)])
        mine(0); mine(1)
        for j in range(3): sm(j).start()
        cw = pltpu.make_async_copy(own.at[0], wz, sem.at[1]); cw.start()
        l1.start()
        ssm[z] = small[...]
        load_rows(z, xl, xs, xb, sem.at[0])
        distances(z, slen, llen, dm)
        ct[...] = jnp.zeros_like(ct)
        lseo[...] = jnp.zeros_like(lseo)
        acc[...] = jnp.zeros_like(acc)
        cw.wait()
        l0.start()
        Z(0, 0); Z(1, 0); mine(2)
    n4 = lax.rem(g, 4)
    zz = jnp.where(n4 == 0, z, jnp.where(n4 == 1, srcs[0], jnp.where(n4 == 2, srcs[1], srcs[2])))
    @pl.when(g < 4)
    def _():
        xv = xb[...].reshape(R, D)
        bs = ssm.at[zz]
        q8o[zz] = ((nt(xv, wz[0:192, :]) + bs[0:1, 0:192]).astype(BF16).astype(F32) * 0.125).astype(BF16)
        ko[zz] = nt(xv, wz[192:384, :]).astype(BF16)
        v = (nt(xv, wz[384:576, :]) + bs[1:2, 0:192]).astype(BF16)
        vo[zz] = v
        vt[...] = v.T
        @pl.when(g == 2)
        def _():
            Z(0, 3)
        def hook(i):
            def on(n, j, fn):
                @pl.when((g == n) & (i == j))
                def _(): fn()
            on(0, 0, lambda: (XY(0, 0),))
            on(0, 1, lambda: (Z(0, 1), Z(2, 0),))
            on(0, 2, lambda: (XY(1, 0),))
            on(0, 3, lambda: (DG(0, 0), Z(1, 2), mine(3),))
            on(1, 0, lambda: (XY(2, 0),))
            on(1, 2, lambda: (DG(1, 0), Z(1, 1),))
            on(2, 1, lambda: (DG(2, 0),))
            on(2, 2, lambda: (XY(0, 1),))
            on(2, 3, lambda: (XY(1, 2), XY(1, 1), XY(0, 2),))
            on(3, 0, lambda: (XY(1, 3),))
            on(3, 1, lambda: (XY(0, 3), Z(2, 2),))
        attend_fwd(z, bs, q8o.at[zz], ko.at[zz], vt, dm, ct, lseo.at[zz], hook)
        cv = ct[...].T
        co[zz] = cv
        acc[...] += nn(cv, wz[576:768, :]).astype(BF16).astype(F32)
    @pl.when(g == 0)
    def _():
        l1.wait(); l2.start(); l0.wait(); Z(0, 2); fetch(0)
    @pl.when(g == 1)
    def _():
        fetch(1); Z(1, 3)
    @pl.when(g == 2)
    def _():
        fetch(2)
    @pl.when(g == 3)
    def _():
        Z(2, 3); DG(1, 1)
    @pl.when(g == 3)
    def _():
        sout[...] = ssm[...]
        for i in range(5):
            rw = slice(128 * i, 128 * i + 128)
            s = xb[i].astype(F32) + acc[rw, :] + vec[0:1, :]
            n, r = norm_fwd(s)
            n1o[rw, :] = n
            r1o[rw, :] = jnp.broadcast_to(r, (128, 128))
            hlo[rw, :] = (n * vec[1:2, :] + vec[2:3, :]).astype(BF16)
        acc[...] = jnp.zeros_like(acc)
        DG(1, 3); DG(0, 1); Z(2, 1); DG(0, 3); DG(0, 2)
        load_rows(z, cl, cs, xb, sem.at[0])
        DG(1, 2)
    for n in (1, 2, 3):
        @pl.when(g == 4 + n)
        def _():
            fcopy(n - 1).wait()
            if n > 1:
                for d in stores(n - 2): d.wait()
    @pl.when(g >= 4)
    def _():
        p = lax.rem(g, 2)
        def on(n, i, j, fn):
            @pl.when((g == n) & (i == j))
            def _(): fn()
        def tile(i, u):
            rw = pl.ds(pl.multiple_of(i * (R // 2), 64), R // 2)
            h = hlo[rw, :]
            gate = nn(h, wf[p, 0])
            up = nn(h, wf[p, 1])
            a, slope = gelu_parts(gate)
            ab[p, rw, :] = a
            bb[p, rw, :] = up * slope
            inner = (a * up).astype(BF16)
            ib[p, rw, :] = inner
            acc[rw, :] += nt(inner, wf[p, 2]).astype(BF16).astype(F32)
            on(4, i, 0, lambda: (load(0), XY(2, 3),))
            on(6, i, 0, lambda: (load(2),))
            return u
        lax.fori_loop(0, 2, tile, 0)
    for n in range(4):
        @pl.when(g == 4 + n)
        def _():
            for d in stores(n): d.start()
    @pl.when(g == 4)
    def _():
        l2.wait(); XY(2, 2); load(1); XY(2, 1)
    @pl.when(g == 5)
    def _():
        DG(2, 1); DG(2, 2); DG(2, 3)
    @pl.when(g == 7)
    def _():
        tot = [jnp.zeros((1, D), F32)] * 3
        for i in range(5):
            rw = slice(128 * i, 128 * i + 128)
            h1 = n1o[rw, :] * vec[1:2, :] + vec[2:3, :]
            n, r = norm_fwd(h1 + acc[rw, :] + vec[3:4, :])
            yo[rw, :] = (n * vec[4:5, :] + vec[5:6, :]).astype(BF16)
            gy = xb[i].astype(F32)
            gs = norm_bwd(gy * vec[4:5, :], n, r)
            gs2o[rw, :] = gs
            gfo[rw, :] = gs.astype(BF16)
            tot = [tot[0] + jnp.sum(gy * n, axis=0, keepdims=True), tot[1] + jnp.sum(gy, axis=0, keepdims=True), tot[2] + jnp.sum(gs, axis=0, keepdims=True)]
        vgo[...] = jnp.concatenate(tot + [jnp.zeros((5, D), F32)], axis=0)
        pass
        for p in range(4):
            zsend_wait(opiece(p, dp), z, p)
        for j in range(3):
            sm(j).wait_send()
            for p in range(4): sent(j, p)
        for n in (2, 3):
            for d in stores(n): d.wait()

def run_kg(slen, llen, own, small, xl, xs, cl, cs, vec):
    V, S = pltpu.VMEM, pltpu.SemaphoreType.DMA
    o = lambda *s: const(s)
    rz = lambda: sds((4, R, E), BF16)
    return pl.pallas_call(
        kg,
        grid_spec=pltpu.PrefetchScalarGridSpec(num_scalar_prefetch=2, grid=(8,),
            in_specs=[ANY, o(8, 256), ANY, ANY, ANY, ANY, o(8, D)],
            out_specs=[ANY, o(4, 8, 256), o(4, R, E), o(4, R, E), o(4, R, E), o(4, R, E), o(4, 8, R), o(R, D), o(R, 128), o(R, D), ANY, ANY, ANY, o(R, D), o(R, D), o(R, D), o(8, D)],
            scratch_shapes=[V((4, 8, 256), F32), V((5, 128, D), BF16), V((5, 512, 128), F32), V((E, R), BF16), V((E, R), BF16), V((R, D), F32), V((D, D), BF16),
                            V((2, 3, D, D), BF16), V((2, R, D), F32), V((2, R, D), F32), V((2, R, D), BF16),
                            S((4, 4, 10)), S((4, 4, 11)), S((2,)), S((3,)), S((4,)), S((2,)), S((2,)), S((3, 2))]),
        out_shape=[sds((4, 4, D, D), BF16), sds((4, 8, 256), F32), rz(), rz(), rz(), rz(), sds((4, 8, R), F32), sds((R, D), F32), sds((R, 128), F32), sds((R, D), BF16),
                   sds((4, R, D), F32), sds((4, R, D), F32), sds((4, R, D), BF16), sds((R, D), BF16), sds((R, D), BF16), sds((R, D), F32), sds((8, D), F32)],
        compiler_params=pltpu.CompilerParams(dimension_semantics=("arbitrary",), collective_id=0, has_side_effects=True, vmem_limit_bytes=VM),
        name="gather_forward")(slen, llen, own, small, xl, xs, cl, cs, vec)

ZO = (3, 0, 2, 1)

def far_order(z):
    e = 1 - ((z + 1) // 2) % 2
    return [z + 1 - 2 * (z % 2), e * ((z + 2) % 4) + (1 - e) * (3 - z), e * (3 - z) + (1 - e) * ((z + 2) % 4)]

H = PR // 2

def zo(g):
    h, e = g // 2, g * (3 - g) // 2
    return (1 - e) * (3 - 2 * h) + e * 2 * h

def add_into(n, dst, src):
    def body(i, u):
        d, r = dst(i), src(i)
        d[...] = (d[...].astype(F32) + r[...].astype(F32)).astype(BF16)
        return u
    lax.fori_loop(0, n, body, 0)

def kx(slen, llen, xl, xs, w, small, q8, k, v, ctx, lse, gs1, g3, yin, vin, gqo, gwo, guo, gdo, yout, dxout, vout,
       xb, dm, kt, gc, gqt, gk, gv, ga, gat, xt, acc, gob, dxs, gbs, stage, vr, vs, l0,
       r03, rx3, ry3, rxy3, ryx3, rl3, rr3, r01, rx1, ry1, rxy1, ryx1, rl1, rr1,
       sem, s0s, s0r, s0l, s1s, s1r, s2s, s2r, ys, yr, vsem_s, vsem_r, loc):
    g = pl.program_id(0)
    dp, y, x, c, z = place()
    xn, yn, cn = dpi(y, 1 - x, c), dpi(1 - y, x, c), dpi(y, x, 1 - c)
    z1, z2 = z + 1 - 2 * (z % 2), (z + 2) % 4
    parts = (1, 3)
    r0, rx, ry, rxy, ryx, rl, rr = (r01, r03), (rx1, rx3), (ry1, ry3), (rxy1, rxy3), (ryx1, ryx3), (rl1, rl3), (rr1, rr3)
    def rows(p): return pl.ds(pl.multiple_of(p * PR, 32), PR)
    def rc(src, dst, ss, rs, dev):
        return pltpu.make_async_remote_copy(src_ref=src, dst_ref=dst, send_sem=ss, recv_sem=rs, device_id=dev, device_id_type=MESH)
    def blk(kd, zz, q):
        return l0.at[zz, q] if kd else gob.at[zz, :, rows(2 * q + c), :]
    def half(kd, zz, q, h):
        return l0.at[zz, q, :, pl.ds(h * H, H), :] if kd else gob.at[zz, :, pl.ds(pl.multiple_of((2 * q + c) * PR + h * H, 16), H), :]
    def st0(kd, zz, q):
        src = (g3 if kd else gob).at[zz, :, rows(2 * q + 1 - c), :]
        return rc(src, r0[kd].at[zz, q], s0s.at[kd, zz, q], s0r.at[kd, zz, q], (cn, z))
    def ld0(zz, q):
        return pltpu.make_async_copy(g3.at[zz, :, rows(2 * q + c), :], l0.at[zz, q], s0l.at[zz, q])
    def stage_0(kd, zz):
        for q in range(4):
            st0(kd, zz, q).start()
            if kd: ld0(zz, q).start()
    def stage_a(kd, zz):
        for q in range(4):
            st0(kd, zz, q).wait_recv()
            if kd: ld0(zz, q).wait()
        n = parts[kd]
        add_into(4 * n, lambda i: blk(kd, zz, i // n).at[i % n], lambda i: r0[kd].at[zz, i // n, i % n])
        for j in range(2):
            s1x(kd, zz, j).start(); s1y(kd, zz, j).start()
    def s1x(kd, zz, j):
        return rc(half(kd, zz, 2 * j + 1 - x, 0), rx[kd].at[zz, j], s1s.at[kd, zz, j], s1r.at[kd, zz, j], (xn, z))
    def s1y(kd, zz, j):
        return rc(half(kd, zz, 2 * (1 - y) + j, 1), ry[kd].at[zz, j], s1s.at[kd, zz, 2 + j], s1r.at[kd, zz, 2 + j], (yn, z))
    def s1xy(kd, zz):
        return rc(half(kd, zz, 2 * (1 - y) + x, 0), rxy[kd].at[zz], s1s.at[kd, zz, 4], s1r.at[kd, zz, 4], (yn, z))
    def s1yx(kd, zz):
        return rc(half(kd, zz, 2 * y + 1 - x, 1), ryx[kd].at[zz], s1s.at[kd, zz, 5], s1r.at[kd, zz, 5], (xn, z))
    def stage_b(kd, zz):
        n = parts[kd]
        for j in range(2): s1x(kd, zz, j).wait_recv()
        add_into(2 * n, lambda i: half(kd, zz, 2 * (i // n) + x, 0).at[i % n], lambda i: rx[kd].at[zz, i // n, i % n])
        s1xy(kd, zz).start()
        for j in range(2): s1y(kd, zz, j).wait_recv()
        add_into(2 * n, lambda i: half(kd, zz, 2 * y + i // n, 1).at[i % n], lambda i: ry[kd].at[zz, i // n, i % n])
        s1yx(kd, zz).start()
    def stage_c(kd, zz):
        n = parts[kd]
        s1xy(kd, zz).wait_recv()
        add_into(n, lambda i: half(kd, zz, 2 * y + x, 0).at[i], lambda i: rxy[kd].at[zz, i])
        s1yx(kd, zz).wait_recv()
        add_into(n, lambda i: half(kd, zz, 2 * y + x, 1).at[i], lambda i: ryx[kd].at[zz, i])
    def mine(kd, zz): return blk(kd, zz, 2 * y + x)
    def zs(kd, zz, right):
        return rc(mine(kd, zz), (rl if right else rr)[kd].at[zz], s2s.at[kd, zz], s2r.at[kd, zz, 0 if right else 1], (dp, z + 1 if right else z - 1))
    def stage_d(kd, zz, hop):
        n = parts[kd]
        if hop < zz:
            @pl.when(z == hop)
            def _():
                if hop > 0:
                    zs(kd, zz, True).wait_recv()
                    add_into(n, lambda i: mine(kd, zz).at[i], lambda i: rl[kd].at[zz, i])
                zs(kd, zz, True).start()
        if 3 - hop > zz:
            @pl.when(z == 3 - hop)
            def _():
                if hop > 0:
                    zs(kd, zz, False).wait_recv()
                    add_into(n, lambda i: mine(kd, zz).at[i], lambda i: rr[kd].at[zz, i])
                zs(kd, zz, False).start()
        if hop == max(zz, 3 - zz):
            @pl.when(z == zz)
            def _():
                if zz > 0: zs(kd, zz, True).wait_recv()
                if zz < 3: zs(kd, zz, False).wait_recv()
                for i in range(n):
                    t = mine(kd, zz)[i].astype(F32)
                    if zz > 0: t += rl[kd][zz, i].astype(F32)
                    if zz < 3: t += rr[kd][zz, i].astype(F32)
                    if kd:
                        if i < 2: guo[i] = t
                        else: gdo[...] = t
                    else:
                        for j in range(3): gqo[j] = t[:, j * E:j * E + E]
                        gwo[...] = t[:, 3 * E:4 * E]
    order = far_order(z)
    def yb(s): return 4 * s + s // 3
    CHUNKS = ((2, 0), (2, 2), (1, 4))
    def yc(t, src, s, h, right):
        n, off = CHUNKS[h]
        dst = (yout, dxout)[t].at[pl.ds(yb(s) + off, n)]
        src = dst if src is None else src.at[pl.ds(off, n)]
        return rc(src, dst, ys.at[t, s, h, right], yr.at[t, s, h], (dp, z + 1 if right else z - 1))
    def ysend(t, src, s, act, hs=(0, 1, 2)):
        for h in hs:
            for right in (1, 0):
                go = (s <= z) & (z < 3) if right else (s >= z) & (z > 0)
                @pl.when(go & (s == 2) if h == 2 else go)
                def _():
                    getattr(yc(t, src, s, h, right), act)()
    def yarr(t, j, h):
        s = order[j]
        if h == 2:
            @pl.when(s == 2)
            def _():
                yc(t, None, s, h, 1).wait_recv()
        else:
            yc(t, None, s, h, 1).wait_recv()
        ysend(t, None, s, "start", (h,))
    def own(t, hf, way):
        n, off = (4, 0) if hf == 0 else (1, 4)
        if way == 0:
            return pltpu.make_async_copy(yin.at[pl.ds(off, n)], stage.at[pl.ds(off, n)], loc.at[t, hf, 0])
        return pltpu.make_async_copy((stage, dxs)[t].at[pl.ds(off, n)], (yout, dxout)[t].at[pl.ds(yb(z) + off, n)], loc.at[t, hf, 1])
    def ownall(fn):
        fn(0)
        @pl.when(z == 2)
        def _():
            fn(1)
    vpeer = [(dp, z1), (dp, z2), (cn, z), (xn, z), (yn, z)]
    def vcopy(i): return rc(vs.at[i], vr.at[i], vsem_s.at[i], vsem_r.at[i], vpeer[i])
    def vstep(i):
        vcopy(i).wait_recv()
        tot = vs[i] + vr[i]
        if i < 4:
            vs[i + 1] = tot
            vcopy(i + 1).start()
        else:
            vout[...] = tot
    F, T, o = 1, 0, ZO
    def S0(kd, u): stage_0(kd, o[u])
    def A(kd, u): stage_a(kd, o[u])
    def B(kd, u): stage_b(kd, o[u])
    def C(kd, u): stage_c(kd, o[u])
    def Z(kd, u, hop): stage_d(kd, o[u], hop)

    @pl.when(g == 0)
    def _():
        barrier_all([(xn, z), (yn, z), (cn, z)] + [(dp, (z + j) % 4) for j in (1, 2, 3)])
        S0(F, 0)
        ysend(0, yin, z, "start")
        ownall(lambda h: own(0, h, 0).start())
        for j in (1, 2, 3): S0(F, j)
        cg = pltpu.make_async_copy(gs1, acc, sem.at[1]); cg.start()
        load_rows(z, xl, xs, xb, sem.at[0])
        distances(z, slen, llen, dm)
        xt[...] = xb[...].reshape(R, D).T
        gbs[...] = jnp.zeros_like(gbs)
        cg.wait()
        ga[...] = acc[...].astype(BF16)
        gat[...] = ga[...].T
        ownall(lambda h: (own(0, h, 0).wait(), own(0, h, 1).start()))
        yarr(0, 2, 2)
    wz, sm = w.at[0, 0], small.at[0]
    gc[...] = nt(ga[...], wz[576:768, :]).astype(BF16)
    kt[...] = k[0].T
    @pl.when(g == 2)
    def _():
        yarr(0, 2, 0)
    @pl.when(g == 3)
    def _():
        yarr(0, 2, 1)
    def hook(i):
        def on(n, j, fn):
            @pl.when((g == n) & (i == j))
            def _(): fn()
        on(0, 0, lambda: A(F, 0))
        on(0, 1, lambda: yarr(0, 0, 0))
        on(0, 3, lambda: A(F, 1))
        on(1, 0, lambda: yarr(0, 0, 1))
        on(1, 2, lambda: yarr(0, 1, 1))
        on(1, 3, lambda: B(F, 0))
        on(2, 2, lambda: (A(T, 0), C(F, 0), Z(F, 0, 0)))
    attend_bwd(z, sm, q8.at[0], k.at[0], v.at[0], kt, gc, dm, lse.at[0], gqt, gk, gv, hook)
    @pl.when(g == 0)
    def _():
        yarr(0, 1, 0)
    zg = zo(g)
    dq = gqt[...].astype(BF16).T
    dk = gk[...].astype(BF16)
    dv = gv[...].astype(BF16)
    gbs[zg, 0:1, 0:192] = jnp.sum(dq.astype(F32), axis=0, keepdims=True)
    gbs[zg, 1:2, 0:192] = jnp.sum(dv.astype(F32), axis=0, keepdims=True)
    acc[...] += nn(dq, wz[0:192, :]) + nn(dk, wz[192:384, :]) + nn(dv, wz[384:576, :])
    def X():
        for i in range(5):
            dxs[i] = acc[128 * i:128 * i + 128, :].astype(BF16)
        vs[0] = vin[...]
        for i in range(4):
            vs[0, 6 + 2 * i:8 + 2 * i, 0:192] = gbs[i, 0:2, 0:192]
        vcopy(0).start()
        ysend(1, dxs, z, "start")
        ownall(lambda h: own(1, h, 1).start())
    @pl.when(g == 1)
    def _():
        yarr(1, 2, 2)
    @pl.when(g == 2)
    def _():
        C(F, 1); Z(F, 1, 0); yarr(0, 1, 2); A(F, 2)
    @pl.when(g == 3)
    def _():
        X(); B(F, 2); A(T, 1)
    for i in range(6):
        rw = slice(128 * i, 128 * i + 128)
        gob[zg, 0, rw, :] = jnp.concatenate([nn(xt[rw, :], dq), nn(xt[rw, :], dk), nn(xt[rw, :], dv), nn(gat[rw, :], ctx[0])], axis=1).astype(BF16)
    @pl.when(g == 0)
    def _():
        S0(T, 0)
    @pl.when(g == 1)
    def _():
        B(F, 1); S0(T, 1)
    @pl.when(g == 2)
    def _():
        S0(T, 2)
    @pl.when(g == 3)
    def _():
        A(F, 3); C(F, 2); Z(F, 1, 1); S0(T, 3); Z(F, 2, 0); Z(F, 0, 1); vstep(0); B(T, 1); B(T, 0)
        yarr(1, 1, 1); B(F, 3); A(T, 2); A(T, 3); C(T, 1); C(T, 0); Z(T, 0, 0); Z(T, 1, 0); yarr(1, 0, 0)
        yarr(1, 0, 2); yarr(1, 1, 0); C(F, 3); Z(F, 0, 2); Z(F, 1, 2); yarr(0, 0, 2); yarr(1, 0, 1); Z(F, 3, 0); vstep(1)
        B(T, 2); yarr(1, 1, 2); C(T, 2); Z(F, 0, 3); Z(T, 2, 0); Z(T, 1, 1); B(T, 3); C(T, 3); vstep(2)
        Z(F, 1, 3); yarr(1, 2, 1); Z(F, 3, 1); Z(T, 0, 1); Z(T, 3, 0); vstep(3); Z(T, 0, 2); Z(T, 0, 3); Z(T, 1, 2)
        Z(T, 1, 3); Z(F, 2, 1); yarr(1, 2, 0); Z(T, 2, 1); Z(F, 3, 2); Z(F, 2, 2); vstep(4); Z(T, 2, 2); Z(T, 3, 2)
        Z(T, 3, 1)
        for kd in (0, 1):
            for zz in ZO:
                for q in range(4): st0(kd, zz, q).wait_send()
                for j in range(2):
                    s1x(kd, zz, j).wait_send(); s1y(kd, zz, j).wait_send()
                s1xy(kd, zz).wait_send(); s1yx(kd, zz).wait_send()
                @pl.when(z < zz)
                def _(): zs(kd, zz, True).wait_send()
                @pl.when(z > zz)
                def _(): zs(kd, zz, False).wait_send()
        for t, src in enumerate((yin, dxs)):
            ysend(t, src, z, "wait_send")
            for j in range(3):
                ysend(t, None, order[j], "wait_send")
            ownall(lambda h: own(t, h, 1).wait())
        for i in range(5): vcopy(i).wait_send()

def run_kx(slen, llen, xl, xs, W, small, q8, k, v, ctx, lse, gs1, g3, yv, vec):
    pz = lambda *s: pl.BlockSpec((1,) + s, lambda g, *_: (zo(g),) + (0,) * len(s))
    rz = lambda: pz(R, E)
    V, S = pltpu.VMEM, pltpu.SemaphoreType.DMA
    b = lambda *s: V(s + (PR, D), BF16)
    h = lambda *s: V(s + (H, D), BF16)
    bufs = lambda n: [b(4, 4, n), h(4, 2, n), h(4, 2, n), h(4, n), h(4, n), b(4, n), b(4, n)]
    scratch = [V((5, 128, D), BF16), V((5, 512, 128), F32), V((E, R), BF16), V((R, E), BF16), V((E, R), F32), V((R, E), F32), V((R, E), F32),
               V((R, D), BF16), V((D, R), BF16), V((D, R), BF16), V((R, D), F32), V((4, 1, D, D), BF16), V((5, 128, D), BF16), V((4, 8, 256), F32),
               V((5, 128, D), BF16), V((5, 16, D), F32), V((5, 16, D), F32), b(4, 4, 3)] + bufs(3) + bufs(1) + [
               S((2,)), S((2, 4, 4)), S((2, 4, 4)), S((4, 4)), S((2, 4, 6)), S((2, 4, 6)), S((2, 4)), S((2, 4, 2)), S((2, 4, 3, 2)), S((2, 4, 3)), S((5,)), S((5,)), S((2, 2, 2))]
    return pl.pallas_call(
        kx,
        grid_spec=pltpu.PrefetchScalarGridSpec(num_scalar_prefetch=2, grid=(4,),
            in_specs=[ANY, ANY, pl.BlockSpec((1, 1, D, D), lambda g, *_: (zo(g), 0, 0, 0)), pz(8, 256), rz(), rz(), rz(), rz(), pz(8, R), ANY, ANY, ANY, const((16, D))],
            out_specs=[const((3, PR, E)), const((PR, E)), const((2, PR, D)), const((PR, D)), ANY, ANY, const((16, D))], scratch_shapes=scratch),
        out_shape=[sds((3, PR, E), F32), sds((PR, E), F32), sds((2, PR, D), F32), sds((PR, D), F32), sds((17, 128, D), BF16), sds((17, 128, D), BF16), sds((16, D), F32)],
        compiler_params=pltpu.CompilerParams(dimension_semantics=("arbitrary",), collective_id=1, has_side_effects=True, vmem_limit_bytes=VM),
        name="attention_backward_send")(slen, llen, xl, xs, W, small, q8, k, v, ctx, lse, gs1, g3, yv, vec)

def alibi_slopes(slope_index, head_total):
    power = 1 << head_total.bit_length() - 1
    f = slope_index.astype(F32)
    return jnp.where(slope_index < power, jnp.exp2(-8.0 * (f + 1.0) / power), jnp.exp2(-4.0 * (2.0 * (f - power) + 1.0) / power))
def prep(slope_index, w_qkv, b_qv, w_out, w_up, w_down):
    a = jnp.concatenate([jnp.transpose(w_qkv, (1, 2, 0)).reshape(576, D), w_out.T], 0)
    own = jnp.stack([a, w_up[:, 0], w_up[:, 1], w_down], 0)
    bt = jnp.transpose(b_qv, (1, 2, 0)).reshape(2, 192)
    sl = jnp.pad(alibi_slopes(slope_index, 12)[None], ((0, 0), (0, 189)))
    small = jnp.pad(jnp.concatenate([bt, sl], 0), ((0, 5), (0, 64)))
    return own, small
def per_device(x_short, x_long, short_lengths, long_lengths, slope_index, w_qkv, b_qv, w_out, b_out, gain1, bias1, w_up, w_down, b_down, gain2, bias2, cot_short, cot_long):
    own, small = prep(slope_index, w_qkv, b_qv, w_out, w_up, w_down)
    row = lax.broadcasted_iota(jnp.int32, (8, D), 0)
    vec = jnp.broadcast_to(bias2[None], (8, D))
    for i, t in enumerate((b_out, gain1, bias1, b_down, gain2)):
        vec = jnp.where(row == i, t[None], vec)
    xl, cl = x_long.reshape(8, 128, D), cot_long.reshape(8, 128, D)
    W, S, q8, k, v, ctx, lse, n1, r1, hl, a, b, inner, y, gf, gs2, vg2 = run_kg(short_lengths, long_lengths, own, small, xl, x_short, cl, cot_short, vec)
    go3, gs1, vg1 = run_kc(W, a, b, inner, gf, hl, gs2, n1, r1, vec)
    m, dpx = lax.axis_index("mp"), lax.axis_index("dp")
    vsum = jnp.concatenate([vg2[:3], vg1[:3], jnp.zeros((10, D), F32)], 0)
    gq, gwo, gup, gdn, Y, DX, vs = run_kx(short_lengths, long_lengths, xl, x_short, W, S, q8, k, v, ctx, lse, gs1, go3, y.reshape(5, 128, D), vsum)
    b = lax.dynamic_slice(vs[6:14, :192].reshape(4, 2, 3, 64), (m, 0, 0, 8 * dpx), (1, 2, 3, 8))[0]
    vs = lax.dynamic_slice(vs[:6], (0, 96 * dpx), (6, 96))
    return (Y[8:], Y[:8].reshape(2, 512, D), DX[8:], DX[:8].reshape(2, 512, D), jnp.transpose(gq, (1, 0, 2)), jnp.transpose(b, (2, 0, 1)), gwo, vs[5], vs[3], vs[4], jnp.transpose(gup, (1, 0, 2)), gdn, vs[2], vs[0], vs[1])
def per_device_any(x_short, x_long, short_lengths, long_lengths, slope_index, w_qkv, b_qv, w_out, b_out, gain1, bias1, w_up, w_down, b_down, gain2, bias2, cot_short, cot_long):
    own, small = prep(slope_index, w_qkv, b_qv, w_out, w_up, w_down)
    W = lax.all_gather(own, "mp"); S = lax.all_gather(small, "mp")
    vec = jnp.stack([b_out, gain1, bias1, b_down, gain2, bias2, bias2, bias2], 0)
    xl, cl = x_long.reshape(8, 128, D), cot_long.reshape(8, 128, D)
    q8, k, v, ctx, lse, n1, r1, hl = run_ka(short_lengths, long_lengths, xl, x_short, W, S, vec)
    a, b, inner, y, gf, gs2, vg2 = run_kb(cl, cot_short, W, hl, n1, vec)
    go3, gs1, vg1 = run_kc(W, a, b, inner, gf, hl, gs2, n1, r1, vec)
    go1, dx, gb = run_kd(short_lengths, long_lengths, xl, x_short, W, S, q8, k, v, ctx, lse, gs1.astype(BF16), gs1)
    m = lax.axis_index("mp")
    def spread(r):
        g = lax.all_gather(r, "mp")
        return jnp.concatenate([g[2], g[3][:512]], 0).reshape(9, 128, D), jnp.stack([g[0][:512], g[1][:512]], 0)
    ys, yl = spread(y); ds, dl = spread(dx)
    G = jnp.concatenate([go1, go3], 1).astype(F32)
    G = lax.psum_scatter(G, "mp", scatter_dimension=0, tiled=True)[0]
    G = lax.psum_scatter(G, "dp", scatter_dimension=1, tiled=True)
    vs = lax.psum(jnp.concatenate([vg2[:3], vg1[:3]], 0), "mp")
    vs = lax.psum_scatter(vs, "dp", scatter_dimension=1, tiled=True)
    gb = lax.psum_scatter(gb[:, :2, :192], "mp", scatter_dimension=0, tiled=True)[0]
    gb = jnp.transpose(gb.reshape(2, 3, 64), (2, 0, 1))
    gb = lax.psum_scatter(gb, "dp", scatter_dimension=0, tiled=True)
    gq = jnp.transpose(G[0][:, :576].reshape(-1, 3, 192), (0, 1, 2))
    return (ys, yl, ds, dl, gq, gb, G[0][:, 576:], vs[5], vs[3], vs[4], jnp.stack([G[1], G[2]], 1), G[3], vs[2], vs[0], vs[1])
def solution(mesh):
    fn = per_device if mesh.shape["dp"] == 8 else per_device_any
    d3 = P("dp", None, None)
    return jax.shard_map(fn, mesh=mesh,
        in_specs=(d3, d3, P("dp"), P("dp"), P("mp"), P(None, None, "mp"), P(None, None, "mp"), P(None, "mp"), P(), P(), P(), P(None, None, "mp"), P(None, "mp"), P(), P(), P(), d3, d3),
        out_specs=(d3, d3, d3, d3, P("dp", None, "mp"), P("dp", None, "mp"), P("dp", "mp"), P("dp"), P("dp"), P("dp"), P("dp", None, "mp"), P("dp", "mp"), P("dp"), P("dp"), P("dp")),
        check_vma=False)
```

```python
import functools
import math

import jax
import jax.numpy as jnp
from jax import lax
from jax.experimental import pallas as pl
from jax.experimental.pallas import tpu as pltpu
from jax.sharding import PartitionSpec as P

F32, BF16 = jnp.float32, jnp.bfloat16
R, D, E = 640, 768, 192
FAR = 1e30
VM = 60 << 20

def nn(a, b): return lax.dot_general(a, b, (((1,), (0,)), ((), ())), preferred_element_type=F32)
def nt(a, b): return lax.dot_general(a, b, (((1,), (1,)), ((), ())), preferred_element_type=F32)

def load_rows(m, long_ref, short_ref, buf, sem):
    @pl.when(m < 2)
    def _():
        c = pltpu.make_async_copy(long_ref.at[pl.ds(4 * m, 4)], buf.at[pl.ds(0, 4)], sem); c.start(); c.wait()
        buf[4] = jnp.zeros((128, D), BF16)
    @pl.when(m == 2)
    def _():
        c = pltpu.make_async_copy(short_ref.at[pl.ds(0, 5)], buf, sem); c.start(); c.wait()
    @pl.when(m == 3)
    def _():
        c = pltpu.make_async_copy(short_ref.at[pl.ds(5, 4)], buf.at[pl.ds(0, 4)], sem); c.start(); c.wait()
        buf[4] = jnp.zeros((128, D), BF16)

def distances(m, slen, llen, dm):
    @pl.when(m < 2)
    def _():
        n = llen[jnp.minimum(m, 1)]
        key = lax.broadcasted_iota(jnp.int32, (512, 128), 0)
        qry = lax.broadcasted_iota(jnp.int32, (512, 128), 1)
        for i in range(4):
            dist = jnp.abs(key - (qry + 128 * i)).astype(F32)
            dm[i] = jnp.where(key < n, dist, FAR)
    @pl.when(m >= 2)
    def _():
        key = lax.broadcasted_iota(jnp.int32, (128, 128), 0)
        qry = lax.broadcasted_iota(jnp.int32, (128, 128), 1)
        dist = jnp.abs(key - qry).astype(F32)
        for i in range(5):
            n = slen[jnp.minimum(5 * (m - 2) + i, 8)] if i == 4 else slen[jnp.maximum(5 * (m - 2), 0) + i]
            dm[i, 0:128, :] = jnp.where(key < n, dist, FAR)

def head_lanes(j):
    return lax.broadcasted_iota(jnp.int32, (1, E), 1) // 64 == j
def head_rows(j):
    return lax.broadcasted_iota(jnp.int32, (E, 1), 0) // 64 == j

def attend_fwd(m, small, q8, k, vt, dm, ct, lse, hook=lambda i: None):
    def block(i, keys, koff):
        cols = pl.ds(pl.multiple_of(i * 128, 128), 128)
        qi = q8[cols, :]
        kk = k[pl.ds(koff, keys), :]
        vv = vt[:, pl.ds(koff, keys)]
        d = dm[i, 0:keys, :]
        out = jnp.zeros((E, 128), F32)
        for j in range(3):
            s = nt(kk, jnp.where(head_lanes(j), qi, jnp.zeros_like(qi))) - small[2:3, j:j + 1] * d
            mx = jnp.max(s, axis=0, keepdims=True)
            ex = jnp.exp(s - mx)
            tot = jnp.sum(ex, axis=0, keepdims=True)
            p = (ex * (1.0 / tot)).astype(BF16)
            out = jnp.where(head_rows(j), nn(vv, p), out)
            lse[j:j + 1, cols] = mx + jnp.log(tot)
        ct[:, cols] = out.astype(BF16)
    @pl.when(m < 2)
    def _():
        lax.fori_loop(0, 4, lambda i, u: (block(i, 512, 0), hook(i), u)[2], 0)
    @pl.when(m >= 2)
    def _():
        lax.fori_loop(0, 5, lambda i, u: (block(i, 128, pl.multiple_of(i * 128, 128)), hook(i), u)[2], 0)

def attend_bwd(m, small, q8, k, v, kt, gc, dm, lse, gqt, gk, gv, hook=lambda i: None):
    gk[...] = jnp.zeros_like(gk)
    gv[...] = jnp.zeros_like(gv)
    def block(i, keys, koff):
        cols = pl.ds(pl.multiple_of(i * 128, 128), 128)
        rows = pl.ds(koff, keys)
        qi, gi = q8[cols, :], gc[cols, :]
        kk, vv, ktt = k[rows, :], v[rows, :], kt[:, rows]
        d = dm[i, 0:keys, :]
        oq = jnp.zeros((E, 128), F32)
        ok = jnp.zeros((keys, E), F32)
        ov = jnp.zeros((keys, E), F32)
        for j in range(3):
            hl = head_lanes(j)
            qj = jnp.where(hl, qi, jnp.zeros_like(qi))
            gj = jnp.where(hl, gi, jnp.zeros_like(gi))
            s = nt(kk, qj) - small[2:3, j:j + 1] * d
            p = jnp.exp(s - lse[j:j + 1, cols])
            gp = nt(vv, gj)
            ov = ov + nn(p.astype(BF16), gj)
            row = jnp.sum(p * gp, axis=0, keepdims=True)
            ds = (p * (gp - row)).astype(BF16)
            oq = jnp.where(head_rows(j), nn(ktt, ds), oq)
            ok = ok + nn(ds, qj)
        gqt[:, cols] = oq * 0.125
        gk[rows, :] += ok
        gv[rows, :] += ov
    @pl.when(m < 2)
    def _():
        lax.fori_loop(0, 4, lambda i, u: (block(i, 512, 0), hook(i), u)[2], 0)
        gqt[:, 512:640] = jnp.zeros((E, 128), F32)
    @pl.when(m >= 2)
    def _():
        lax.fori_loop(0, 5, lambda i, u: (block(i, 128, pl.multiple_of(i * 128, 128)), hook(i), u)[2], 0)

def norm_fwd(s):
    mean = jnp.mean(s, axis=1, keepdims=True)
    c = s - mean
    r = lax.rsqrt(jnp.mean(c * c, axis=1, keepdims=True) + 1e-12)
    return c * r, r

def norm_bwd(gn, normed, r):
    return r * (gn - jnp.mean(gn, axis=1, keepdims=True) - normed * jnp.mean(gn * normed, axis=1, keepdims=True))

def row_tiles(fn, tile=640):
    def body(i, u):
        fn(pl.ds(pl.multiple_of(i * tile, tile), tile)); return u
    lax.fori_loop(0, R // tile, body, 0)

def ka(slen, llen, xl, xs, w, small, vec, q8o, ko, vo, co, lseo, n1o, r1o, hlo, xb, dm, vt, ct, acc, sem):
    z = pl.program_id(0)
    m = lax.axis_index("mp")
    @pl.when(z == 0)
    def _():
        load_rows(m, xl, xs, xb, sem)
        distances(m, slen, llen, dm)
        ct[...] = jnp.zeros_like(ct)
        lseo[...] = jnp.zeros_like(lseo)
        acc[...] = jnp.zeros_like(acc)
    x = xb[...].reshape(R, D)
    wz, sm = w.at[0, 0], small.at[0]
    q8o[0] = ((nt(x, wz[0:192, :]) + sm[0:1, 0:192]).astype(BF16).astype(F32) * 0.125).astype(BF16)
    ko[0] = nt(x, wz[192:384, :]).astype(BF16)
    v = (nt(x, wz[384:576, :]) + sm[1:2, 0:192]).astype(BF16)
    vo[0] = v
    vt[...] = v.T
    attend_fwd(m, sm, q8o.at[0], ko.at[0], vt, dm, ct, lseo.at[0])
    co[0] = ct[...].T
    acc[...] += nn(co[0], wz[576:768, :]).astype(BF16).astype(F32)
    @pl.when(z == 3)
    def _():
        for i in range(5):
            rows = slice(128 * i, 128 * i + 128)
            s = xb[i].astype(F32) + acc[rows, :] + vec[0:1, :]
            n, r = norm_fwd(s)
            n1o[rows, :] = n
            r1o[rows, :] = jnp.broadcast_to(r, (128, 128))
            hlo[rows, :] = (n * vec[1:2, :] + vec[2:3, :]).astype(BF16)

def const(shape): return pl.BlockSpec(shape, lambda z, *_: (0,) * len(shape))
def perz(shape): return pl.BlockSpec((1,) + shape, lambda z, *_: (z,) + (0,) * len(shape))
ANY = pl.BlockSpec(memory_space=pl.ANY)
def sds(shape, dt): return jax.ShapeDtypeStruct(shape, dt)
def part(p): return pl.BlockSpec((1, 1, D, D), lambda z, *_: (z, p, 0, 0))

def call(kernel, in_specs, outs, scratch, name, args, grid=(4,), prefetch=2):
    return pl.pallas_call(
        kernel,
        grid_spec=pltpu.PrefetchScalarGridSpec(num_scalar_prefetch=prefetch, grid=grid, in_specs=in_specs,
            out_specs=[o[0] for o in outs], scratch_shapes=scratch),
        out_shape=[o[1] for o in outs],
        compiler_params=pltpu.CompilerParams(dimension_semantics=("arbitrary",), vmem_limit_bytes=VM),
        name=name)(*args)

def run_ka(slen, llen, xl, xs, W, small, vec):
    rz = lambda: (perz((R, E)), sds((4, R, E), BF16))
    return call(ka, [ANY, ANY, part(0), perz((8, 256)), const((8, D))],
        [rz(), rz(), rz(), rz(), (perz((8, R)), sds((4, 8, R), F32)), (const((R, D)), sds((R, D), F32)), (const((R, 128)), sds((R, 128), F32)), (const((R, D)), sds((R, D), BF16))],
        [pltpu.VMEM((5, 128, D), BF16), pltpu.VMEM((5, 512, 128), F32), pltpu.VMEM((E, R), BF16), pltpu.VMEM((E, R), BF16), pltpu.VMEM((R, D), F32), pltpu.SemaphoreType.DMA],
        "attention_forward", (slen, llen, xl, xs, W, small, vec))

def gelu_parts(g):
    cdf = 0.5 * (1.0 + lax.erf(g * (2.0 ** -0.5)))
    pdf = jnp.exp(-0.5 * g * g) * (1.0 / math.sqrt(2 * math.pi))
    return g * cdf, cdf + g * pdf

def kb(cl, cs, wg, wu, wd, hl, n1, vec, ao, bo, io, yo, gfo, gs2o, vgo, acc, cb, sem):
    z = pl.program_id(0)
    m = lax.axis_index("mp")
    @pl.when(z == 0)
    def _():
        load_rows(m, cl, cs, cb, sem)
        acc[...] = jnp.zeros_like(acc)
    def tile(rows):
        h = hl[rows, :]
        gate = nn(h, wg[0, 0])
        up = nn(h, wu[0, 0])
        a, slope = gelu_parts(gate)
        ao[0, rows, :] = a
        bo[0, rows, :] = up * slope
        inner = (a * up).astype(BF16)
        io[0, rows, :] = inner
        acc[rows, :] += nt(inner, wd[0, 0]).astype(BF16).astype(F32)
    row_tiles(tile)
    @pl.when(z == 3)
    def _():
        tot = [jnp.zeros((1, D), F32)] * 3
        for i in range(5):
            rows = slice(128 * i, 128 * i + 128)
            h1 = n1[rows, :] * vec[1:2, :] + vec[2:3, :]
            n, r = norm_fwd(h1 + acc[rows, :] + vec[3:4, :])
            yo[rows, :] = (n * vec[4:5, :] + vec[5:6, :]).astype(BF16)
            gy = cb[i].astype(F32)
            gs = norm_bwd(gy * vec[4:5, :], n, r)
            gs2o[rows, :] = gs
            gfo[rows, :] = gs.astype(BF16)
            tot = [tot[0] + jnp.sum(gy * n, axis=0, keepdims=True), tot[1] + jnp.sum(gy, axis=0, keepdims=True), tot[2] + jnp.sum(gs, axis=0, keepdims=True)]
        vgo[...] = jnp.concatenate(tot + [jnp.zeros((5, D), F32)], axis=0)

def run_kb(cl, cs, W, hl, n1, vec):
    z32 = lambda: (perz((R, D)), sds((4, R, D), F32))
    return call(kb, [ANY, ANY, part(1), part(2), part(3), const((R, D)), const((R, D)), const((8, D))],
        [z32(), z32(), (perz((R, D)), sds((4, R, D), BF16)), (const((R, D)), sds((R, D), BF16)), (const((R, D)), sds((R, D), BF16)), (const((R, D)), sds((R, D), F32)), (const((8, D)), sds((8, D), F32))],
        [pltpu.VMEM((R, D), F32), pltpu.VMEM((5, 128, D), BF16), pltpu.SemaphoreType.DMA],
        "feed_forward", (cl, cs, W, W, W, hl, n1, vec), prefetch=0)

def kc(wg, wu, wd, a, b, inner, gf, hl, gs2, n1, r1, vec, go, gs1o, vgo, acc, gft, hlt, gg):
    z = pl.program_id(0)
    @pl.when(z == 0)
    def _():
        acc[...] = gs2[...]
        gft[...] = gf[...].T
        hlt[...] = hl[...].T
    def tile(rows):
        gi = nn(gf[rows, :], wd[0, 0])
        g1 = (gi * b[0, rows, :]).astype(BF16)
        g2 = (gi * a[0, rows, :]).astype(BF16)
        gg[0, rows, :] = g1
        gg[1, rows, :] = g2
        acc[rows, :] += nt(g1, wg[0, 0]) + nt(g2, wu[0, 0])
    row_tiles(tile)
    def wtile(rows):
        go[0, 2, rows, :] = nn(gft[rows, :], inner[0]).astype(BF16)
        go[0, 0, rows, :] = nn(hlt[rows, :], gg[0]).astype(BF16)
        go[0, 1, rows, :] = nn(hlt[rows, :], gg[1]).astype(BF16)
    wtile(slice(0, D))
    @pl.when(z == 3)
    def _():
        tot = [jnp.zeros((1, D), F32)] * 3
        for i in range(5):
            rows = slice(128 * i, 128 * i + 128)
            gh, n = acc[rows, :], n1[rows, :]
            gs = norm_bwd(gh * vec[1:2, :], n, r1[rows, 0:1])
            gs1o[rows, :] = gs
            tot = [tot[0] + jnp.sum(gh * n, axis=0, keepdims=True), tot[1] + jnp.sum(gh, axis=0, keepdims=True), tot[2] + jnp.sum(gs, axis=0, keepdims=True)]
        vgo[...] = jnp.concatenate(tot + [jnp.zeros((5, D), F32)], axis=0)

def run_kc(W, a, b, inner, gf, hl, gs2, n1, r1, vec):
    c = lambda dt: const((R, D))
    return call(kc, [part(1), part(2), part(3), perz((R, D)), perz((R, D)), perz((R, D)), c(0), c(0), c(0), c(0), const((R, 128)), const((8, D))],
        [(pl.BlockSpec((1, 3, D, D), lambda z: (z, 0, 0, 0)), sds((4, 3, D, D), BF16)), (const((R, D)), sds((R, D), F32)), (const((8, D)), sds((8, D), F32))],
        [pltpu.VMEM((R, D), F32), pltpu.VMEM((D, R), BF16), pltpu.VMEM((D, R), BF16), pltpu.VMEM((2, R, D), BF16)],
        "feed_backward", (W, W, W, a, b, inner, gf, hl, gs2, n1, r1, vec), prefetch=0)

def kd(slen, llen, xl, xs, w, small, q8, k, v, ctx, lse, ga, gs1, go, dxo, gbo, xb, dm, kt, gc, gqt, gk, gv, gat, xt, acc, sem):
    z = pl.program_id(0)
    m = lax.axis_index("mp")
    @pl.when(z == 0)
    def _():
        load_rows(m, xl, xs, xb, sem)
        distances(m, slen, llen, dm)
        acc[...] = gs1[...]
        gat[...] = ga[...].T
        xt[...] = xb[...].reshape(R, D).T
        gbo[...] = jnp.zeros_like(gbo)
    wz, sm = w.at[0, 0], small.at[0]
    gc[...] = nt(ga[...], wz[576:768, :]).astype(BF16)
    kt[...] = k[0].T
    attend_bwd(m, sm, q8.at[0], k.at[0], v.at[0], kt, gc, dm, lse.at[0], gqt, gk, gv)
    dq = gqt[...].astype(BF16).T
    dk = gk[...].astype(BF16)
    dv = gv[...].astype(BF16)
    gbo[z, 0:1, 0:192] = jnp.sum(dq.astype(F32), axis=0, keepdims=True)
    gbo[z, 1:2, 0:192] = jnp.sum(dv.astype(F32), axis=0, keepdims=True)
    acc[...] += nn(dq, wz[0:192, :]) + nn(dk, wz[192:384, :]) + nn(dv, wz[384:576, :])
    def wtile(rows):
        xr = xt[rows, :]
        go[0, 0, rows, :] = jnp.concatenate([nn(xr, dq), nn(xr, dk), nn(xr, dv), nn(gat[rows, :], ctx[0])], axis=1).astype(BF16)
    for i in range(6):
        wtile(slice(128 * i, 128 * i + 128))
    @pl.when(z == 3)
    def _():
        dxo[...] = acc[...].astype(BF16)

def run_kd(slen, llen, xl, xs, W, small, q8, k, v, ctx, lse, ga, gs1):
    rz = lambda: perz((R, E))
    rd = const((R, D))
    return call(kd, [ANY, ANY, part(0), perz((8, 256)), rz(), rz(), rz(), rz(), perz((8, R)), rd, rd],
        [(pl.BlockSpec((1, 1, D, D), lambda z, *_: (z, 0, 0, 0)), sds((4, 1, D, D), BF16)), (rd, sds((R, D), BF16)), (const((4, 8, 256)), sds((4, 8, 256), F32))],
        [pltpu.VMEM((5, 128, D), BF16), pltpu.VMEM((5, 512, 128), F32), pltpu.VMEM((E, R), BF16), pltpu.VMEM((R, E), BF16), pltpu.VMEM((E, R), F32), pltpu.VMEM((R, E), F32), pltpu.VMEM((R, E), F32),
         pltpu.VMEM((D, R), BF16), pltpu.VMEM((D, R), BF16), pltpu.VMEM((R, D), F32), pltpu.SemaphoreType.DMA],
        "attention_backward", (slen, llen, xl, xs, W, small, q8, k, v, ctx, lse, ga, gs1))

MESH = pl.DeviceIdType.MESH
PR = 96

def place():
    dp = lax.axis_index("dp"); z = lax.axis_index("mp")
    return dp, dp // 4, (dp // 2) % 2, dp % 2, z

def dpi(y, x, c):
    return (y * 2 + x) * 2 + c

def barrier_all(peers):
    b = pltpu.get_barrier_semaphore()
    for d in peers:
        pl.semaphore_signal(b, inc=1, device_id=d, device_id_type=MESH)
    pl.semaphore_wait(b, len(peers))

def kg(slen, llen, own, small, xl, xs, cl, cs, vec, out, sout, q8o, ko, vo, co, lseo, n1o, r1o, hlo, ao, bo, io, yo, gfo, gs2o, vgo,
       ssm, xb, dm, vt, ct, acc, wz, wf, ab, bb, ib, recv, send, loc, ss, sr, sem, lsem, osem):
    g = pl.program_id(0)
    dp, y, x, c, z = place()
    xn, yn, cn = dpi(y, 1 - x, c), dpi(1 - y, x, c), dpi(y, x, 1 - c)
    dn = dpi(1 - y, 1 - x, c)
    def sm(j): return pltpu.make_async_remote_copy(src_ref=small, dst_ref=ssm.at[z], send_sem=ss.at[j], recv_sem=sr.at[z], device_id=(dp, (z + 1 + j) % 4), device_id_type=MESH)
    e = 1 - ((z + 1) // 2) % 2
    srcs = [z + 1 - 2 * (z % 2), e * ((z + 2) % 4) + (1 - e) * (3 - z), e * (3 - z) + (1 - e) * ((z + 2) % 4)]

    def rows(p, h):
        if h is None:
            return pl.ds(pl.multiple_of(p * PR, 32), PR)
        return pl.ds(pl.multiple_of(p * PR + h * (PR // 2), 16), PR // 2)
    def piece(s, g, p, h=None):
        return out.at[s, g, rows(p, h), :]
    def opiece(g, p):
        return own.at[g, rows(p, None), :]
    def cp(src, dst, s, g, k, r, dev):
        return pltpu.make_async_remote_copy(src_ref=src, dst_ref=dst, send_sem=send.at[s, g, k], recv_sem=recv.at[s, g, r], device_id=dev, device_id_type=MESH)
    def zsend(src, s, g):
        @pl.when((s <= z) & (z < 3))
        def _():
            cp(src, piece(s, g, dp), s, g, 0, 0, (dp, z + 1)).start()
        @pl.when((s >= z) & (z > 0))
        def _():
            cp(src, piece(s, g, dp), s, g, 1, 0, (dp, z - 1)).start()
    def zsend_wait(src, s, g):
        @pl.when((s <= z) & (z < 3))
        def _():
            cp(src, piece(s, g, dp), s, g, 0, 0, (dp, z + 1)).wait_send()
        @pl.when((s >= z) & (z > 0))
        def _():
            cp(src, piece(s, g, dp), s, g, 1, 0, (dp, z - 1)).wait_send()
    def simple(s, g):
        me, xp, yp, dg = dp, xn, yn, dn
        return dict(
            x=lambda: cp(piece(s, g, me), piece(s, g, me), s, g, 2, 1, (xn, z)),
            y=lambda: cp(piece(s, g, me), piece(s, g, me), s, g, 3, 2, (yn, z)),
            c=lambda: cp(piece(s, g, me), piece(s, g, me), s, g, 4, 3, (cn, z)),
            cx=lambda: cp(piece(s, g, xp), piece(s, g, xp), s, g, 5, 4, (cn, z)),
            cy=lambda: cp(piece(s, g, yp), piece(s, g, yp), s, g, 6, 5, (cn, z)),
            yf=lambda: cp(piece(s, g, xp, 0), piece(s, g, xp, 0), s, g, 7, 6, (yn, z)),
            xf=lambda: cp(piece(s, g, yp, 1), piece(s, g, yp, 1), s, g, 8, 7, (xn, z)),
            cd0=lambda: cp(piece(s, g, dg, 0), piece(s, g, dg, 0), s, g, 9, 8, (cn, z)),
            cd1=lambda: cp(piece(s, g, dg, 1), piece(s, g, dg, 1), s, g, 10, 9, (cn, z)),
        )
    def wrecv(ref, s, g, r):
        pltpu.make_async_remote_copy(src_ref=ref, dst_ref=ref, send_sem=send.at[s, g, 0], recv_sem=recv.at[s, g, r], device_id=(cn, z), device_id_type=MESH).wait_recv()
    def zarr(j, g):
        s = srcs[j]
        wrecv(piece(s, g, dp), s, g, 0)
        zsend(piece(s, g, dp), s, g)
        m = simple(s, g)
        m["x"]().start(); m["y"]().start(); m["c"]().start()
    def xyarr(j, g):
        s = srcs[j]; m = simple(s, g)
        wrecv(piece(s, g, xn), s, g, 1)
        m["yf"]().start(); m["cx"]().start()
        wrecv(piece(s, g, yn), s, g, 2)
        m["xf"]().start(); m["cy"]().start()
    def diag(j, g):
        s = srcs[j]; m = simple(s, g)
        wrecv(piece(s, g, dn, 0), s, g, 6)
        m["cd0"]().start()
        wrecv(piece(s, g, dn, 1), s, g, 7)
        m["cd1"]().start()
    def landed(j, g):
        s = srcs[j]
        cdx, cdy, cdd = dpi(y, 1 - x, 1 - c), dpi(1 - y, x, 1 - c), dpi(1 - y, 1 - x, 1 - c)
        wrecv(piece(s, g, cn), s, g, 3)
        wrecv(piece(s, g, cdx), s, g, 4)
        wrecv(piece(s, g, cdy), s, g, 5)
        wrecv(piece(s, g, cdd, 0), s, g, 8)
        wrecv(piece(s, g, cdd, 1), s, g, 9)
    def sent(j, g):
        s = srcs[j]; m = simple(s, g)
        zsend_wait(piece(s, g, dp), s, g)
        for k in ("x", "y", "c", "cx", "cy", "yf", "xf", "cd0", "cd1"):
            m[k]().wait_send()
    l0 = pltpu.make_async_copy(wz, out.at[z, 0], loc.at[0])
    l1 = pltpu.make_async_copy(own.at[pl.ds(1, 3)], wf.at[0], lsem.at[0])
    l2 = pltpu.make_async_copy(wf.at[0], out.at[z, pl.ds(1, 3)], loc.at[1])
    def fetch(j):
        landed(j, 0)
        cw = pltpu.make_async_copy(out.at[srcs[j], 0], wz, sem.at[1]); cw.start()
        pltpu.make_async_remote_copy(src_ref=small, dst_ref=ssm.at[srcs[j]], send_sem=ss.at[j], recv_sem=sr.at[srcs[j]], device_id=(cn, z), device_id_type=MESH).wait_recv()
        cw.wait()
    def fcopy(j): return pltpu.make_async_copy(out.at[srcs[j], pl.ds(1, 3)], wf.at[(j + 1) % 2], lsem.at[(j + 1) % 2])
    def load(j):
        for p in (1, 2, 3): landed(j, p)
        fcopy(j).start()
    blocks = [z] + srcs
    def stores(n):
        return [pltpu.make_async_copy(f.at[n % 2], t.at[blocks[n]], osem.at[i, n % 2]) for i, (f, t) in enumerate(((ab, ao), (bb, bo), (ib, io)))]
    Z, XY, DG = zarr, xyarr, diag
    def mine(p): zsend(opiece(p, dp), z, p)

    @pl.when(g == 0)
    def _():
        barrier_all([(xn, z), (yn, z), (cn, z)] + [(dp, (z + j) % 4) for j in (1, 2, 3)])
        mine(0); mine(1)
        for j in range(3): sm(j).start()
        cw = pltpu.make_async_copy(own.at[0], wz, sem.at[1]); cw.start()
        l1.start()
        ssm[z] = small[...]
        load_rows(z, xl, xs, xb, sem.at[0])
        distances(z, slen, llen, dm)
        ct[...] = jnp.zeros_like(ct)
        lseo[...] = jnp.zeros_like(lseo)
        acc[...] = jnp.zeros_like(acc)
        cw.wait()
        l0.start()
        Z(0, 0); Z(1, 0); mine(2)
    n4 = lax.rem(g, 4)
    zz = jnp.where(n4 == 0, z, jnp.where(n4 == 1, srcs[0], jnp.where(n4 == 2, srcs[1], srcs[2])))
    @pl.when(g < 4)
    def _():
        xv = xb[...].reshape(R, D)
        bs = ssm.at[zz]
        q8o[zz] = ((nt(xv, wz[0:192, :]) + bs[0:1, 0:192]).astype(BF16).astype(F32) * 0.125).astype(BF16)
        ko[zz] = nt(xv, wz[192:384, :]).astype(BF16)
        v = (nt(xv, wz[384:576, :]) + bs[1:2, 0:192]).astype(BF16)
        vo[zz] = v
        vt[...] = v.T
        @pl.when(g == 2)
        def _():
            Z(0, 3)
        def hook(i):
            def on(n, j, fn):
                @pl.when((g == n) & (i == j))
                def _(): fn()
            on(0, 0, lambda: (XY(0, 0),))
            on(0, 1, lambda: (Z(0, 1), Z(2, 0),))
            on(0, 2, lambda: (XY(1, 0),))
            on(0, 3, lambda: (DG(0, 0), Z(1, 2), mine(3),))
            on(1, 0, lambda: (XY(2, 0),))
            on(1, 2, lambda: (DG(1, 0), Z(1, 1),))
            on(2, 1, lambda: (DG(2, 0),))
            on(2, 2, lambda: (XY(0, 1),))
            on(2, 3, lambda: (XY(1, 2), XY(1, 1), XY(0, 2),))
            on(3, 0, lambda: (XY(1, 3),))
            on(3, 1, lambda: (XY(0, 3), Z(2, 2),))
        attend_fwd(z, bs, q8o.at[zz], ko.at[zz], vt, dm, ct, lseo.at[zz], hook)
        cv = ct[...].T
        co[zz] = cv
        acc[...] += nn(cv, wz[576:768, :]).astype(BF16).astype(F32)
    @pl.when(g == 0)
    def _():
        l1.wait(); l2.start(); l0.wait(); Z(0, 2); fetch(0)
    @pl.when(g == 1)
    def _():
        fetch(1); Z(1, 3)
    @pl.when(g == 2)
    def _():
        fetch(2)
    @pl.when(g == 3)
    def _():
        Z(2, 3); DG(1, 1)
    @pl.when(g == 3)
    def _():
        sout[...] = ssm[...]
        for i in range(5):
            rw = slice(128 * i, 128 * i + 128)
            s = xb[i].astype(F32) + acc[rw, :] + vec[0:1, :]
            n, r = norm_fwd(s)
            n1o[rw, :] = n
            r1o[rw, :] = jnp.broadcast_to(r, (128, 128))
            hlo[rw, :] = (n * vec[1:2, :] + vec[2:3, :]).astype(BF16)
        acc[...] = jnp.zeros_like(acc)
        DG(1, 3); DG(0, 1); Z(2, 1); DG(0, 3); DG(0, 2)
        load_rows(z, cl, cs, xb, sem.at[0])
        DG(1, 2)
    for n in (1, 2, 3):
        @pl.when(g == 4 + n)
        def _():
            fcopy(n - 1).wait()
            if n > 1:
                for d in stores(n - 2): d.wait()
    @pl.when(g >= 4)
    def _():
        p = lax.rem(g, 2)
        def on(n, i, j, fn):
            @pl.when((g == n) & (i == j))
            def _(): fn()
        def tile(i, u):
            rw = pl.ds(pl.multiple_of(i * (R // 2), 64), R // 2)
            h = hlo[rw, :]
            gate = nn(h, wf[p, 0])
            up = nn(h, wf[p, 1])
            a, slope = gelu_parts(gate)
            ab[p, rw, :] = a
            bb[p, rw, :] = up * slope
            inner = (a * up).astype(BF16)
            ib[p, rw, :] = inner
            acc[rw, :] += nt(inner, wf[p, 2]).astype(BF16).astype(F32)
            on(4, i, 0, lambda: (load(0), XY(2, 3),))
            on(6, i, 0, lambda: (load(2),))
            return u
        lax.fori_loop(0, 2, tile, 0)
    for n in range(4):
        @pl.when(g == 4 + n)
        def _():
            for d in stores(n): d.start()
    @pl.when(g == 4)
    def _():
        l2.wait(); XY(2, 2); load(1); XY(2, 1)
    @pl.when(g == 5)
    def _():
        DG(2, 1); DG(2, 2); DG(2, 3)
    @pl.when(g == 7)
    def _():
        tot = [jnp.zeros((1, D), F32)] * 3
        for i in range(5):
            rw = slice(128 * i, 128 * i + 128)
            h1 = n1o[rw, :] * vec[1:2, :] + vec[2:3, :]
            n, r = norm_fwd(h1 + acc[rw, :] + vec[3:4, :])
            yo[rw, :] = (n * vec[4:5, :] + vec[5:6, :]).astype(BF16)
            gy = xb[i].astype(F32)
            gs = norm_bwd(gy * vec[4:5, :], n, r)
            gs2o[rw, :] = gs
            gfo[rw, :] = gs.astype(BF16)
            tot = [tot[0] + jnp.sum(gy * n, axis=0, keepdims=True), tot[1] + jnp.sum(gy, axis=0, keepdims=True), tot[2] + jnp.sum(gs, axis=0, keepdims=True)]
        vgo[...] = jnp.concatenate(tot + [jnp.zeros((5, D), F32)], axis=0)
        pass
        for p in range(4):
            zsend_wait(opiece(p, dp), z, p)
        for j in range(3):
            sm(j).wait_send()
            for p in range(4): sent(j, p)
        for n in (2, 3):
            for d in stores(n): d.wait()

def run_kg(slen, llen, own, small, xl, xs, cl, cs, vec):
    V, S = pltpu.VMEM, pltpu.SemaphoreType.DMA
    o = lambda *s: const(s)
    rz = lambda: sds((4, R, E), BF16)
    return pl.pallas_call(
        kg,
        grid_spec=pltpu.PrefetchScalarGridSpec(num_scalar_prefetch=2, grid=(8,),
            in_specs=[ANY, o(8, 256), ANY, ANY, ANY, ANY, o(8, D)],
            out_specs=[ANY, o(4, 8, 256), o(4, R, E), o(4, R, E), o(4, R, E), o(4, R, E), o(4, 8, R), o(R, D), o(R, 128), o(R, D), ANY, ANY, ANY, o(R, D), o(R, D), o(R, D), o(8, D)],
            scratch_shapes=[V((4, 8, 256), F32), V((5, 128, D), BF16), V((5, 512, 128), F32), V((E, R), BF16), V((E, R), BF16), V((R, D), F32), V((D, D), BF16),
                            V((2, 3, D, D), BF16), V((2, R, D), F32), V((2, R, D), F32), V((2, R, D), BF16),
                            S((4, 4, 10)), S((4, 4, 11)), S((2,)), S((3,)), S((4,)), S((2,)), S((2,)), S((3, 2))]),
        out_shape=[sds((4, 4, D, D), BF16), sds((4, 8, 256), F32), rz(), rz(), rz(), rz(), sds((4, 8, R), F32), sds((R, D), F32), sds((R, 128), F32), sds((R, D), BF16),
                   sds((4, R, D), F32), sds((4, R, D), F32), sds((4, R, D), BF16), sds((R, D), BF16), sds((R, D), BF16), sds((R, D), F32), sds((8, D), F32)],
        compiler_params=pltpu.CompilerParams(dimension_semantics=("arbitrary",), collective_id=0, has_side_effects=True, vmem_limit_bytes=VM),
        name="gather_forward")(slen, llen, own, small, xl, xs, cl, cs, vec)

ZO = (3, 0, 2, 1)

def far_order(z):
    e = 1 - ((z + 1) // 2) % 2
    return [z + 1 - 2 * (z % 2), e * ((z + 2) % 4) + (1 - e) * (3 - z), e * (3 - z) + (1 - e) * ((z + 2) % 4)]

H = PR // 2

def zo(g):
    h, e = g // 2, g * (3 - g) // 2
    return (1 - e) * (3 - 2 * h) + e * 2 * h

def add_into(n, dst, src):
    def body(i, u):
        d, r = dst(i), src(i)
        d[...] = (d[...].astype(F32) + r[...].astype(F32)).astype(BF16)
        return u
    lax.fori_loop(0, n, body, 0)

def kx(slen, llen, xl, xs, w, small, q8, k, v, ctx, lse, gs1, g3, yin, vin2, vin1, gqo, gwo, guo, gdo, yout, dxout, vout,
       xb, dm, kt, gc, gqt, gk, gv, ga, gat, xt, acc, gob, dxs, gbs, stage, vr, vs, l0,
       r03, rx3, ry3, rxy3, ryx3, rl3, rr3, r01, rx1, ry1, rxy1, ryx1, rl1, rr1,
       sem, s0s, s0r, s0l, s1s, s1r, s2s, s2r, ys, yr, vsem_s, vsem_r, loc):
    g = pl.program_id(0)
    dp, y, x, c, z = place()
    xn, yn, cn = dpi(y, 1 - x, c), dpi(1 - y, x, c), dpi(y, x, 1 - c)
    z1, z2 = z + 1 - 2 * (z % 2), (z + 2) % 4
    parts = (1, 3)
    r0, rx, ry, rxy, ryx, rl, rr = (r01, r03), (rx1, rx3), (ry1, ry3), (rxy1, rxy3), (ryx1, ryx3), (rl1, rl3), (rr1, rr3)
    def rows(p): return pl.ds(pl.multiple_of(p * PR, 32), PR)
    def rc(src, dst, ss, rs, dev):
        return pltpu.make_async_remote_copy(src_ref=src, dst_ref=dst, send_sem=ss, recv_sem=rs, device_id=dev, device_id_type=MESH)
    def blk(kd, zz, q):
        return l0.at[zz, q] if kd else gob.at[zz, :, rows(2 * q + c), :]
    def half(kd, zz, q, h):
        return l0.at[zz, q, :, pl.ds(h * H, H), :] if kd else gob.at[zz, :, pl.ds(pl.multiple_of((2 * q + c) * PR + h * H, 16), H), :]
    def st0(kd, zz, q):
        src = (g3 if kd else gob).at[zz, :, rows(2 * q + 1 - c), :]
        return rc(src, r0[kd].at[zz, q], s0s.at[kd, zz, q], s0r.at[kd, zz, q], (cn, z))
    def ld0(zz, q):
        return pltpu.make_async_copy(g3.at[zz, :, rows(2 * q + c), :], l0.at[zz, q], s0l.at[zz, q])
    def stage_0(kd, zz):
        for q in range(4):
            st0(kd, zz, q).start()
            if kd: ld0(zz, q).start()
    def stage_a(kd, zz):
        for q in range(4):
            st0(kd, zz, q).wait_recv()
            if kd: ld0(zz, q).wait()
        n = parts[kd]
        add_into(4 * n, lambda i: blk(kd, zz, i // n).at[i % n], lambda i: r0[kd].at[zz, i // n, i % n])
        for j in range(2):
            s1x(kd, zz, j).start(); s1y(kd, zz, j).start()
    def s1x(kd, zz, j):
        return rc(half(kd, zz, 2 * j + 1 - x, 0), rx[kd].at[zz, j], s1s.at[kd, zz, j], s1r.at[kd, zz, j], (xn, z))
    def s1y(kd, zz, j):
        return rc(half(kd, zz, 2 * (1 - y) + j, 1), ry[kd].at[zz, j], s1s.at[kd, zz, 2 + j], s1r.at[kd, zz, 2 + j], (yn, z))
    def s1xy(kd, zz):
        return rc(half(kd, zz, 2 * (1 - y) + x, 0), rxy[kd].at[zz], s1s.at[kd, zz, 4], s1r.at[kd, zz, 4], (yn, z))
    def s1yx(kd, zz):
        return rc(half(kd, zz, 2 * y + 1 - x, 1), ryx[kd].at[zz], s1s.at[kd, zz, 5], s1r.at[kd, zz, 5], (xn, z))
    def stage_b(kd, zz):
        n = parts[kd]
        for j in range(2): s1x(kd, zz, j).wait_recv()
        add_into(2 * n, lambda i: half(kd, zz, 2 * (i // n) + x, 0).at[i % n], lambda i: rx[kd].at[zz, i // n, i % n])
        s1xy(kd, zz).start()
        for j in range(2): s1y(kd, zz, j).wait_recv()
        add_into(2 * n, lambda i: half(kd, zz, 2 * y + i // n, 1).at[i % n], lambda i: ry[kd].at[zz, i // n, i % n])
        s1yx(kd, zz).start()
    def stage_c(kd, zz):
        n = parts[kd]
        s1xy(kd, zz).wait_recv()
        add_into(n, lambda i: half(kd, zz, 2 * y + x, 0).at[i], lambda i: rxy[kd].at[zz, i])
        s1yx(kd, zz).wait_recv()
        add_into(n, lambda i: half(kd, zz, 2 * y + x, 1).at[i], lambda i: ryx[kd].at[zz, i])
    def mine(kd, zz): return blk(kd, zz, 2 * y + x)
    def zs(kd, zz, right):
        return rc(mine(kd, zz), (rl if right else rr)[kd].at[zz], s2s.at[kd, zz], s2r.at[kd, zz, 0 if right else 1], (dp, z + 1 if right else z - 1))
    def stage_d(kd, zz, hop):
        n = parts[kd]
        if hop < zz:
            @pl.when(z == hop)
            def _():
                if hop > 0:
                    zs(kd, zz, True).wait_recv()
                    add_into(n, lambda i: mine(kd, zz).at[i], lambda i: rl[kd].at[zz, i])
                zs(kd, zz, True).start()
        if 3 - hop > zz:
            @pl.when(z == 3 - hop)
            def _():
                if hop > 0:
                    zs(kd, zz, False).wait_recv()
                    add_into(n, lambda i: mine(kd, zz).at[i], lambda i: rr[kd].at[zz, i])
                zs(kd, zz, False).start()
        if hop == max(zz, 3 - zz):
            @pl.when(z == zz)
            def _():
                if zz > 0: zs(kd, zz, True).wait_recv()
                if zz < 3: zs(kd, zz, False).wait_recv()
                for i in range(n):
                    t = mine(kd, zz)[i].astype(F32)
                    if zz > 0: t += rl[kd][zz, i].astype(F32)
                    if zz < 3: t += rr[kd][zz, i].astype(F32)
                    if kd:
                        if i < 2: guo[i] = t
                        else: gdo[...] = t
                    else:
                        for j in range(3): gqo[j] = t[:, j * E:j * E + E]
                        gwo[...] = t[:, 3 * E:4 * E]
    order = far_order(z)
    def yb(s): return 4 * s + s // 3
    CHUNKS = ((2, 0), (2, 2), (1, 4))
    def yc(t, src, s, h, right):
        n, off = CHUNKS[h]
        dst = (yout, dxout)[t].at[pl.ds(yb(s) + off, n)]
        src = dst if src is None else src.at[pl.ds(off, n)]
        return rc(src, dst, ys.at[t, s, h, right], yr.at[t, s, h], (dp, z + 1 if right else z - 1))
    def ysend(t, src, s, act, hs=(0, 1, 2)):
        for h in hs:
            for right in (1, 0):
                go = (s <= z) & (z < 3) if right else (s >= z) & (z > 0)
                @pl.when(go & (s == 2) if h == 2 else go)
                def _():
                    getattr(yc(t, src, s, h, right), act)()
    def yarr(t, j, h):
        s = order[j]
        if h == 2:
            @pl.when(s == 2)
            def _():
                yc(t, None, s, h, 1).wait_recv()
        else:
            yc(t, None, s, h, 1).wait_recv()
        ysend(t, None, s, "start", (h,))
    def own(t, hf, way):
        n, off = (4, 0) if hf == 0 else (1, 4)
        if way == 0:
            return pltpu.make_async_copy(yin.at[pl.ds(off, n)], stage.at[pl.ds(off, n)], loc.at[t, hf, 0])
        return pltpu.make_async_copy((stage, dxs)[t].at[pl.ds(off, n)], (yout, dxout)[t].at[pl.ds(yb(z) + off, n)], loc.at[t, hf, 1])
    def ownall(fn):
        fn(0)
        @pl.when(z == 2)
        def _():
            fn(1)
    vpeer = [(dp, z1), (dp, z2), (cn, z), (xn, z), (yn, z)]
    def vcopy(i): return rc(vs.at[i], vr.at[i], vsem_s.at[i], vsem_r.at[i], vpeer[i])
    def vstep(i):
        vcopy(i).wait_recv()
        tot = vs[i] + vr[i]
        if i < 4:
            vs[i + 1] = tot
            vcopy(i + 1).start()
        else:
            vout[...] = tot
    F, T, o = 1, 0, ZO
    def S0(kd, u): stage_0(kd, o[u])
    def A(kd, u): stage_a(kd, o[u])
    def B(kd, u): stage_b(kd, o[u])
    def C(kd, u): stage_c(kd, o[u])
    def Z(kd, u, hop): stage_d(kd, o[u], hop)

    @pl.when(g == 0)
    def _():
        barrier_all([(xn, z), (yn, z), (cn, z)] + [(dp, (z + j) % 4) for j in (1, 2, 3)])
        S0(F, 0)
        ysend(0, yin, z, "start")
        ownall(lambda h: own(0, h, 0).start())
        for j in (1, 2, 3): S0(F, j)
        cg = pltpu.make_async_copy(gs1, acc, sem.at[1]); cg.start()
        load_rows(z, xl, xs, xb, sem.at[0])
        distances(z, slen, llen, dm)
        xt[...] = xb[...].reshape(R, D).T
        gbs[...] = jnp.zeros_like(gbs)
        cg.wait()
        ga[...] = acc[...].astype(BF16)
        gat[...] = ga[...].T
        ownall(lambda h: (own(0, h, 0).wait(), own(0, h, 1).start()))
        yarr(0, 2, 2)
    wz, sm = w.at[0, 0], small.at[0]
    gc[...] = nt(ga[...], wz[576:768, :]).astype(BF16)
    kt[...] = k[0].T
    @pl.when(g == 2)
    def _():
        yarr(0, 2, 0)
    @pl.when(g == 3)
    def _():
        yarr(0, 2, 1)
    def hook(i):
        def on(n, j, fn):
            @pl.when((g == n) & (i == j))
            def _(): fn()
        on(0, 0, lambda: A(F, 0))
        on(0, 1, lambda: yarr(0, 0, 0))
        on(0, 3, lambda: A(F, 1))
        on(1, 0, lambda: yarr(0, 0, 1))
        on(1, 2, lambda: yarr(0, 1, 1))
        on(1, 3, lambda: B(F, 0))
        on(2, 2, lambda: (A(T, 0), C(F, 0), Z(F, 0, 0)))
    attend_bwd(z, sm, q8.at[0], k.at[0], v.at[0], kt, gc, dm, lse.at[0], gqt, gk, gv, hook)
    @pl.when(g == 0)
    def _():
        yarr(0, 1, 0)
    zg = zo(g)
    dq = gqt[...].astype(BF16).T
    dk = gk[...].astype(BF16)
    dv = gv[...].astype(BF16)
    gbs[zg, 0:1, 0:192] = jnp.sum(dq.astype(F32), axis=0, keepdims=True)
    gbs[zg, 1:2, 0:192] = jnp.sum(dv.astype(F32), axis=0, keepdims=True)
    acc[...] += nn(dq, wz[0:192, :]) + nn(dk, wz[192:384, :]) + nn(dv, wz[384:576, :])
    def X():
        for i in range(5):
            dxs[i] = acc[128 * i:128 * i + 128, :].astype(BF16)
        vs[0] = jnp.zeros((16, D), F32)
        vs[0, 0:3, :] = vin2[0:3, :]
        vs[0, 3:6, :] = vin1[0:3, :]
        for i in range(4):
            vs[0, 6 + 2 * i:8 + 2 * i, 0:192] = gbs[i, 0:2, 0:192]
        vcopy(0).start()
        ysend(1, dxs, z, "start")
        ownall(lambda h: own(1, h, 1).start())
    @pl.when(g == 1)
    def _():
        yarr(1, 2, 2)
    @pl.when(g == 2)
    def _():
        C(F, 1); Z(F, 1, 0); yarr(0, 1, 2); A(F, 2)
    @pl.when(g == 3)
    def _():
        X(); B(F, 2); A(T, 1)
    for i in range(6):
        rw = slice(128 * i, 128 * i + 128)
        gob[zg, 0, rw, :] = jnp.concatenate([nn(xt[rw, :], dq), nn(xt[rw, :], dk), nn(xt[rw, :], dv), nn(gat[rw, :], ctx[0])], axis=1).astype(BF16)
    @pl.when(g == 0)
    def _():
        S0(T, 0)
    @pl.when(g == 1)
    def _():
        B(F, 1); S0(T, 1)
    @pl.when(g == 2)
    def _():
        S0(T, 2)
    @pl.when(g == 3)
    def _():
        A(F, 3); C(F, 2); Z(F, 1, 1); S0(T, 3); Z(F, 2, 0); Z(F, 0, 1); vstep(0); B(T, 1); B(T, 0)
        yarr(1, 1, 1); B(F, 3); A(T, 2); A(T, 3); C(T, 1); C(T, 0); Z(T, 0, 0); Z(T, 1, 0); yarr(1, 0, 0)
        yarr(1, 0, 2); yarr(1, 1, 0); C(F, 3); Z(F, 0, 2); Z(F, 1, 2); yarr(0, 0, 2); yarr(1, 0, 1); Z(F, 3, 0); vstep(1)
        B(T, 2); yarr(1, 1, 2); C(T, 2); Z(F, 0, 3); Z(T, 2, 0); Z(T, 1, 1); B(T, 3); C(T, 3); vstep(2)
        Z(F, 1, 3); yarr(1, 2, 1); Z(F, 3, 1); Z(T, 0, 1); Z(T, 3, 0); vstep(3); Z(T, 0, 2); Z(T, 0, 3); Z(T, 1, 2)
        Z(T, 1, 3); Z(F, 2, 1); yarr(1, 2, 0); Z(T, 2, 1); Z(F, 3, 2); Z(F, 2, 2); vstep(4); Z(T, 2, 2); Z(T, 3, 2)
        Z(T, 3, 1)
        for kd in (0, 1):
            for zz in ZO:
                for q in range(4): st0(kd, zz, q).wait_send()
                for j in range(2):
                    s1x(kd, zz, j).wait_send(); s1y(kd, zz, j).wait_send()
                s1xy(kd, zz).wait_send(); s1yx(kd, zz).wait_send()
                @pl.when(z < zz)
                def _(): zs(kd, zz, True).wait_send()
                @pl.when(z > zz)
                def _(): zs(kd, zz, False).wait_send()
        for t, src in enumerate((yin, dxs)):
            ysend(t, src, z, "wait_send")
            for j in range(3):
                ysend(t, None, order[j], "wait_send")
            ownall(lambda h: own(t, h, 1).wait())
        for i in range(5): vcopy(i).wait_send()

def run_kx(slen, llen, xl, xs, W, small, q8, k, v, ctx, lse, gs1, g3, yv, v2, v1):
    pz = lambda *s: pl.BlockSpec((1,) + s, lambda g, *_: (zo(g),) + (0,) * len(s))
    rz = lambda: pz(R, E)
    V, S = pltpu.VMEM, pltpu.SemaphoreType.DMA
    b = lambda *s: V(s + (PR, D), BF16)
    h = lambda *s: V(s + (H, D), BF16)
    bufs = lambda n: [b(4, 4, n), h(4, 2, n), h(4, 2, n), h(4, n), h(4, n), b(4, n), b(4, n)]
    scratch = [V((5, 128, D), BF16), V((5, 512, 128), F32), V((E, R), BF16), V((R, E), BF16), V((E, R), F32), V((R, E), F32), V((R, E), F32),
               V((R, D), BF16), V((D, R), BF16), V((D, R), BF16), V((R, D), F32), V((4, 1, D, D), BF16), V((5, 128, D), BF16), V((4, 8, 256), F32),
               V((5, 128, D), BF16), V((5, 16, D), F32), V((5, 16, D), F32), b(4, 4, 3)] + bufs(3) + bufs(1) + [
               S((2,)), S((2, 4, 4)), S((2, 4, 4)), S((4, 4)), S((2, 4, 6)), S((2, 4, 6)), S((2, 4)), S((2, 4, 2)), S((2, 4, 3, 2)), S((2, 4, 3)), S((5,)), S((5,)), S((2, 2, 2))]
    return pl.pallas_call(
        kx,
        grid_spec=pltpu.PrefetchScalarGridSpec(num_scalar_prefetch=2, grid=(4,),
            in_specs=[ANY, ANY, pl.BlockSpec((1, 1, D, D), lambda g, *_: (zo(g), 0, 0, 0)), pz(8, 256), rz(), rz(), rz(), rz(), pz(8, R), ANY, ANY, ANY, const((8, D)), const((8, D))],
            out_specs=[const((3, PR, E)), const((PR, E)), const((2, PR, D)), const((PR, D)), ANY, ANY, const((16, D))], scratch_shapes=scratch),
        out_shape=[sds((3, PR, E), F32), sds((PR, E), F32), sds((2, PR, D), F32), sds((PR, D), F32), sds((17, 128, D), BF16), sds((17, 128, D), BF16), sds((16, D), F32)],
        compiler_params=pltpu.CompilerParams(dimension_semantics=("arbitrary",), collective_id=1, has_side_effects=True, vmem_limit_bytes=VM),
        name="attention_backward_send")(slen, llen, xl, xs, W, small, q8, k, v, ctx, lse, gs1, g3, yv, v2, v1)

def split_rows(y, d, gq, gw, gd, yl, ys, dl, ds, gqo, gwo, gdo, buf, si, so):
    moves = [(y, 0, 0, 8, yl), (y, 0, 8, 9, ys), (d, 1, 0, 8, dl), (d, 1, 8, 9, ds)]
    put = lambda i: pltpu.make_async_copy(moves[i][0].at[pl.ds(moves[i][2], moves[i][3])], buf.at[moves[i][1], pl.ds(moves[i][2], moves[i][3])], si.at[i])
    out = lambda i: pltpu.make_async_copy(buf.at[moves[i][1], pl.ds(moves[i][2], moves[i][3])], moves[i][4], so.at[i])
    for i in range(4): put(i).start()
    gqo[...] = gq[...]
    gwo[...] = gw[...]
    gdo[...] = gd[...]
    for i in range(4):
        put(i).wait(); out(i).start()
    for i in range(4): out(i).wait()

def run_split(Y, DX, gq, gwo, gdn):
    V = pl.BlockSpec(memory_space=pltpu.VMEM)
    S = pltpu.SemaphoreType.DMA
    r = lambda n: sds((n, 128, D), BF16)
    return pl.pallas_call(split_rows, in_specs=[ANY, ANY, V, V, V], out_specs=[ANY] * 4 + [V] * 3,
        out_shape=[r(8), r(9), r(8), r(9), sds((3, PR, E), F32), sds((PR, E), F32), sds((PR, D), F32)],
        scratch_shapes=[pltpu.VMEM((2, 17, 128, D), BF16), S((4,)), S((4,))],
        compiler_params=pltpu.CompilerParams(vmem_limit_bytes=VM), name="split_rows")(Y, DX, gq, gwo, gdn)

def alibi_slopes(slope_index, head_total):
    power = 1 << head_total.bit_length() - 1
    f = slope_index.astype(F32)
    return jnp.where(slope_index < power, jnp.exp2(-8.0 * (f + 1.0) / power), jnp.exp2(-4.0 * (2.0 * (f - power) + 1.0) / power))
def prep(slope_index, w_qkv, b_qv, w_out, w_up, w_down):
    a = jnp.concatenate([jnp.transpose(w_qkv, (1, 2, 0)).reshape(576, D), w_out.T], 0)
    own = jnp.stack([a, w_up[:, 0], w_up[:, 1], w_down], 0)
    bt = jnp.transpose(b_qv, (1, 2, 0)).reshape(2, 192)
    sl = jnp.pad(alibi_slopes(slope_index, 12)[None], ((0, 0), (0, 189)))
    small = jnp.pad(jnp.concatenate([bt, sl], 0), ((0, 5), (0, 64)))
    return own, small
def per_device(x_short, x_long, short_lengths, long_lengths, slope_index, w_qkv, b_qv, w_out, b_out, gain1, bias1, w_up, w_down, b_down, gain2, bias2, cot_short, cot_long):
    own, small = prep(slope_index, w_qkv, b_qv, w_out, w_up, w_down)
    row = lax.broadcasted_iota(jnp.int32, (8, D), 0)
    vec = jnp.broadcast_to(bias2[None], (8, D))
    for i, t in enumerate((b_out, gain1, bias1, b_down, gain2)):
        vec = jnp.where(row == i, t[None], vec)
    xl, cl = x_long.reshape(8, 128, D), cot_long.reshape(8, 128, D)
    W, S, q8, k, v, ctx, lse, n1, r1, hl, a, b, inner, y, gf, gs2, vg2 = run_kg(short_lengths, long_lengths, own, small, xl, x_short, cl, cot_short, vec)
    go3, gs1, vg1 = run_kc(W, a, b, inner, gf, hl, gs2, n1, r1, vec)
    m, dpx = lax.axis_index("mp"), lax.axis_index("dp")
    gq, gwo, gup, gdn, Y, DX, vs = run_kx(short_lengths, long_lengths, xl, x_short, W, S, q8, k, v, ctx, lse, gs1, go3, y.reshape(5, 128, D), vg2, vg1)
    b = lax.dynamic_slice(vs[6:14, :192].reshape(4, 2, 3, 64), (m, 0, 0, 8 * dpx), (1, 2, 3, 8))[0]
    vs = lax.dynamic_slice(vs[:6], (0, 96 * dpx), (6, 96))
    yl, ys, dl, ds, gq, gwo, gdn = run_split(Y, DX, gq, gwo, gdn)
    return (ys, yl.reshape(2, 512, D), ds, dl.reshape(2, 512, D), jnp.transpose(gq, (1, 0, 2)), jnp.transpose(b, (2, 0, 1)), gwo, vs[5], vs[3], vs[4], jnp.transpose(gup, (1, 0, 2)), gdn, vs[2], vs[0], vs[1])
def per_device_any(x_short, x_long, short_lengths, long_lengths, slope_index, w_qkv, b_qv, w_out, b_out, gain1, bias1, w_up, w_down, b_down, gain2, bias2, cot_short, cot_long):
    own, small = prep(slope_index, w_qkv, b_qv, w_out, w_up, w_down)
    W = lax.all_gather(own, "mp"); S = lax.all_gather(small, "mp")
    vec = jnp.stack([b_out, gain1, bias1, b_down, gain2, bias2, bias2, bias2], 0)
    xl, cl = x_long.reshape(8, 128, D), cot_long.reshape(8, 128, D)
    q8, k, v, ctx, lse, n1, r1, hl = run_ka(short_lengths, long_lengths, xl, x_short, W, S, vec)
    a, b, inner, y, gf, gs2, vg2 = run_kb(cl, cot_short, W, hl, n1, vec)
    go3, gs1, vg1 = run_kc(W, a, b, inner, gf, hl, gs2, n1, r1, vec)
    go1, dx, gb = run_kd(short_lengths, long_lengths, xl, x_short, W, S, q8, k, v, ctx, lse, gs1.astype(BF16), gs1)
    m = lax.axis_index("mp")
    def spread(r):
        g = lax.all_gather(r, "mp")
        return jnp.concatenate([g[2], g[3][:512]], 0).reshape(9, 128, D), jnp.stack([g[0][:512], g[1][:512]], 0)
    ys, yl = spread(y); ds, dl = spread(dx)
    G = jnp.concatenate([go1, go3], 1).astype(F32)
    G = lax.psum_scatter(G, "mp", scatter_dimension=0, tiled=True)[0]
    G = lax.psum_scatter(G, "dp", scatter_dimension=1, tiled=True)
    vs = lax.psum(jnp.concatenate([vg2[:3], vg1[:3]], 0), "mp")
    vs = lax.psum_scatter(vs, "dp", scatter_dimension=1, tiled=True)
    gb = lax.psum_scatter(gb[:, :2, :192], "mp", scatter_dimension=0, tiled=True)[0]
    gb = jnp.transpose(gb.reshape(2, 3, 64), (2, 0, 1))
    gb = lax.psum_scatter(gb, "dp", scatter_dimension=0, tiled=True)
    gq = jnp.transpose(G[0][:, :576].reshape(-1, 3, 192), (0, 1, 2))
    return (ys, yl, ds, dl, gq, gb, G[0][:, 576:], vs[5], vs[3], vs[4], jnp.stack([G[1], G[2]], 1), G[3], vs[2], vs[0], vs[1])
def solution(mesh):
    fn = per_device if mesh.shape["dp"] == 8 else per_device_any
    d3 = P("dp", None, None)
    return jax.shard_map(fn, mesh=mesh,
        in_specs=(d3, d3, P("dp"), P("dp"), P("mp"), P(None, None, "mp"), P(None, None, "mp"), P(None, "mp"), P(), P(), P(), P(None, None, "mp"), P(None, "mp"), P(), P(), P(), d3, d3),
        out_specs=(d3, d3, d3, d3, P("dp", None, "mp"), P("dp", None, "mp"), P("dp", "mp"), P("dp"), P("dp"), P("dp"), P("dp", None, "mp"), P("dp", "mp"), P("dp"), P("dp"), P("dp")),
        check_vma=False)
```

```python
import functools
import math

import jax
import jax.numpy as jnp
from jax import lax
from jax.experimental import pallas as pl
from jax.experimental.pallas import tpu as pltpu
from jax.sharding import PartitionSpec as P

F32, BF16 = jnp.float32, jnp.bfloat16
R, D, E = 640, 768, 192
FAR = 1e30
VM = 60 << 20

def nn(a, b): return lax.dot_general(a, b, (((1,), (0,)), ((), ())), preferred_element_type=F32)
def nt(a, b): return lax.dot_general(a, b, (((1,), (1,)), ((), ())), preferred_element_type=F32)

def load_rows(m, long_ref, short_ref, buf, sem):
    @pl.when(m < 2)
    def _():
        c = pltpu.make_async_copy(long_ref.at[pl.ds(4 * m, 4)], buf.at[pl.ds(0, 4)], sem); c.start(); c.wait()
        buf[4] = jnp.zeros((128, D), BF16)
    @pl.when(m == 2)
    def _():
        c = pltpu.make_async_copy(short_ref.at[pl.ds(0, 5)], buf, sem); c.start(); c.wait()
    @pl.when(m == 3)
    def _():
        c = pltpu.make_async_copy(short_ref.at[pl.ds(5, 4)], buf.at[pl.ds(0, 4)], sem); c.start(); c.wait()
        buf[4] = jnp.zeros((128, D), BF16)

def distances(m, slen, llen, dm):
    @pl.when(m < 2)
    def _():
        n = llen[jnp.minimum(m, 1)]
        key = lax.broadcasted_iota(jnp.int32, (512, 128), 0)
        qry = lax.broadcasted_iota(jnp.int32, (512, 128), 1)
        for i in range(4):
            dist = jnp.abs(key - (qry + 128 * i)).astype(F32)
            dm[i] = jnp.where(key < n, dist, FAR)
    @pl.when(m >= 2)
    def _():
        key = lax.broadcasted_iota(jnp.int32, (128, 128), 0)
        qry = lax.broadcasted_iota(jnp.int32, (128, 128), 1)
        dist = jnp.abs(key - qry).astype(F32)
        for i in range(5):
            n = slen[jnp.minimum(5 * (m - 2) + i, 8)] if i == 4 else slen[jnp.maximum(5 * (m - 2), 0) + i]
            dm[i, 0:128, :] = jnp.where(key < n, dist, FAR)

def head_lanes(j):
    return lax.broadcasted_iota(jnp.int32, (1, E), 1) // 64 == j
def head_rows(j):
    return lax.broadcasted_iota(jnp.int32, (E, 1), 0) // 64 == j

def attend_fwd(m, small, q8, k, vt, dm, ct, lse, hook=lambda i: None):
    def block(i, keys, koff):
        cols = pl.ds(pl.multiple_of(i * 128, 128), 128)
        qi = q8[cols, :]
        kk = k[pl.ds(koff, keys), :]
        vv = vt[:, pl.ds(koff, keys)]
        d = dm[i, 0:keys, :]
        out = jnp.zeros((E, 128), F32)
        for j in range(3):
            s = nt(kk, jnp.where(head_lanes(j), qi, jnp.zeros_like(qi))) - small[2:3, j:j + 1] * d
            mx = jnp.max(s, axis=0, keepdims=True)
            ex = jnp.exp(s - mx)
            tot = jnp.sum(ex, axis=0, keepdims=True)
            p = (ex * (1.0 / tot)).astype(BF16)
            out = jnp.where(head_rows(j), nn(vv, p), out)
            lse[j:j + 1, cols] = mx + jnp.log(tot)
        ct[:, cols] = out.astype(BF16)
    @pl.when(m < 2)
    def _():
        lax.fori_loop(0, 4, lambda i, u: (block(i, 512, 0), hook(i), u)[2], 0)
    @pl.when(m >= 2)
    def _():
        lax.fori_loop(0, 5, lambda i, u: (block(i, 128, pl.multiple_of(i * 128, 128)), hook(i), u)[2], 0)

def attend_bwd(m, small, q8, k, v, kt, gc, dm, lse, gqt, gk, gv, hook=lambda i: None):
    gk[...] = jnp.zeros_like(gk)
    gv[...] = jnp.zeros_like(gv)
    def block(i, keys, koff):
        cols = pl.ds(pl.multiple_of(i * 128, 128), 128)
        rows = pl.ds(koff, keys)
        qi, gi = q8[cols, :], gc[cols, :]
        kk, vv, ktt = k[rows, :], v[rows, :], kt[:, rows]
        d = dm[i, 0:keys, :]
        oq = jnp.zeros((E, 128), F32)
        ok = jnp.zeros((keys, E), F32)
        ov = jnp.zeros((keys, E), F32)
        for j in range(3):
            hl = head_lanes(j)
            qj = jnp.where(hl, qi, jnp.zeros_like(qi))
            gj = jnp.where(hl, gi, jnp.zeros_like(gi))
            s = nt(kk, qj) - small[2:3, j:j + 1] * d
            p = jnp.exp(s - lse[j:j + 1, cols])
            gp = nt(vv, gj)
            ov = ov + nn(p.astype(BF16), gj)
            row = jnp.sum(p * gp, axis=0, keepdims=True)
            ds = (p * (gp - row)).astype(BF16)
            oq = jnp.where(head_rows(j), nn(ktt, ds), oq)
            ok = ok + nn(ds, qj)
        gqt[:, cols] = oq * 0.125
        gk[rows, :] += ok
        gv[rows, :] += ov
    @pl.when(m < 2)
    def _():
        lax.fori_loop(0, 4, lambda i, u: (block(i, 512, 0), hook(i), u)[2], 0)
        gqt[:, 512:640] = jnp.zeros((E, 128), F32)
    @pl.when(m >= 2)
    def _():
        lax.fori_loop(0, 5, lambda i, u: (block(i, 128, pl.multiple_of(i * 128, 128)), hook(i), u)[2], 0)

def norm_fwd(s):
    mean = jnp.mean(s, axis=1, keepdims=True)
    c = s - mean
    r = lax.rsqrt(jnp.mean(c * c, axis=1, keepdims=True) + 1e-12)
    return c * r, r

def norm_bwd(gn, normed, r):
    return r * (gn - jnp.mean(gn, axis=1, keepdims=True) - normed * jnp.mean(gn * normed, axis=1, keepdims=True))

def row_tiles(fn, tile=640):
    def body(i, u):
        fn(pl.ds(pl.multiple_of(i * tile, tile), tile)); return u
    lax.fori_loop(0, R // tile, body, 0)

def ka(slen, llen, xl, xs, w, small, vec, q8o, ko, vo, co, lseo, n1o, r1o, hlo, xb, dm, vt, ct, acc, sem):
    z = pl.program_id(0)
    m = lax.axis_index("mp")
    @pl.when(z == 0)
    def _():
        load_rows(m, xl, xs, xb, sem)
        distances(m, slen, llen, dm)
        ct[...] = jnp.zeros_like(ct)
        lseo[...] = jnp.zeros_like(lseo)
        acc[...] = jnp.zeros_like(acc)
    x = xb[...].reshape(R, D)
    wz, sm = w.at[0, 0], small.at[0]
    q8o[0] = ((nt(x, wz[0:192, :]) + sm[0:1, 0:192]).astype(BF16).astype(F32) * 0.125).astype(BF16)
    ko[0] = nt(x, wz[192:384, :]).astype(BF16)
    v = (nt(x, wz[384:576, :]) + sm[1:2, 0:192]).astype(BF16)
    vo[0] = v
    vt[...] = v.T
    attend_fwd(m, sm, q8o.at[0], ko.at[0], vt, dm, ct, lseo.at[0])
    co[0] = ct[...].T
    acc[...] += nn(co[0], wz[576:768, :]).astype(BF16).astype(F32)
    @pl.when(z == 3)
    def _():
        for i in range(5):
            rows = slice(128 * i, 128 * i + 128)
            s = xb[i].astype(F32) + acc[rows, :] + vec[0:1, :]
            n, r = norm_fwd(s)
            n1o[rows, :] = n
            r1o[rows, :] = jnp.broadcast_to(r, (128, 128))
            hlo[rows, :] = (n * vec[1:2, :] + vec[2:3, :]).astype(BF16)

def const(shape): return pl.BlockSpec(shape, lambda z, *_: (0,) * len(shape))
def perz(shape): return pl.BlockSpec((1,) + shape, lambda z, *_: (z,) + (0,) * len(shape))
ANY = pl.BlockSpec(memory_space=pl.ANY)
def sds(shape, dt): return jax.ShapeDtypeStruct(shape, dt)
def part(p): return pl.BlockSpec((1, 1, D, D), lambda z, *_: (z, p, 0, 0))

def call(kernel, in_specs, outs, scratch, name, args, grid=(4,), prefetch=2):
    return pl.pallas_call(
        kernel,
        grid_spec=pltpu.PrefetchScalarGridSpec(num_scalar_prefetch=prefetch, grid=grid, in_specs=in_specs,
            out_specs=[o[0] for o in outs], scratch_shapes=scratch),
        out_shape=[o[1] for o in outs],
        compiler_params=pltpu.CompilerParams(dimension_semantics=("arbitrary",), vmem_limit_bytes=VM),
        name=name)(*args)

def run_ka(slen, llen, xl, xs, W, small, vec):
    rz = lambda: (perz((R, E)), sds((4, R, E), BF16))
    return call(ka, [ANY, ANY, part(0), perz((8, 256)), const((8, D))],
        [rz(), rz(), rz(), rz(), (perz((8, R)), sds((4, 8, R), F32)), (const((R, D)), sds((R, D), F32)), (const((R, 128)), sds((R, 128), F32)), (const((R, D)), sds((R, D), BF16))],
        [pltpu.VMEM((5, 128, D), BF16), pltpu.VMEM((5, 512, 128), F32), pltpu.VMEM((E, R), BF16), pltpu.VMEM((E, R), BF16), pltpu.VMEM((R, D), F32), pltpu.SemaphoreType.DMA],
        "attention_forward", (slen, llen, xl, xs, W, small, vec))

def gelu_parts(g):
    cdf = 0.5 * (1.0 + lax.erf(g * (2.0 ** -0.5)))
    pdf = jnp.exp(-0.5 * g * g) * (1.0 / math.sqrt(2 * math.pi))
    return g * cdf, cdf + g * pdf

def kb(cl, cs, wg, wu, wd, hl, n1, vec, ao, bo, io, yo, gfo, gs2o, vgo, acc, cb, sem):
    z = pl.program_id(0)
    m = lax.axis_index("mp")
    @pl.when(z == 0)
    def _():
        load_rows(m, cl, cs, cb, sem)
        acc[...] = jnp.zeros_like(acc)
    def tile(rows):
        h = hl[rows, :]
        gate = nn(h, wg[0, 0])
        up = nn(h, wu[0, 0])
        a, slope = gelu_parts(gate)
        ao[0, rows, :] = a
        bo[0, rows, :] = up * slope
        inner = (a * up).astype(BF16)
        io[0, rows, :] = inner
        acc[rows, :] += nt(inner, wd[0, 0]).astype(BF16).astype(F32)
    row_tiles(tile)
    @pl.when(z == 3)
    def _():
        tot = [jnp.zeros((1, D), F32)] * 3
        for i in range(5):
            rows = slice(128 * i, 128 * i + 128)
            h1 = n1[rows, :] * vec[1:2, :] + vec[2:3, :]
            n, r = norm_fwd(h1 + acc[rows, :] + vec[3:4, :])
            yo[rows, :] = (n * vec[4:5, :] + vec[5:6, :]).astype(BF16)
            gy = cb[i].astype(F32)
            gs = norm_bwd(gy * vec[4:5, :], n, r)
            gs2o[rows, :] = gs
            gfo[rows, :] = gs.astype(BF16)
            tot = [tot[0] + jnp.sum(gy * n, axis=0, keepdims=True), tot[1] + jnp.sum(gy, axis=0, keepdims=True), tot[2] + jnp.sum(gs, axis=0, keepdims=True)]
        vgo[...] = jnp.concatenate(tot + [jnp.zeros((5, D), F32)], axis=0)

def run_kb(cl, cs, W, hl, n1, vec):
    z32 = lambda: (perz((R, D)), sds((4, R, D), F32))
    return call(kb, [ANY, ANY, part(1), part(2), part(3), const((R, D)), const((R, D)), const((8, D))],
        [z32(), z32(), (perz((R, D)), sds((4, R, D), BF16)), (const((R, D)), sds((R, D), BF16)), (const((R, D)), sds((R, D), BF16)), (const((R, D)), sds((R, D), F32)), (const((8, D)), sds((8, D), F32))],
        [pltpu.VMEM((R, D), F32), pltpu.VMEM((5, 128, D), BF16), pltpu.SemaphoreType.DMA],
        "feed_forward", (cl, cs, W, W, W, hl, n1, vec), prefetch=0)

def kc(wg, wu, wd, a, b, inner, gf, hl, gs2, n1, r1, vec, go, gs1o, vgo, acc, gft, hlt, gg):
    z = pl.program_id(0)
    @pl.when(z == 0)
    def _():
        acc[...] = gs2[...]
        gft[...] = gf[...].T
        hlt[...] = hl[...].T
    def tile(rows):
        gi = nn(gf[rows, :], wd[0, 0])
        g1 = (gi * b[0, rows, :]).astype(BF16)
        g2 = (gi * a[0, rows, :]).astype(BF16)
        gg[0, rows, :] = g1
        gg[1, rows, :] = g2
        acc[rows, :] += nt(g1, wg[0, 0]) + nt(g2, wu[0, 0])
    row_tiles(tile)
    def wtile(rows):
        go[0, 2, rows, :] = nn(gft[rows, :], inner[0]).astype(BF16)
        go[0, 0, rows, :] = nn(hlt[rows, :], gg[0]).astype(BF16)
        go[0, 1, rows, :] = nn(hlt[rows, :], gg[1]).astype(BF16)
    wtile(slice(0, D))
    @pl.when(z == 3)
    def _():
        tot = [jnp.zeros((1, D), F32)] * 3
        for i in range(5):
            rows = slice(128 * i, 128 * i + 128)
            gh, n = acc[rows, :], n1[rows, :]
            gs = norm_bwd(gh * vec[1:2, :], n, r1[rows, 0:1])
            gs1o[rows, :] = gs
            tot = [tot[0] + jnp.sum(gh * n, axis=0, keepdims=True), tot[1] + jnp.sum(gh, axis=0, keepdims=True), tot[2] + jnp.sum(gs, axis=0, keepdims=True)]
        vgo[...] = jnp.concatenate(tot + [jnp.zeros((5, D), F32)], axis=0)

def run_kc(W, a, b, inner, gf, hl, gs2, n1, r1, vec):
    c = lambda dt: const((R, D))
    return call(kc, [part(1), part(2), part(3), perz((R, D)), perz((R, D)), perz((R, D)), c(0), c(0), c(0), c(0), const((R, 128)), const((8, D))],
        [(pl.BlockSpec((1, 3, D, D), lambda z: (z, 0, 0, 0)), sds((4, 3, D, D), BF16)), (const((R, D)), sds((R, D), F32)), (const((8, D)), sds((8, D), F32))],
        [pltpu.VMEM((R, D), F32), pltpu.VMEM((D, R), BF16), pltpu.VMEM((D, R), BF16), pltpu.VMEM((2, R, D), BF16)],
        "feed_backward", (W, W, W, a, b, inner, gf, hl, gs2, n1, r1, vec), prefetch=0)

def kd(slen, llen, xl, xs, w, small, q8, k, v, ctx, lse, ga, gs1, go, dxo, gbo, xb, dm, kt, gc, gqt, gk, gv, gat, xt, acc, sem):
    z = pl.program_id(0)
    m = lax.axis_index("mp")
    @pl.when(z == 0)
    def _():
        load_rows(m, xl, xs, xb, sem)
        distances(m, slen, llen, dm)
        acc[...] = gs1[...]
        gat[...] = ga[...].T
        xt[...] = xb[...].reshape(R, D).T
        gbo[...] = jnp.zeros_like(gbo)
    wz, sm = w.at[0, 0], small.at[0]
    gc[...] = nt(ga[...], wz[576:768, :]).astype(BF16)
    kt[...] = k[0].T
    attend_bwd(m, sm, q8.at[0], k.at[0], v.at[0], kt, gc, dm, lse.at[0], gqt, gk, gv)
    dq = gqt[...].astype(BF16).T
    dk = gk[...].astype(BF16)
    dv = gv[...].astype(BF16)
    gbo[z, 0:1, 0:192] = jnp.sum(dq.astype(F32), axis=0, keepdims=True)
    gbo[z, 1:2, 0:192] = jnp.sum(dv.astype(F32), axis=0, keepdims=True)
    acc[...] += nn(dq, wz[0:192, :]) + nn(dk, wz[192:384, :]) + nn(dv, wz[384:576, :])
    def wtile(rows):
        xr = xt[rows, :]
        go[0, 0, rows, :] = jnp.concatenate([nn(xr, dq), nn(xr, dk), nn(xr, dv), nn(gat[rows, :], ctx[0])], axis=1).astype(BF16)
    for i in range(6):
        wtile(slice(128 * i, 128 * i + 128))
    @pl.when(z == 3)
    def _():
        dxo[...] = acc[...].astype(BF16)

def run_kd(slen, llen, xl, xs, W, small, q8, k, v, ctx, lse, ga, gs1):
    rz = lambda: perz((R, E))
    rd = const((R, D))
    return call(kd, [ANY, ANY, part(0), perz((8, 256)), rz(), rz(), rz(), rz(), perz((8, R)), rd, rd],
        [(pl.BlockSpec((1, 1, D, D), lambda z, *_: (z, 0, 0, 0)), sds((4, 1, D, D), BF16)), (rd, sds((R, D), BF16)), (const((4, 8, 256)), sds((4, 8, 256), F32))],
        [pltpu.VMEM((5, 128, D), BF16), pltpu.VMEM((5, 512, 128), F32), pltpu.VMEM((E, R), BF16), pltpu.VMEM((R, E), BF16), pltpu.VMEM((E, R), F32), pltpu.VMEM((R, E), F32), pltpu.VMEM((R, E), F32),
         pltpu.VMEM((D, R), BF16), pltpu.VMEM((D, R), BF16), pltpu.VMEM((R, D), F32), pltpu.SemaphoreType.DMA],
        "attention_backward", (slen, llen, xl, xs, W, small, q8, k, v, ctx, lse, ga, gs1))

MESH = pl.DeviceIdType.MESH
PR = 96

def place():
    dp = lax.axis_index("dp"); z = lax.axis_index("mp")
    return dp, dp // 4, (dp // 2) % 2, dp % 2, z

def dpi(y, x, c):
    return (y * 2 + x) * 2 + c

def barrier_all(peers):
    b = pltpu.get_barrier_semaphore()
    for d in peers:
        pl.semaphore_signal(b, inc=1, device_id=d, device_id_type=MESH)
    pl.semaphore_wait(b, len(peers))

def kg(slen, llen, own, small, xl, xs, cl, cs, vec, out, sout, q8o, ko, vo, co, lseo, n1o, r1o, hlo, ao, bo, io, yo, gfo, gs2o, vgo,
       ssm, xb, dm, vt, ct, acc, wz, wf, ab, bb, ib, recv, send, loc, ss, sr, sem, lsem, osem):
    g = pl.program_id(0)
    dp, y, x, c, z = place()
    xn, yn, cn = dpi(y, 1 - x, c), dpi(1 - y, x, c), dpi(y, x, 1 - c)
    dn = dpi(1 - y, 1 - x, c)
    def sm(j): return pltpu.make_async_remote_copy(src_ref=small, dst_ref=ssm.at[z], send_sem=ss.at[j], recv_sem=sr.at[z], device_id=(dp, (z + 1 + j) % 4), device_id_type=MESH)
    e = 1 - ((z + 1) // 2) % 2
    srcs = [z + 1 - 2 * (z % 2), e * ((z + 2) % 4) + (1 - e) * (3 - z), e * (3 - z) + (1 - e) * ((z + 2) % 4)]

    def rows(p, h):
        if h is None:
            return pl.ds(pl.multiple_of(p * PR, 32), PR)
        return pl.ds(pl.multiple_of(p * PR + h * (PR // 2), 16), PR // 2)
    def piece(s, g, p, h=None):
        return out.at[s, g, rows(p, h), :]
    def opiece(g, p):
        return own.at[g, rows(p, None), :]
    def cp(src, dst, s, g, k, r, dev):
        return pltpu.make_async_remote_copy(src_ref=src, dst_ref=dst, send_sem=send.at[s, g, k], recv_sem=recv.at[s, g, r], device_id=dev, device_id_type=MESH)
    def zsend(src, s, g):
        @pl.when((s <= z) & (z < 3))
        def _():
            cp(src, piece(s, g, dp), s, g, 0, 0, (dp, z + 1)).start()
        @pl.when((s >= z) & (z > 0))
        def _():
            cp(src, piece(s, g, dp), s, g, 1, 0, (dp, z - 1)).start()
    def zsend_wait(src, s, g):
        @pl.when((s <= z) & (z < 3))
        def _():
            cp(src, piece(s, g, dp), s, g, 0, 0, (dp, z + 1)).wait_send()
        @pl.when((s >= z) & (z > 0))
        def _():
            cp(src, piece(s, g, dp), s, g, 1, 0, (dp, z - 1)).wait_send()
    def simple(s, g):
        me, xp, yp, dg = dp, xn, yn, dn
        return dict(
            x=lambda: cp(piece(s, g, me), piece(s, g, me), s, g, 2, 1, (xn, z)),
            y=lambda: cp(piece(s, g, me), piece(s, g, me), s, g, 3, 2, (yn, z)),
            c=lambda: cp(piece(s, g, me), piece(s, g, me), s, g, 4, 3, (cn, z)),
            cx=lambda: cp(piece(s, g, xp), piece(s, g, xp), s, g, 5, 4, (cn, z)),
            cy=lambda: cp(piece(s, g, yp), piece(s, g, yp), s, g, 6, 5, (cn, z)),
            yf=lambda: cp(piece(s, g, xp, 0), piece(s, g, xp, 0), s, g, 7, 6, (yn, z)),
            xf=lambda: cp(piece(s, g, yp, 1), piece(s, g, yp, 1), s, g, 8, 7, (xn, z)),
            cd0=lambda: cp(piece(s, g, dg, 0), piece(s, g, dg, 0), s, g, 9, 8, (cn, z)),
            cd1=lambda: cp(piece(s, g, dg, 1), piece(s, g, dg, 1), s, g, 10, 9, (cn, z)),
        )
    def wrecv(ref, s, g, r):
        pltpu.make_async_remote_copy(src_ref=ref, dst_ref=ref, send_sem=send.at[s, g, 0], recv_sem=recv.at[s, g, r], device_id=(cn, z), device_id_type=MESH).wait_recv()
    def zarr(j, g):
        s = srcs[j]
        wrecv(piece(s, g, dp), s, g, 0)
        zsend(piece(s, g, dp), s, g)
        m = simple(s, g)
        m["x"]().start(); m["y"]().start(); m["c"]().start()
    def xyarr(j, g):
        s = srcs[j]; m = simple(s, g)
        wrecv(piece(s, g, xn), s, g, 1)
        m["yf"]().start(); m["cx"]().start()
        wrecv(piece(s, g, yn), s, g, 2)
        m["xf"]().start(); m["cy"]().start()
    def diag(j, g):
        s = srcs[j]; m = simple(s, g)
        wrecv(piece(s, g, dn, 0), s, g, 6)
        m["cd0"]().start()
        wrecv(piece(s, g, dn, 1), s, g, 7)
        m["cd1"]().start()
    def landed(j, g):
        s = srcs[j]
        cdx, cdy, cdd = dpi(y, 1 - x, 1 - c), dpi(1 - y, x, 1 - c), dpi(1 - y, 1 - x, 1 - c)
        wrecv(piece(s, g, cn), s, g, 3)
        wrecv(piece(s, g, cdx), s, g, 4)
        wrecv(piece(s, g, cdy), s, g, 5)
        wrecv(piece(s, g, cdd, 0), s, g, 8)
        wrecv(piece(s, g, cdd, 1), s, g, 9)
    def sent(j, g):
        s = srcs[j]; m = simple(s, g)
        zsend_wait(piece(s, g, dp), s, g)
        for k in ("x", "y", "c", "cx", "cy", "yf", "xf", "cd0", "cd1"):
            m[k]().wait_send()
    l0 = pltpu.make_async_copy(wz, out.at[z, 0], loc.at[0])
    l1 = pltpu.make_async_copy(own.at[pl.ds(1, 3)], wf.at[0], lsem.at[0])
    l2 = pltpu.make_async_copy(wf.at[0], out.at[z, pl.ds(1, 3)], loc.at[1])
    def fetch(j):
        landed(j, 0)
        cw = pltpu.make_async_copy(out.at[srcs[j], 0], wz, sem.at[1]); cw.start()
        pltpu.make_async_remote_copy(src_ref=small, dst_ref=ssm.at[srcs[j]], send_sem=ss.at[j], recv_sem=sr.at[srcs[j]], device_id=(cn, z), device_id_type=MESH).wait_recv()
        cw.wait()
    def fcopy(j): return pltpu.make_async_copy(out.at[srcs[j], pl.ds(1, 3)], wf.at[(j + 1) % 2], lsem.at[(j + 1) % 2])
    def load(j):
        for p in (1, 2, 3): landed(j, p)
        fcopy(j).start()
    blocks = [z] + srcs
    def stores(n):
        return [pltpu.make_async_copy(f.at[n % 2], t.at[blocks[n]], osem.at[i, n % 2]) for i, (f, t) in enumerate(((ab, ao), (bb, bo), (ib, io)))]
    Z, XY, DG = zarr, xyarr, diag
    def mine(p): zsend(opiece(p, dp), z, p)

    @pl.when(g == 0)
    def _():
        barrier_all([(xn, z), (yn, z), (cn, z)] + [(dp, (z + j) % 4) for j in (1, 2, 3)])
        mine(0); mine(1)
        for j in range(3): sm(j).start()
        cw = pltpu.make_async_copy(own.at[0], wz, sem.at[1]); cw.start()
        l1.start()
        ssm[z] = small[...]
        load_rows(z, xl, xs, xb, sem.at[0])
        distances(z, slen, llen, dm)
        ct[...] = jnp.zeros_like(ct)
        lseo[...] = jnp.zeros_like(lseo)
        acc[...] = jnp.zeros_like(acc)
        cw.wait()
        l0.start()
        Z(0, 0); Z(1, 0); mine(2)
    n4 = lax.rem(g, 4)
    zz = jnp.where(n4 == 0, z, jnp.where(n4 == 1, srcs[0], jnp.where(n4 == 2, srcs[1], srcs[2])))
    @pl.when(g < 4)
    def _():
        xv = xb[...].reshape(R, D)
        bs = ssm.at[zz]
        q8o[zz] = ((nt(xv, wz[0:192, :]) + bs[0:1, 0:192]).astype(BF16).astype(F32) * 0.125).astype(BF16)
        ko[zz] = nt(xv, wz[192:384, :]).astype(BF16)
        v = (nt(xv, wz[384:576, :]) + bs[1:2, 0:192]).astype(BF16)
        vo[zz] = v
        vt[...] = v.T
        @pl.when(g == 2)
        def _():
            Z(0, 3)
        def hook(i):
            def on(n, j, fn):
                @pl.when((g == n) & (i == j))
                def _(): fn()
            on(0, 0, lambda: (XY(0, 0),))
            on(0, 1, lambda: (Z(0, 1), Z(2, 0),))
            on(0, 2, lambda: (XY(1, 0),))
            on(0, 3, lambda: (DG(0, 0), Z(1, 2), mine(3),))
            on(1, 0, lambda: (XY(2, 0),))
            on(1, 2, lambda: (DG(1, 0), Z(1, 1),))
            on(2, 1, lambda: (DG(2, 0),))
            on(2, 2, lambda: (XY(0, 1),))
            on(2, 3, lambda: (XY(1, 2), XY(1, 1), XY(0, 2),))
            on(3, 0, lambda: (XY(1, 3),))
            on(3, 1, lambda: (XY(0, 3), Z(2, 2),))
        attend_fwd(z, bs, q8o.at[zz], ko.at[zz], vt, dm, ct, lseo.at[zz], hook)
        cv = ct[...].T
        co[zz] = cv
        acc[...] += nn(cv, wz[576:768, :]).astype(BF16).astype(F32)
    @pl.when(g == 0)
    def _():
        l1.wait(); l2.start(); l0.wait(); Z(0, 2); fetch(0)
    @pl.when(g == 1)
    def _():
        fetch(1); Z(1, 3)
    @pl.when(g == 2)
    def _():
        fetch(2)
    @pl.when(g == 3)
    def _():
        Z(2, 3); DG(1, 1)
    @pl.when(g == 3)
    def _():
        sout[...] = ssm[...]
        for i in range(5):
            rw = slice(128 * i, 128 * i + 128)
            s = xb[i].astype(F32) + acc[rw, :] + vec[0:1, :]
            n, r = norm_fwd(s)
            n1o[rw, :] = n
            r1o[rw, :] = jnp.broadcast_to(r, (128, 128))
            hlo[rw, :] = (n * vec[1:2, :] + vec[2:3, :]).astype(BF16)
        acc[...] = jnp.zeros_like(acc)
        DG(1, 3); DG(0, 1); Z(2, 1); DG(0, 3); DG(0, 2)
        load_rows(z, cl, cs, xb, sem.at[0])
        DG(1, 2)
    for n in (1, 2, 3):
        @pl.when(g == 4 + n)
        def _():
            fcopy(n - 1).wait()
            if n > 1:
                for d in stores(n - 2): d.wait()
    @pl.when(g >= 4)
    def _():
        p = lax.rem(g, 2)
        def on(n, i, j, fn):
            @pl.when((g == n) & (i == j))
            def _(): fn()
        def tile(i, u):
            rw = pl.ds(pl.multiple_of(i * (R // 2), 64), R // 2)
            h = hlo[rw, :]
            gate = nn(h, wf[p, 0])
            up = nn(h, wf[p, 1])
            a, slope = gelu_parts(gate)
            ab[p, rw, :] = a
            bb[p, rw, :] = up * slope
            inner = (a * up).astype(BF16)
            ib[p, rw, :] = inner
            acc[rw, :] += nt(inner, wf[p, 2]).astype(BF16).astype(F32)
            on(4, i, 0, lambda: (load(0), XY(2, 3),))
            on(6, i, 0, lambda: (load(2),))
            return u
        lax.fori_loop(0, 2, tile, 0)
    for n in range(4):
        @pl.when(g == 4 + n)
        def _():
            for d in stores(n): d.start()
    @pl.when(g == 4)
    def _():
        l2.wait(); XY(2, 2); load(1); XY(2, 1)
    @pl.when(g == 5)
    def _():
        DG(2, 1); DG(2, 2); DG(2, 3)
    @pl.when(g == 7)
    def _():
        tot = [jnp.zeros((1, D), F32)] * 3
        for i in range(5):
            rw = slice(128 * i, 128 * i + 128)
            h1 = n1o[rw, :] * vec[1:2, :] + vec[2:3, :]
            n, r = norm_fwd(h1 + acc[rw, :] + vec[3:4, :])
            yo[rw, :] = (n * vec[4:5, :] + vec[5:6, :]).astype(BF16)
            gy = xb[i].astype(F32)
            gs = norm_bwd(gy * vec[4:5, :], n, r)
            gs2o[rw, :] = gs
            gfo[rw, :] = gs.astype(BF16)
            tot = [tot[0] + jnp.sum(gy * n, axis=0, keepdims=True), tot[1] + jnp.sum(gy, axis=0, keepdims=True), tot[2] + jnp.sum(gs, axis=0, keepdims=True)]
        vgo[...] = jnp.concatenate(tot + [jnp.zeros((5, D), F32)], axis=0)
        pass
        for p in range(4):
            zsend_wait(opiece(p, dp), z, p)
        for j in range(3):
            sm(j).wait_send()
            for p in range(4): sent(j, p)
        for n in (2, 3):
            for d in stores(n): d.wait()

def run_kg(slen, llen, own, small, xl, xs, cl, cs, vec):
    V, S = pltpu.VMEM, pltpu.SemaphoreType.DMA
    o = lambda *s: const(s)
    rz = lambda: sds((4, R, E), BF16)
    return pl.pallas_call(
        kg,
        grid_spec=pltpu.PrefetchScalarGridSpec(num_scalar_prefetch=2, grid=(8,),
            in_specs=[ANY, o(8, 256), ANY, ANY, ANY, ANY, o(8, D)],
            out_specs=[ANY, o(4, 8, 256), o(4, R, E), o(4, R, E), o(4, R, E), o(4, R, E), o(4, 8, R), o(R, D), o(R, 128), o(R, D), ANY, ANY, ANY, o(R, D), o(R, D), o(R, D), o(8, D)],
            scratch_shapes=[V((4, 8, 256), F32), V((5, 128, D), BF16), V((5, 512, 128), F32), V((E, R), BF16), V((E, R), BF16), V((R, D), F32), V((D, D), BF16),
                            V((2, 3, D, D), BF16), V((2, R, D), F32), V((2, R, D), F32), V((2, R, D), BF16),
                            S((4, 4, 10)), S((4, 4, 11)), S((2,)), S((3,)), S((4,)), S((2,)), S((2,)), S((3, 2))]),
        out_shape=[sds((4, 4, D, D), BF16), sds((4, 8, 256), F32), rz(), rz(), rz(), rz(), sds((4, 8, R), F32), sds((R, D), F32), sds((R, 128), F32), sds((R, D), BF16),
                   sds((4, R, D), F32), sds((4, R, D), F32), sds((4, R, D), BF16), sds((R, D), BF16), sds((R, D), BF16), sds((R, D), F32), sds((8, D), F32)],
        compiler_params=pltpu.CompilerParams(dimension_semantics=("arbitrary",), collective_id=0, has_side_effects=True, vmem_limit_bytes=VM),
        name="gather_forward")(slen, llen, own, small, xl, xs, cl, cs, vec)

ZO = (3, 0, 2, 1)

def far_order(z):
    e = 1 - ((z + 1) // 2) % 2
    return [z + 1 - 2 * (z % 2), e * ((z + 2) % 4) + (1 - e) * (3 - z), e * (3 - z) + (1 - e) * ((z + 2) % 4)]

H = PR // 2

def zo(g):
    h, e = g // 2, g * (3 - g) // 2
    return (1 - e) * (3 - 2 * h) + e * 2 * h

def add_into(n, dst, src):
    def body(i, u):
        d, r = dst(i), src(i)
        d[...] = (d[...].astype(F32) + r[...].astype(F32)).astype(BF16)
        return u
    lax.fori_loop(0, n, body, 0)

def kx(slen, llen, xl, xs, w, small, q8, k, v, ctx, lse, gs1, g3, yin, vin2, vin1, gqo, gwo, guo, gdo, yout, dxout, vout,
       xb, dm, kt, gc, gqt, gk, gv, ga, gat, xt, acc, gob, dxs, gbs, stage, vr, vs, l0,
       r03, rx3, ry3, rxy3, ryx3, rl3, rr3, r01, rx1, ry1, rxy1, ryx1, rl1, rr1,
       sem, s0s, s0r, s0l, s1s, s1r, s2s, s2r, ys, yr, vsem_s, vsem_r, loc):
    g = pl.program_id(0)
    dp, y, x, c, z = place()
    xn, yn, cn = dpi(y, 1 - x, c), dpi(1 - y, x, c), dpi(y, x, 1 - c)
    z1, z2 = z + 1 - 2 * (z % 2), (z + 2) % 4
    parts = (1, 3)
    r0, rx, ry, rxy, ryx, rl, rr = (r01, r03), (rx1, rx3), (ry1, ry3), (rxy1, rxy3), (ryx1, ryx3), (rl1, rl3), (rr1, rr3)
    def rows(p): return pl.ds(pl.multiple_of(p * PR, 32), PR)
    def rc(src, dst, ss, rs, dev):
        return pltpu.make_async_remote_copy(src_ref=src, dst_ref=dst, send_sem=ss, recv_sem=rs, device_id=dev, device_id_type=MESH)
    def blk(kd, zz, q):
        return l0.at[zz, q] if kd else gob.at[zz, :, rows(2 * q + c), :]
    def half(kd, zz, q, h):
        return l0.at[zz, q, :, pl.ds(h * H, H), :] if kd else gob.at[zz, :, pl.ds(pl.multiple_of((2 * q + c) * PR + h * H, 16), H), :]
    def st0(kd, zz, q):
        src = (g3 if kd else gob).at[zz, :, rows(2 * q + 1 - c), :]
        return rc(src, r0[kd].at[zz, q], s0s.at[kd, zz, q], s0r.at[kd, zz, q], (cn, z))
    def ld0(zz, q):
        return pltpu.make_async_copy(g3.at[zz, :, rows(2 * q + c), :], l0.at[zz, q], s0l.at[zz, q])
    def stage_0(kd, zz):
        for q in range(4):
            st0(kd, zz, q).start()
            if kd: ld0(zz, q).start()
    def stage_a(kd, zz):
        for q in range(4):
            st0(kd, zz, q).wait_recv()
            if kd: ld0(zz, q).wait()
        n = parts[kd]
        add_into(4 * n, lambda i: blk(kd, zz, i // n).at[i % n], lambda i: r0[kd].at[zz, i // n, i % n])
        for j in range(2):
            s1x(kd, zz, j).start(); s1y(kd, zz, j).start()
    def s1x(kd, zz, j):
        return rc(half(kd, zz, 2 * j + 1 - x, 0), rx[kd].at[zz, j], s1s.at[kd, zz, j], s1r.at[kd, zz, j], (xn, z))
    def s1y(kd, zz, j):
        return rc(half(kd, zz, 2 * (1 - y) + j, 1), ry[kd].at[zz, j], s1s.at[kd, zz, 2 + j], s1r.at[kd, zz, 2 + j], (yn, z))
    def s1xy(kd, zz):
        return rc(half(kd, zz, 2 * (1 - y) + x, 0), rxy[kd].at[zz], s1s.at[kd, zz, 4], s1r.at[kd, zz, 4], (yn, z))
    def s1yx(kd, zz):
        return rc(half(kd, zz, 2 * y + 1 - x, 1), ryx[kd].at[zz], s1s.at[kd, zz, 5], s1r.at[kd, zz, 5], (xn, z))
    def stage_b(kd, zz):
        n = parts[kd]
        for j in range(2): s1x(kd, zz, j).wait_recv()
        add_into(2 * n, lambda i: half(kd, zz, 2 * (i // n) + x, 0).at[i % n], lambda i: rx[kd].at[zz, i // n, i % n])
        s1xy(kd, zz).start()
        for j in range(2): s1y(kd, zz, j).wait_recv()
        add_into(2 * n, lambda i: half(kd, zz, 2 * y + i // n, 1).at[i % n], lambda i: ry[kd].at[zz, i // n, i % n])
        s1yx(kd, zz).start()
    def stage_c(kd, zz):
        n = parts[kd]
        s1xy(kd, zz).wait_recv()
        add_into(n, lambda i: half(kd, zz, 2 * y + x, 0).at[i], lambda i: rxy[kd].at[zz, i])
        s1yx(kd, zz).wait_recv()
        add_into(n, lambda i: half(kd, zz, 2 * y + x, 1).at[i], lambda i: ryx[kd].at[zz, i])
    def mine(kd, zz): return blk(kd, zz, 2 * y + x)
    def zs(kd, zz, right):
        return rc(mine(kd, zz), (rl if right else rr)[kd].at[zz], s2s.at[kd, zz], s2r.at[kd, zz, 0 if right else 1], (dp, z + 1 if right else z - 1))
    def stage_d(kd, zz, hop):
        n = parts[kd]
        if hop < zz:
            @pl.when(z == hop)
            def _():
                if hop > 0:
                    zs(kd, zz, True).wait_recv()
                    add_into(n, lambda i: mine(kd, zz).at[i], lambda i: rl[kd].at[zz, i])
                zs(kd, zz, True).start()
        if 3 - hop > zz:
            @pl.when(z == 3 - hop)
            def _():
                if hop > 0:
                    zs(kd, zz, False).wait_recv()
                    add_into(n, lambda i: mine(kd, zz).at[i], lambda i: rr[kd].at[zz, i])
                zs(kd, zz, False).start()
        if hop == max(zz, 3 - zz):
            @pl.when(z == zz)
            def _():
                if zz > 0: zs(kd, zz, True).wait_recv()
                if zz < 3: zs(kd, zz, False).wait_recv()
                for i in range(n):
                    t = mine(kd, zz)[i].astype(F32)
                    if zz > 0: t += rl[kd][zz, i].astype(F32)
                    if zz < 3: t += rr[kd][zz, i].astype(F32)
                    if kd:
                        if i < 2: guo[i] = t
                        else: gdo[...] = t
                    else:
                        for j in range(3): gqo[j] = t[:, j * E:j * E + E]
                        gwo[...] = t[:, 3 * E:4 * E]
    order = far_order(z)
    def yb(s): return 4 * s + s // 3
    CHUNKS = ((2, 0), (2, 2), (1, 4))
    def yc(t, src, s, h, right):
        n, off = CHUNKS[h]
        dst = (yout, dxout)[t].at[pl.ds(yb(s) + off, n)]
        src = dst if src is None else src.at[pl.ds(off, n)]
        return rc(src, dst, ys.at[t, s, h, right], yr.at[t, s, h], (dp, z + 1 if right else z - 1))
    def ysend(t, src, s, act, hs=(0, 1, 2)):
        for h in hs:
            for right in (1, 0):
                go = (s <= z) & (z < 3) if right else (s >= z) & (z > 0)
                @pl.when(go & (s == 2) if h == 2 else go)
                def _():
                    getattr(yc(t, src, s, h, right), act)()
    def yarr(t, j, h):
        s = order[j]
        if h == 2:
            @pl.when(s == 2)
            def _():
                yc(t, None, s, h, 1).wait_recv()
        else:
            yc(t, None, s, h, 1).wait_recv()
        ysend(t, None, s, "start", (h,))
    def own(t, hf, way):
        n, off = (4, 0) if hf == 0 else (1, 4)
        if way == 0:
            return pltpu.make_async_copy(yin.at[pl.ds(off, n)], stage.at[pl.ds(off, n)], loc.at[t, hf, 0])
        return pltpu.make_async_copy((stage, dxs)[t].at[pl.ds(off, n)], (yout, dxout)[t].at[pl.ds(yb(z) + off, n)], loc.at[t, hf, 1])
    def ownall(fn):
        fn(0)
        @pl.when(z == 2)
        def _():
            fn(1)
    vpeer = [(dp, z1), (dp, z2), (cn, z), (xn, z), (yn, z)]
    def vcopy(i): return rc(vs.at[i], vr.at[i], vsem_s.at[i], vsem_r.at[i], vpeer[i])
    def vstep(i):
        vcopy(i).wait_recv()
        tot = vs[i] + vr[i]
        if i < 4:
            vs[i + 1] = tot
            vcopy(i + 1).start()
        else:
            vout[...] = tot
    F, T, o = 1, 0, ZO
    def S0(kd, u): stage_0(kd, o[u])
    def A(kd, u): stage_a(kd, o[u])
    def B(kd, u): stage_b(kd, o[u])
    def C(kd, u): stage_c(kd, o[u])
    def Z(kd, u, hop): stage_d(kd, o[u], hop)

    @pl.when(g == 0)
    def _():
        barrier_all([(xn, z), (yn, z), (cn, z)] + [(dp, (z + j) % 4) for j in (1, 2, 3)])
        S0(F, 0)
        ysend(0, yin, z, "start")
        ownall(lambda h: own(0, h, 0).start())
        for j in (1, 2, 3): S0(F, j)
        cg = pltpu.make_async_copy(gs1, acc, sem.at[1]); cg.start()
        load_rows(z, xl, xs, xb, sem.at[0])
        distances(z, slen, llen, dm)
        xt[...] = xb[...].reshape(R, D).T
        gbs[...] = jnp.zeros_like(gbs)
        cg.wait()
        ga[...] = acc[...].astype(BF16)
        gat[...] = ga[...].T
        ownall(lambda h: (own(0, h, 0).wait(), own(0, h, 1).start()))
        yarr(0, 2, 2)
    wz, sm = w.at[0, 0], small.at[0]
    gc[...] = nt(ga[...], wz[576:768, :]).astype(BF16)
    kt[...] = k[0].T
    @pl.when(g == 2)
    def _():
        yarr(0, 2, 0)
    @pl.when(g == 3)
    def _():
        yarr(0, 2, 1)
    def hook(i):
        def on(n, j, fn):
            @pl.when((g == n) & (i == j))
            def _(): fn()
        on(0, 0, lambda: A(F, 0))
        on(0, 1, lambda: yarr(0, 0, 0))
        on(0, 3, lambda: A(F, 1))
        on(1, 0, lambda: yarr(0, 0, 1))
        on(1, 2, lambda: yarr(0, 1, 1))
        on(1, 3, lambda: B(F, 0))
        on(2, 2, lambda: (A(T, 0), C(F, 0), Z(F, 0, 0)))
    attend_bwd(z, sm, q8.at[0], k.at[0], v.at[0], kt, gc, dm, lse.at[0], gqt, gk, gv, hook)
    @pl.when(g == 0)
    def _():
        yarr(0, 1, 0)
    zg = zo(g)
    dq = gqt[...].astype(BF16).T
    dk = gk[...].astype(BF16)
    dv = gv[...].astype(BF16)
    gbs[zg, 0:1, 0:192] = jnp.sum(dq.astype(F32), axis=0, keepdims=True)
    gbs[zg, 1:2, 0:192] = jnp.sum(dv.astype(F32), axis=0, keepdims=True)
    acc[...] += nn(dq, wz[0:192, :]) + nn(dk, wz[192:384, :]) + nn(dv, wz[384:576, :])
    def X():
        for i in range(5):
            dxs[i] = acc[128 * i:128 * i + 128, :].astype(BF16)
        vs[0] = jnp.zeros((16, D), F32)
        vs[0, 0:3, :] = vin2[0:3, :]
        vs[0, 3:6, :] = vin1[0:3, :]
        for i in range(4):
            vs[0, 6 + 2 * i:8 + 2 * i, 0:192] = gbs[i, 0:2, 0:192]
        vcopy(0).start()
        ysend(1, dxs, z, "start")
        ownall(lambda h: own(1, h, 1).start())
    @pl.when(g == 1)
    def _():
        yarr(1, 2, 2)
    @pl.when(g == 2)
    def _():
        C(F, 1); Z(F, 1, 0); yarr(0, 1, 2); A(F, 2)
    @pl.when(g == 3)
    def _():
        X(); B(F, 2); A(T, 1)
    for i in range(6):
        rw = slice(128 * i, 128 * i + 128)
        gob[zg, 0, rw, :] = jnp.concatenate([nn(xt[rw, :], dq), nn(xt[rw, :], dk), nn(xt[rw, :], dv), nn(gat[rw, :], ctx[0])], axis=1).astype(BF16)
    @pl.when(g == 0)
    def _():
        S0(T, 0)
    @pl.when(g == 1)
    def _():
        B(F, 1); S0(T, 1)
    @pl.when(g == 2)
    def _():
        S0(T, 2)
    @pl.when(g == 3)
    def _():
        A(F, 3); C(F, 2); Z(F, 1, 1); S0(T, 3); Z(F, 2, 0); Z(F, 0, 1); vstep(0); B(T, 1); B(T, 0)
        yarr(1, 1, 1); B(F, 3); A(T, 2); A(T, 3); C(T, 1); C(T, 0); Z(T, 0, 0); Z(T, 1, 0); yarr(1, 0, 0)
        yarr(1, 0, 2); yarr(1, 1, 0); C(F, 3); Z(F, 0, 2); Z(F, 1, 2); yarr(0, 0, 2); yarr(1, 0, 1); Z(F, 3, 0); vstep(1)
        B(T, 2); yarr(1, 1, 2); C(T, 2); Z(F, 0, 3); Z(T, 2, 0); Z(T, 1, 1); B(T, 3); C(T, 3); vstep(2)
        Z(F, 1, 3); yarr(1, 2, 1); Z(F, 3, 1); Z(T, 0, 1); Z(T, 3, 0); vstep(3); Z(T, 0, 2); Z(T, 0, 3); Z(T, 1, 2)
        Z(T, 1, 3); Z(F, 2, 1); yarr(1, 2, 0); Z(T, 2, 1); Z(F, 3, 2); Z(F, 2, 2); vstep(4); Z(T, 2, 2); Z(T, 3, 2)
        Z(T, 3, 1)
        for kd in (0, 1):
            for zz in ZO:
                for q in range(4): st0(kd, zz, q).wait_send()
                for j in range(2):
                    s1x(kd, zz, j).wait_send(); s1y(kd, zz, j).wait_send()
                s1xy(kd, zz).wait_send(); s1yx(kd, zz).wait_send()
                @pl.when(z < zz)
                def _(): zs(kd, zz, True).wait_send()
                @pl.when(z > zz)
                def _(): zs(kd, zz, False).wait_send()
        for t, src in enumerate((yin, dxs)):
            ysend(t, src, z, "wait_send")
            for j in range(3):
                ysend(t, None, order[j], "wait_send")
            ownall(lambda h: own(t, h, 1).wait())
        for i in range(5): vcopy(i).wait_send()

def run_kx(slen, llen, xl, xs, W, small, q8, k, v, ctx, lse, gs1, g3, yv, v2, v1):
    pz = lambda *s: pl.BlockSpec((1,) + s, lambda g, *_: (zo(g),) + (0,) * len(s))
    rz = lambda: pz(R, E)
    V, S = pltpu.VMEM, pltpu.SemaphoreType.DMA
    b = lambda *s: V(s + (PR, D), BF16)
    h = lambda *s: V(s + (H, D), BF16)
    bufs = lambda n: [b(4, 4, n), h(4, 2, n), h(4, 2, n), h(4, n), h(4, n), b(4, n), b(4, n)]
    scratch = [V((5, 128, D), BF16), V((5, 512, 128), F32), V((E, R), BF16), V((R, E), BF16), V((E, R), F32), V((R, E), F32), V((R, E), F32),
               V((R, D), BF16), V((D, R), BF16), V((D, R), BF16), V((R, D), F32), V((4, 1, D, D), BF16), V((5, 128, D), BF16), V((4, 8, 256), F32),
               V((5, 128, D), BF16), V((5, 16, D), F32), V((5, 16, D), F32), b(4, 4, 3)] + bufs(3) + bufs(1) + [
               S((2,)), S((2, 4, 4)), S((2, 4, 4)), S((4, 4)), S((2, 4, 6)), S((2, 4, 6)), S((2, 4)), S((2, 4, 2)), S((2, 4, 3, 2)), S((2, 4, 3)), S((5,)), S((5,)), S((2, 2, 2))]
    return pl.pallas_call(
        kx,
        grid_spec=pltpu.PrefetchScalarGridSpec(num_scalar_prefetch=2, grid=(4,),
            in_specs=[ANY, ANY, pl.BlockSpec((1, 1, D, D), lambda g, *_: (zo(g), 0, 0, 0)), pz(8, 256), rz(), rz(), rz(), rz(), pz(8, R), ANY, ANY, ANY, const((8, D)), const((8, D))],
            out_specs=[const((3, PR, E)), const((PR, E)), const((2, PR, D)), const((PR, D)), ANY, ANY, const((16, D))], scratch_shapes=scratch),
        out_shape=[sds((3, PR, E), F32), sds((PR, E), F32), sds((2, PR, D), F32), sds((PR, D), F32), sds((17, 128, D), BF16), sds((17, 128, D), BF16), sds((16, D), F32)],
        compiler_params=pltpu.CompilerParams(dimension_semantics=("arbitrary",), collective_id=1, has_side_effects=True, vmem_limit_bytes=VM),
        name="attention_backward_send")(slen, llen, xl, xs, W, small, q8, k, v, ctx, lse, gs1, g3, yv, v2, v1)

def split_rows(y, d, gq, gw, gd, yl, ys, dl, ds, gqo, gwo, gdo, buf, si, so):
    moves = [(t, i, f, n, h, f - 8 * (f // 8)) for i, (t, lo, sh) in enumerate(((y, yl, ys), (d, dl, ds))) for f, n, h in ((0, 4, lo), (4, 4, lo), (8, 5, sh), (13, 4, sh))]
    def put(i):
        t, j, f, n, _, _ = moves[i]
        return pltpu.make_async_copy(t.at[pl.ds(f, n)], buf.at[j, pl.ds(f, n)], si.at[i])
    def out(i):
        _, j, f, n, h, o = moves[i]
        return pltpu.make_async_copy(buf.at[j, pl.ds(f, n)], h.at[pl.ds(o, n)], so.at[i])
    for i in range(8): put(i).start()
    gqo[...] = gq[...]
    gwo[...] = gw[...]
    gdo[...] = gd[...]
    for i in range(8):
        put(i).wait(); out(i).start()
    for i in range(8): out(i).wait()

def run_split(Y, DX, gq, gwo, gdn):
    V = pl.BlockSpec(memory_space=pltpu.VMEM)
    S = pltpu.SemaphoreType.DMA
    r = lambda n: sds((n, 128, D), BF16)
    return pl.pallas_call(split_rows, in_specs=[ANY, ANY, V, V, V], out_specs=[ANY] * 4 + [V] * 3,
        out_shape=[r(8), r(9), r(8), r(9), sds((3, PR, E), F32), sds((PR, E), F32), sds((PR, D), F32)],
        scratch_shapes=[pltpu.VMEM((2, 17, 128, D), BF16), S((8,)), S((8,))],
        compiler_params=pltpu.CompilerParams(vmem_limit_bytes=VM), name="split_rows")(Y, DX, gq, gwo, gdn)

def alibi_slopes(slope_index, head_total):
    power = 1 << head_total.bit_length() - 1
    f = slope_index.astype(F32)
    return jnp.where(slope_index < power, jnp.exp2(-8.0 * (f + 1.0) / power), jnp.exp2(-4.0 * (2.0 * (f - power) + 1.0) / power))
def prep(slope_index, w_qkv, b_qv, w_out, w_up, w_down):
    a = jnp.concatenate([jnp.transpose(w_qkv, (1, 2, 0)).reshape(576, D), w_out.T], 0)
    own = jnp.stack([a, w_up[:, 0], w_up[:, 1], w_down], 0)
    bt = jnp.transpose(b_qv, (1, 2, 0)).reshape(2, 192)
    sl = jnp.pad(alibi_slopes(slope_index, 12)[None], ((0, 0), (0, 189)))
    small = jnp.pad(jnp.concatenate([bt, sl], 0), ((0, 5), (0, 64)))
    return own, small
def per_device(x_short, x_long, short_lengths, long_lengths, slope_index, w_qkv, b_qv, w_out, b_out, gain1, bias1, w_up, w_down, b_down, gain2, bias2, cot_short, cot_long):
    own, small = prep(slope_index, w_qkv, b_qv, w_out, w_up, w_down)
    row = lax.broadcasted_iota(jnp.int32, (8, D), 0)
    vec = jnp.broadcast_to(bias2[None], (8, D))
    for i, t in enumerate((b_out, gain1, bias1, b_down, gain2)):
        vec = jnp.where(row == i, t[None], vec)
    xl, cl = x_long.reshape(8, 128, D), cot_long.reshape(8, 128, D)
    W, S, q8, k, v, ctx, lse, n1, r1, hl, a, b, inner, y, gf, gs2, vg2 = run_kg(short_lengths, long_lengths, own, small, xl, x_short, cl, cot_short, vec)
    go3, gs1, vg1 = run_kc(W, a, b, inner, gf, hl, gs2, n1, r1, vec)
    m, dpx = lax.axis_index("mp"), lax.axis_index("dp")
    gq, gwo, gup, gdn, Y, DX, vs = run_kx(short_lengths, long_lengths, xl, x_short, W, S, q8, k, v, ctx, lse, gs1, go3, y.reshape(5, 128, D), vg2, vg1)
    b = lax.dynamic_slice(vs[6:14, :192].reshape(4, 2, 3, 64), (m, 0, 0, 8 * dpx), (1, 2, 3, 8))[0]
    vs = lax.dynamic_slice(vs[:6], (0, 96 * dpx), (6, 96))
    yl, ys, dl, ds, gq, gwo, gdn = run_split(Y, DX, gq, gwo, gdn)
    return (ys, yl.reshape(2, 512, D), ds, dl.reshape(2, 512, D), jnp.transpose(gq, (1, 0, 2)), jnp.transpose(b, (2, 0, 1)), gwo, vs[5], vs[3], vs[4], jnp.transpose(gup, (1, 0, 2)), gdn, vs[2], vs[0], vs[1])
def per_device_any(x_short, x_long, short_lengths, long_lengths, slope_index, w_qkv, b_qv, w_out, b_out, gain1, bias1, w_up, w_down, b_down, gain2, bias2, cot_short, cot_long):
    own, small = prep(slope_index, w_qkv, b_qv, w_out, w_up, w_down)
    W = lax.all_gather(own, "mp"); S = lax.all_gather(small, "mp")
    vec = jnp.stack([b_out, gain1, bias1, b_down, gain2, bias2, bias2, bias2], 0)
    xl, cl = x_long.reshape(8, 128, D), cot_long.reshape(8, 128, D)
    q8, k, v, ctx, lse, n1, r1, hl = run_ka(short_lengths, long_lengths, xl, x_short, W, S, vec)
    a, b, inner, y, gf, gs2, vg2 = run_kb(cl, cot_short, W, hl, n1, vec)
    go3, gs1, vg1 = run_kc(W, a, b, inner, gf, hl, gs2, n1, r1, vec)
    go1, dx, gb = run_kd(short_lengths, long_lengths, xl, x_short, W, S, q8, k, v, ctx, lse, gs1.astype(BF16), gs1)
    m = lax.axis_index("mp")
    def spread(r):
        g = lax.all_gather(r, "mp")
        return jnp.concatenate([g[2], g[3][:512]], 0).reshape(9, 128, D), jnp.stack([g[0][:512], g[1][:512]], 0)
    ys, yl = spread(y); ds, dl = spread(dx)
    G = jnp.concatenate([go1, go3], 1).astype(F32)
    G = lax.psum_scatter(G, "mp", scatter_dimension=0, tiled=True)[0]
    G = lax.psum_scatter(G, "dp", scatter_dimension=1, tiled=True)
    vs = lax.psum(jnp.concatenate([vg2[:3], vg1[:3]], 0), "mp")
    vs = lax.psum_scatter(vs, "dp", scatter_dimension=1, tiled=True)
    gb = lax.psum_scatter(gb[:, :2, :192], "mp", scatter_dimension=0, tiled=True)[0]
    gb = jnp.transpose(gb.reshape(2, 3, 64), (2, 0, 1))
    gb = lax.psum_scatter(gb, "dp", scatter_dimension=0, tiled=True)
    gq = jnp.transpose(G[0][:, :576].reshape(-1, 3, 192), (0, 1, 2))
    return (ys, yl, ds, dl, gq, gb, G[0][:, 576:], vs[5], vs[3], vs[4], jnp.stack([G[1], G[2]], 1), G[3], vs[2], vs[0], vs[1])
def solution(mesh):
    fn = per_device if mesh.shape["dp"] == 8 else per_device_any
    d3 = P("dp", None, None)
    return jax.shard_map(fn, mesh=mesh,
        in_specs=(d3, d3, P("dp"), P("dp"), P("mp"), P(None, None, "mp"), P(None, None, "mp"), P(None, "mp"), P(), P(), P(), P(None, None, "mp"), P(None, "mp"), P(), P(), P(), d3, d3),
        out_specs=(d3, d3, d3, d3, P("dp", None, "mp"), P("dp", None, "mp"), P("dp", "mp"), P("dp"), P("dp"), P("dp"), P("dp", None, "mp"), P("dp", "mp"), P("dp"), P("dp"), P("dp")),
        check_vma=False)
```
